256 devices in a mesh: mp: 16 (over y, z_hi, core), replica: 16 (over x, z_lo).
Axes of the slice: x: 4, y: 4, z: 8 (z_hi: 2, z_lo: 4; z = z_hi * 4 + z_lo), core: 2. Of those that a mesh axis runs over, the one named last changes fastest.
Arguments:
- weight: float32 [2560, 5120], P('mp'), may hold values from -6 to 6
- first_moment: bfloat16 [16, 2560, 5120], P('replica', 'mp'), may hold values from -0.0011978149 to 0.0011978149
- second_moment: bfloat16 [16, 2560, 5120], P('replica', 'mp'), may hold values from 9.95351e-09 to 9.983778e-07
- outer_momentum: float32 [2560, 5120], P(('mp', 'replica')), may hold values from -0.3 to 0.3
- act_table: bfloat16 [2048, 5120], P(None, 'mp'), may hold values from -6 to 6
- token_ids: int32 [16, 2, 512], P('replica'), may hold values from 0 to 2047
- targets: bfloat16 [16, 2, 512, 2560], P('replica', None, None, 'mp'), may hold values from -6 to 6
Outputs:
- new_weight: float32 [2560, 5120], P('mp')
- momentum: float32 [2560, 5120], P(('mp', 'replica'))
The draws below stay inside these ranges and needn't reach their ends.
All inputs are finite; a program needn't handle non-finite values. Where the reference program divides by a largest or mean magnitude, that divisor is 1e-20 or more.
Results may differ from the reference program's by a relative error of at most 0.002.
Values may be sent and summed in bfloat16 or wider, within the bound.
No kernel may reach another device: no remote copies, remote signals or barrier semaphores. Data moves between devices by JAX's collectives and lax.ppermute only.
A program may use at most 64 MiB of HBM per device.

```python
import math
import jax
import jax.numpy as jnp
from jax import lax

D_IN = 5120
D_OUT = 2560
TOK = 512
STEPS = 2
TABLE = 2048
BLOCK = 128
PRIOR_STEPS = 3
REPLICAS = 16


def set_ends(array, rng, least, largest):
    place = [jax.random.randint(jax.random.fold_in(rng, axis), (), 0, length) for axis, length in enumerate(array.shape)]
    widest = array.shape.index(max(array.shape))
    beside = place[:widest] + [(place[widest] + 1) % array.shape[widest]] + place[widest + 1:]
    return array.at[tuple(place)].set(least).at[tuple(beside)].set(largest)


def levels(own_key, shape, shards, smallest, top_value):
    loudness = 1.0
    for dim, shards_of in shards:
        draws = jax.random.uniform(jax.random.fold_in(jax.random.fold_in(own_key, 6), dim), (shards_of,), jnp.float32, smallest / len(shards), top_value / len(shards))
        loudness = loudness * jnp.repeat(jnp.exp(draws), shape[dim] // shards_of).reshape((-1,) + (1,) * (len(shape) - 1 - dim))
    return loudness


def bell_draw(stream_key, dims, spread, reach, split=(), kind=jnp.bfloat16):
    gain = levels(stream_key, dims, split, -0.22, 0.18) if split else 1.0
    drawn = jax.random.normal(stream_key, dims, jnp.float32) * spread * gain
    return jnp.minimum(jnp.maximum(drawn, -reach), reach).astype(kind)


def setup_inputs(seed: int = 0) -> dict:
    seeds = jax.random.split(jax.random.key(seed), 8)
    weight = bell_draw(seeds[0], (D_OUT, D_IN), 1.0, 6.0, ((0, 16),), jnp.float32)
    first_moment = bell_draw(seeds[1], (REPLICAS, D_OUT, D_IN), 0.0002, 0.0011978149, ((0, 16), (1, 16)))
    second_moment = jnp.clip(jnp.exp(math.log(9.98377799987793e-07) - 4.6082065 * jax.random.uniform(seeds[2], (REPLICAS, D_OUT, D_IN), jnp.float32) ** levels(seeds[2], (REPLICAS, D_OUT, D_IN), ((0, 16), (1, 16)), -0.2, 0.2)), 9.953510016202927e-09, 9.98377799987793e-07).astype(jnp.bfloat16)
    outer_momentum = bell_draw(seeds[3], (D_OUT, D_IN), 0.05, 0.3, ((0, 256),), jnp.float32)
    act_table = bell_draw(seeds[4], (TABLE, D_IN), 1.0, 6.0, ((1, 16),))
    token_ids = set_ends(jax.random.randint(seeds[5], (REPLICAS, STEPS, TOK), 0, TABLE), jax.random.fold_in(seeds[5], 1), 0, TABLE - 1).astype(jnp.int32)
    targets = bell_draw(seeds[6], (REPLICAS, STEPS, TOK, D_OUT), 1.0, 6.0, ((0, 16), (3, 16)))
    return {"weight": weight, "first_moment": first_moment, "second_moment": second_moment, "outer_momentum": outer_momentum, "act_table": act_table, "token_ids": token_ids, "targets": targets}


beta_first = 0.9
beta_second = 0.95
adam_epsilon = 1e-08
inner_rate = 0.1
weight_decay = 0.1
outer_mu = 0.9
outer_rate = 0.7
scale_epsilon = 1e-06

def encode(values):
    row_count = values.shape[0]
    blocks = values.reshape(row_count, -1, BLOCK)
    scales = (lax.optimization_barrier(jnp.max(jnp.abs(blocks), axis=2)) + scale_epsilon).astype(jnp.bfloat16)
    code_values = (blocks / scales.astype(jnp.float32)[:, :, None]).astype(jnp.bfloat16)
    return (code_values.reshape(row_count, -1), scales)

def decode(code_values, scales):
    row_count = code_values.shape[0]
    blocks = code_values.astype(jnp.float32).reshape(row_count, scales.shape[1], -1)
    return (blocks * scales.astype(jnp.float32)[:, :, None]).reshape(row_count, -1)

def inner_steps(weight, first, second, table_rows, wanted_all, act_table):
    factor = D_IN ** (-0.5)
    current = weight
    moment_one = first.astype(jnp.float32)
    moment_two = second.astype(jnp.float32)
    for inner_step in range(STEPS):
        inputs = jnp.take(act_table, table_rows[inner_step], axis=0)
        weight_half = current.astype(jnp.bfloat16)
        output = jnp.dot(inputs, weight_half.T, preferred_element_type=jnp.float32) * factor
        signal = (output - wanted_all[inner_step].astype(jnp.float32)).astype(jnp.bfloat16)
        gradient = jnp.dot(signal.T, inputs, preferred_element_type=jnp.float32) * (factor / TOK)
        step_count = PRIOR_STEPS + inner_step + 1
        moment_one = beta_first * moment_one + (1.0 - beta_first) * gradient
        moment_two = beta_second * moment_two + (1.0 - beta_second) * gradient * gradient
        update = moment_one / (1.0 - beta_first ** step_count) / (jnp.sqrt(moment_two / (1.0 - beta_second ** step_count)) + adam_epsilon)
        current = current - inner_rate * (update + weight_decay * current)
    return weight - current

def reference(weight, first_moment, second_moment, outer_momentum, act_table, token_ids, targets):

    def add_replica(running, replica_index):
        delta = inner_steps(weight, first_moment[replica_index], second_moment[replica_index], token_ids[replica_index], targets[replica_index], act_table)
        code_values, scales = encode(delta)
        return (running + decode(code_values, scales), None)
    summed, _ = lax.scan(add_replica, jnp.zeros(weight.shape, jnp.float32), jnp.arange(REPLICAS, dtype=jnp.int32))
    average = summed / REPLICAS
    momentum = outer_mu * outer_momentum + average
    outer_update = average + outer_mu * momentum
    update_codes, update_scales = encode(outer_update)
    new_weight = weight - outer_rate * decode(update_codes, update_scales)
    return (new_weight, momentum)
```

```python
import functools

import jax
import jax.numpy as jnp
from jax import lax
from jax.experimental import pallas as pl
from jax.experimental.pallas import tpu as pltpu
from jax.sharding import Mesh, PartitionSpec as P

STEPS = 2
BLOCK = 128
PRIOR_STEPS = 3

beta_first = 0.9
beta_second = 0.95
adam_epsilon = 1e-08
inner_rate = 0.1
weight_decay = 0.1
outer_mu = 0.9
outer_rate = 0.7
scale_epsilon = 1e-06

ROWS = 160
WIDTH = 5120
TOK = 512
CHUNK = 320
PAIR = 2 * CHUNK
SLOTS = 8
COLS = 512
TILE = 16
QUARTER = WIDTH // 4
PAYLOAD = WIDTH + BLOCK
SMALL = QUARTER + BLOCK

F32 = jnp.float32
BF16 = jnp.bfloat16
FACTOR = WIDTH ** (-0.5)


ANY = pl.BlockSpec(memory_space=pl.ANY)
VM = pl.BlockSpec(memory_space=pltpu.VMEM)
SM = pl.BlockSpec(memory_space=pltpu.SMEM)


def params(mib):
    return pltpu.CompilerParams(vmem_limit_bytes=mib << 20)


def gather_kernel(ids_ref, table_ref, out_ref):
    ids = ids_ref[...]
    total = jnp.zeros((CHUNK, TOK), F32)
    step = 512
    for start in range(0, table_ref.shape[1], step):
        row = lax.broadcasted_iota(jnp.int32, (step, TOK), 0) + start
        pick = jnp.where(row == ids, 1.0, 0.0).astype(BF16)
        total = total + jnp.dot(
            table_ref[:, start : start + step], pick, preferred_element_type=F32
        )
    out_ref[...] = total.astype(BF16)


def gather(ids, table_t):
    return pl.pallas_call(
        gather_kernel,
        out_shape=jax.ShapeDtypeStruct((CHUNK, TOK), BF16),
        in_specs=[VM, VM],
        out_specs=VM,
        compiler_params=params(16),
        name="gather",
    )(ids, table_t)


def forward_part(x_copies, w_copies, w_buf, x_buf, where_ref):
    total = jnp.zeros((ROWS, TOK), F32)
    for slot in range(SLOTS):
        for copy in x_copies[slot] + w_copies[slot]:
            copy.wait()
        at = pl.multiple_of(where_ref[slot] * PAIR, PAIR)
        total = total + jnp.dot(
            w_buf[:, pl.ds(at, PAIR)].astype(BF16),
            x_buf[pl.ds(at, PAIR), :],
            preferred_element_type=F32,
        )
    return total


def load_inputs(where_ref, xs, w_ref, x_buf, w_buf, x_sem, w_sem):
    core = where_ref[SLOTS]
    x_copies, w_copies = [], []
    for slot in range(SLOTS):
        at = pl.multiple_of(where_ref[slot] * PAIR, PAIR)
        mine = pl.multiple_of(at + core * CHUNK, CHUNK)
        other = pl.multiple_of(at + (1 - core) * CHUNK, CHUNK)
        x_copies.append(
            [
                pltpu.make_async_copy(xs[slot], x_buf.at[pl.ds(mine, CHUNK)], x_sem.at[slot]),
                pltpu.make_async_copy(
                    xs[SLOTS + slot], x_buf.at[pl.ds(other, CHUNK)], x_sem.at[SLOTS + slot]
                ),
            ]
        )
        w_copies.append(
            [
                pltpu.make_async_copy(
                    w_ref.at[:, pl.ds(at, PAIR)], w_buf.at[:, pl.ds(at, PAIR)], w_sem.at[slot]
                )
            ]
        )
    for copies in (x_copies, w_copies):
        for slot in range(SLOTS):
            for copy in copies[slot]:
                copy.start()
    return x_copies, w_copies


def gradient_block(signal, x_buf, start):
    return lax.dot_general(
        signal,
        x_buf[pl.ds(start, COLS), :],
        (((1,), (1,)), ((), ())),
        preferred_element_type=F32,
    ) * (FACTOR / TOK)


def adam(step_count, gradient, one, two, current):
    one = beta_first * one + (1.0 - beta_first) * gradient
    two = beta_second * two + (1.0 - beta_second) * gradient * gradient
    update = (one * (1.0 / (1.0 - beta_first**step_count))) / (
        jnp.sqrt(two * (1.0 / (1.0 - beta_second**step_count))) + adam_epsilon
    )
    return one, two, current - inner_rate * (update + weight_decay * current)


def first_kernel(where_ref, target_ref, w_ref, one_ref, two_ref, *refs):
    xs = refs[: 2 * SLOTS]
    cur_out, one_out, two_out = refs[2 * SLOTS : 2 * SLOTS + 3]
    (x_buf, w_buf, one_buf, two_buf, cur_new, one_new, two_new, grad, x_sem, w_sem, s_sem, o_sem) = refs[
        2 * SLOTS + 3 :
    ]
    x_copies, w_copies = load_inputs(where_ref, xs, w_ref, x_buf, w_buf, x_sem, w_sem)
    states = [
        pltpu.make_async_copy(one_ref, one_buf, s_sem.at[0]),
        pltpu.make_async_copy(two_ref, two_buf, s_sem.at[1]),
    ]
    for copy in states:
        copy.start()
    output = forward_part(x_copies, w_copies, w_buf, x_buf, where_ref) * FACTOR
    signal = (output - target_ref[...].astype(F32)).astype(BF16)
    for copy in states:
        copy.wait()

    def column(block, carry):
        start = pl.multiple_of(block * COLS, COLS)
        grad[...] = gradient_block(signal, x_buf, start)

        def rows(tile, carry):
            row = pl.multiple_of(tile * TILE, TILE)
            here = (pl.ds(row, TILE), pl.ds(start, COLS))
            one, two, current = adam(
                PRIOR_STEPS + 1,
                grad[pl.ds(row, TILE), :],
                one_buf[here].astype(F32),
                two_buf[here].astype(F32),
                w_buf[here],
            )
            one_new[here] = one
            two_new[here] = two
            cur_new[here] = current
            return carry

        lax.fori_loop(0, ROWS // TILE, rows, 0)
        return carry

    lax.fori_loop(0, WIDTH // COLS, column, 0)
    outs = [
        pltpu.make_async_copy(cur_new, cur_out, o_sem.at[0]),
        pltpu.make_async_copy(one_new, one_out, o_sem.at[1]),
        pltpu.make_async_copy(two_new, two_out, o_sem.at[2]),
    ]
    for copy in outs:
        copy.start()
    for copy in outs:
        copy.wait()


def first_step(where, target, weight, one, two, xs):
    state = jax.ShapeDtypeStruct((ROWS, WIDTH), F32)
    return pl.pallas_call(
        first_kernel,
        out_shape=(state, state, state),
        in_specs=[SM, VM] + [ANY] * (3 + 2 * SLOTS),
        out_specs=(ANY, ANY, ANY),
        scratch_shapes=[
            pltpu.VMEM((WIDTH, TOK), BF16),
            pltpu.VMEM((ROWS, WIDTH), F32),
            pltpu.VMEM((ROWS, WIDTH), BF16),
            pltpu.VMEM((ROWS, WIDTH), BF16),
            pltpu.VMEM((ROWS, WIDTH), F32),
            pltpu.VMEM((ROWS, WIDTH), F32),
            pltpu.VMEM((ROWS, WIDTH), F32),
            pltpu.VMEM((ROWS, COLS), F32),
            pltpu.SemaphoreType.DMA((2 * SLOTS,)),
            pltpu.SemaphoreType.DMA((SLOTS,)),
            pltpu.SemaphoreType.DMA((2,)),
            pltpu.SemaphoreType.DMA((3,)),
        ],
        compiler_params=params(40),
        name="first_step",
    )(where, target, weight, one, two, *xs)


def second_kernel(where_ref, target_ref, w_ref, cur_ref, one_ref, two_ref, *refs):
    xs = refs[: 2 * SLOTS]
    code_ref = refs[2 * SLOTS]
    (x_buf, w_buf, cur_buf, one_buf, two_buf, grad, scale_buf, x_sem, w_sem, s_sem) = refs[2 * SLOTS + 1 :]
    x_copies, w_copies = load_inputs(where_ref, xs, cur_ref, x_buf, cur_buf, x_sem, w_sem)
    states = [
        pltpu.make_async_copy(one_ref, one_buf, s_sem.at[0]),
        pltpu.make_async_copy(two_ref, two_buf, s_sem.at[1]),
        pltpu.make_async_copy(w_ref, w_buf, s_sem.at[2]),
    ]
    for copy in states:
        copy.start()
    output = forward_part(x_copies, w_copies, cur_buf, x_buf, where_ref) * FACTOR
    signal = (output - target_ref[...].astype(F32)).astype(BF16)
    for copy in states:
        copy.wait()
    scale_buf[...] = jnp.zeros_like(scale_buf)
    blocks = COLS // BLOCK

    def column(block, carry):
        start = pl.multiple_of(block * COLS, COLS)
        grad[...] = gradient_block(signal, x_buf, start)

        def rows(tile, carry):
            row = pl.multiple_of(tile * TILE, TILE)
            lane = lax.broadcasted_iota(jnp.int32, (TILE, BLOCK), 1)
            scales = scale_buf[pl.ds(row, TILE), :]
            for part in range(blocks):
                offset = pl.multiple_of(start + part * BLOCK, BLOCK)
                here = (pl.ds(row, TILE), pl.ds(offset, BLOCK))
                _, _, current = adam(
                    PRIOR_STEPS + 2,
                    grad[pl.ds(row, TILE), part * BLOCK : (part + 1) * BLOCK],
                    one_buf[here],
                    two_buf[here],
                    cur_buf[here],
                )
                delta = w_buf[here] - current
                top = jnp.max(jnp.abs(delta), axis=1, keepdims=True) + scale_epsilon
                scale = jnp.broadcast_to(top.astype(BF16).astype(F32), (TILE, BLOCK))
                code_ref[here] = (delta / scale).astype(BF16)
                scales = jnp.where(lane == block * blocks + part, scale, scales)
            scale_buf[pl.ds(row, TILE), :] = scales
            return carry

        lax.fori_loop(0, ROWS // TILE, rows, 0)
        return carry

    lax.fori_loop(0, WIDTH // COLS, column, 0)
    code_ref[:, WIDTH:] = scale_buf[...].astype(BF16)


def second_step(where, target, weight, current, one, two, xs):
    return pl.pallas_call(
        second_kernel,
        out_shape=jax.ShapeDtypeStruct((ROWS, PAYLOAD), BF16),
        in_specs=[SM, VM] + [ANY] * (4 + 2 * SLOTS),
        out_specs=VM,
        scratch_shapes=[
            pltpu.VMEM((WIDTH, TOK), BF16),
            pltpu.VMEM((ROWS, WIDTH), F32),
            pltpu.VMEM((ROWS, WIDTH), F32),
            pltpu.VMEM((ROWS, WIDTH), F32),
            pltpu.VMEM((ROWS, WIDTH), F32),
            pltpu.VMEM((ROWS, COLS), F32),
            pltpu.VMEM((ROWS, BLOCK), F32),
            pltpu.SemaphoreType.DMA((2 * SLOTS,)),
            pltpu.SemaphoreType.DMA((SLOTS,)),
            pltpu.SemaphoreType.DMA((3,)),
        ],
        compiler_params=params(40),
        name="second_step",
    )(where, target, weight, current, one, two, *xs)


def partial_kernel(got_ref, out_ref, part, piece):
    sources, rows = got_ref.shape[0], got_ref.shape[1]
    scales = [got_ref[source, :, WIDTH:].astype(F32) for source in range(sources)]
    for block in range(WIDTH // BLOCK):
        here = slice(block * BLOCK, (block + 1) * BLOCK)
        total = jnp.zeros((rows, BLOCK), F32)
        for source in range(sources):
            scale = scales[source][:, block : block + 1]
            total = total + got_ref[source, :, here].astype(F32) * scale
        part[:, here] = total
    own = rows // 4
    for line in range(4):
        for group in range(4):
            piece[line, group * own : (group + 1) * own, :] = part[
                line * own : (line + 1) * own, group * QUARTER : (group + 1) * QUARTER
            ]
        out_ref[line] = piece[line].astype(BF16)


def partial_sums(got):
    sources, rows, _ = got.shape
    return pl.pallas_call(
        partial_kernel,
        out_shape=jax.ShapeDtypeStruct((4, rows, QUARTER), BF16),
        in_specs=[VM],
        out_specs=VM,
        scratch_shapes=[
            pltpu.VMEM((rows, WIDTH), F32),
            pltpu.VMEM((4, rows, QUARTER), F32),
        ],
        compiler_params=params(16),
        name="partial_sums",
    )(got)


def outer_kernel(got_ref, outer_ref, momentum_ref, code_ref, held, sent):
    own = outer_ref.shape[0]
    for group in range(4):
        held[group * own : (group + 1) * own, :] = outer_ref[:, group * QUARTER : (group + 1) * QUARTER]
    lane = lax.broadcasted_iota(jnp.int32, (4 * own, BLOCK), 1)
    scales = jnp.zeros((4 * own, BLOCK), F32)
    for block in range(QUARTER // BLOCK):
        here = slice(block * BLOCK, (block + 1) * BLOCK)
        total = got_ref[0, :, here].astype(F32)
        for source in range(1, 4):
            total = total + got_ref[source, :, here].astype(F32)
        average = total * (1.0 / 16)
        momentum = outer_mu * held[:, here] + average
        sent[:, here] = momentum
        update = average + outer_mu * momentum
        top = jnp.max(jnp.abs(update), axis=1, keepdims=True) + scale_epsilon
        scale = jnp.broadcast_to(top.astype(BF16).astype(F32), (4 * own, BLOCK))
        code_ref[:, here] = (update / scale).astype(BF16)
        scales = jnp.where(lane == block, scale, scales)
    code_ref[:, QUARTER:] = scales.astype(BF16)
    for group in range(4):
        momentum_ref[:, group * QUARTER : (group + 1) * QUARTER] = sent[group * own : (group + 1) * own, :]


def outer_step(got, outer_momentum):
    own, width = outer_momentum.shape
    return pl.pallas_call(
        outer_kernel,
        out_shape=(
            jax.ShapeDtypeStruct((own, width), F32),
            jax.ShapeDtypeStruct((4 * own, SMALL), BF16),
        ),
        in_specs=[VM, VM],
        out_specs=(VM, VM),
        scratch_shapes=[
            pltpu.VMEM((4 * own, QUARTER), F32),
            pltpu.VMEM((4 * own, QUARTER), F32),
        ],
        compiler_params=params(16),
        name="outer_step",
    )(got, outer_momentum)


def final_kernel(where_ref, w_ref, *refs):
    pieces = refs[:16]
    out_ref = refs[16]
    w_buf, got, block_buf, new_buf, w_sem, got_sem, out_sem = refs[17:]
    own = ROWS // 16
    copies = []
    for index in range(16):
        copies.append(pltpu.make_async_copy(pieces[index], got.at[where_ref[index]], got_sem.at[index]))
    for copy in copies:
        copy.start()
    load = pltpu.make_async_copy(w_ref, w_buf, w_sem)
    load.start()
    for copy in copies:
        copy.wait()
    load.wait()
    outs = []
    for x in range(4):
        for line in range(4):
            piece = got.at[x * 4 + line]
            scales = piece[:, QUARTER:].astype(F32)
            for block in range(QUARTER // BLOCK):
                here = slice(block * BLOCK, (block + 1) * BLOCK)
                value = piece[:, here].astype(F32) * scales[:, block : block + 1]
                for group in range(4):
                    there = slice(group * QUARTER + block * BLOCK, group * QUARTER + (block + 1) * BLOCK)
                    block_buf[line * own : (line + 1) * own, there] = value[group * own : (group + 1) * own, :]
        rows = slice(x * 4 * own, (x + 1) * 4 * own)
        new_buf[rows, :] = w_buf[rows, :] - outer_rate * block_buf[...]
        outs.append(pltpu.make_async_copy(new_buf.at[rows], out_ref.at[rows], out_sem.at[x]))
        outs[-1].start()
    for copy in outs:
        copy.wait()


def final_step(where, weight, pieces):
    return pl.pallas_call(
        final_kernel,
        out_shape=jax.ShapeDtypeStruct((ROWS, WIDTH), F32),
        in_specs=[SM, ANY] + [ANY] * 16,
        out_specs=ANY,
        scratch_shapes=[
            pltpu.VMEM((ROWS, WIDTH), F32),
            pltpu.VMEM((16, ROWS // 4, SMALL), BF16),
            pltpu.VMEM((ROWS // 4, WIDTH), F32),
            pltpu.VMEM((ROWS, WIDTH), F32),
            pltpu.SemaphoreType.DMA,
            pltpu.SemaphoreType.DMA((16,)),
            pltpu.SemaphoreType.DMA((4,)),
        ],
        compiler_params=params(32),
        name="final_step",
    )(where, weight, *pieces)


def shift(value, axis, by):
    size = lax.axis_size(axis)
    return lax.ppermute(value, axis, [(i, (i + by) % size) for i in range(size)])


def spread(own):
    far = shift(own, "zh", 1)
    left, right = shift(own, "y", 1), shift(own, "y", -1)
    opposite = shift(left, "y", 1)
    far_left, far_right = shift(far, "y", 1), shift(far, "y", -1)
    far_opposite = shift(far_right, "y", -1)
    mine = [own, far, left, right, opposite, far_left, far_right, far_opposite]
    return mine + [shift(chunk, "c", 1) for chunk in mine]


def shards(weight, first_moment, second_moment, outer_momentum, act_table, token_ids, targets):
    y, zh, core = lax.axis_index("y"), lax.axis_index("zh"), lax.axis_index("c")
    x, zl = lax.axis_index("x"), lax.axis_index("zl")
    step_y = jnp.array([0, 0, -1, 1, 2, -1, 1, 2, 0], jnp.int32)
    step_z = jnp.array([0, 1, 0, 0, 0, 1, 1, 1, 0], jnp.int32)
    chip = ((y + step_y + 4) % 4) * 2 + (zh + step_z) % 2
    where = jnp.where(jnp.arange(9) == 8, core, chip).astype(jnp.int32)

    table_t = act_table.T
    ids = token_ids[0]
    wanted = jnp.transpose(targets[0], (0, 2, 1))
    chunks = [gather(ids[step : step + 1], table_t) for step in range(STEPS)]
    inputs = [spread(chunk) for chunk in chunks]

    current, one, two = first_step(where, wanted[0], weight, first_moment[0], second_moment[0], inputs[0])
    payload = second_step(where, wanted[1], weight, current, one, two, inputs[1])

    got = lax.all_to_all(payload.reshape(4, ROWS // 4, PAYLOAD), "x", 0, 0, tiled=True)
    parts = partial_sums(got)
    sums = lax.all_to_all(parts, "zl", 0, 0, tiled=True)
    momentum, codes = outer_step(sums, outer_momentum)

    line = [codes] + [shift(codes, "zl", by) for by in (1, 2, 3)]
    pieces = list(line)
    for by in (1, 2, 3):
        pieces += [shift(piece, "x", by) for piece in line]
    index = jnp.arange(16, dtype=jnp.int32)
    place = ((x - index // 4 + 4) % 4) * 4 + (zl - index % 4 + 4) % 4
    new_weight = final_step(place.astype(jnp.int32), weight, pieces)
    return (new_weight, momentum)


def solution(mesh):
    inner = Mesh(mesh.devices.reshape(4, 2, 2, 4, 4), ("y", "zh", "c", "x", "zl"))
    mp, replica = ("y", "zh", "c"), ("x", "zl")
    in_specs = (
        P(mp, None),
        P(replica, mp, None),
        P(replica, mp, None),
        P(mp + replica, None),
        P(None, mp),
        P(replica, None, None),
        P(replica, None, None, mp),
    )
    out_specs = (P(mp, None), P(mp + replica, None))
    return jax.shard_map(shards, mesh=inner, in_specs=in_specs, out_specs=out_specs, check_vma=False)
```

```python
import functools

import jax
import jax.numpy as jnp
from jax import lax
from jax.experimental import pallas as pl
from jax.experimental.pallas import tpu as pltpu
from jax.sharding import Mesh, PartitionSpec as P

STEPS = 2
BLOCK = 128
PRIOR_STEPS = 3

beta_first = 0.9
beta_second = 0.95
adam_epsilon = 1e-08
inner_rate = 0.1
weight_decay = 0.1
outer_mu = 0.9
outer_rate = 0.7
scale_epsilon = 1e-06

ROWS = 160
WIDTH = 5120
TOK = 512
CHUNK = 320
PAIR = 2 * CHUNK
SLOTS = 8
COLS = 512
TILE = 16
HALF = WIDTH // 2
QUARTER = HALF // 4
PAYLOAD = HALF + BLOCK

F32 = jnp.float32
BF16 = jnp.bfloat16
FACTOR = WIDTH ** (-0.5)


HB = pl.BlockSpec(memory_space=pltpu.HBM)
VM = pl.BlockSpec(memory_space=pltpu.VMEM)
SM = pl.BlockSpec(memory_space=pltpu.SMEM)


def params(mib):
    return pltpu.CompilerParams(vmem_limit_bytes=mib << 20)


def gather_kernel(ids_ref, table_ref, out_ref):
    ids = ids_ref[...]
    total = jnp.zeros((CHUNK, TOK), F32)
    step = 512
    for start in range(0, table_ref.shape[1], step):
        row = lax.broadcasted_iota(jnp.int32, (step, TOK), 0) + start
        pick = jnp.where(row == ids, 1.0, 0.0).astype(BF16)
        total = total + jnp.dot(
            table_ref[:, start : start + step], pick, preferred_element_type=F32
        )
    out_ref[...] = total.astype(BF16)


def gather(ids, table_t):
    return pl.pallas_call(
        gather_kernel,
        out_shape=jax.ShapeDtypeStruct((CHUNK, TOK), BF16),
        in_specs=[VM, VM],
        out_specs=VM,
        compiler_params=params(16),
        name="gather",
    )(ids, table_t)


def input_copies(where_ref, groups, x_buf, sems, half=None):
    core = where_ref[SLOTS]
    out = []
    slot = 0
    for own_ref, other_ref in groups:
        for place in range(own_ref.shape[0] // CHUNK):
            at = where_ref[slot] * PAIR
            if half is not None:
                at = at - half * HALF
            rows = pl.ds(place * CHUNK, CHUNK)
            mine = pl.multiple_of(at + core * CHUNK, CHUNK)
            other = pl.multiple_of(at + (1 - core) * CHUNK, CHUNK)
            out.append(
                [
                    pltpu.make_async_copy(own_ref.at[rows], x_buf.at[pl.ds(mine, CHUNK)], sems.at[slot]),
                    pltpu.make_async_copy(
                        other_ref.at[rows], x_buf.at[pl.ds(other, CHUNK)], sems.at[SLOTS + slot]
                    ),
                ]
            )
            slot += 1
    return out


def forward_kernel(groups, parts, where_ref, target_ref, *refs):
    w_refs = refs[:parts]
    refs = refs[parts:]
    xs = [(refs[2 * g], refs[2 * g + 1]) for g in range(groups)]
    signal_ref = refs[2 * groups]
    x_buf, w_buf, x_sem, w_sem = refs[2 * groups + 1 :]
    copies = input_copies(where_ref, xs, x_buf, x_sem)
    per = SLOTS // parts
    for slot in range(SLOTS):
        chip = where_ref[slot]
        at = pl.multiple_of(chip * PAIR, PAIR)
        for part in range(parts):
            inside = pl.multiple_of((chip % per) * PAIR, PAIR)
            w_copy = pltpu.make_async_copy(
                w_refs[part].at[:, pl.ds(inside, PAIR)], w_buf.at[:, pl.ds(at, PAIR)], w_sem.at[slot]
            )
            pl.when(chip // per == part)(w_copy.start)
        for copy in copies[slot]:
            copy.start()
        copies[slot].append(w_copy)
    total = jnp.zeros((ROWS, TOK), F32)
    for slot in range(SLOTS):
        for copy in copies[slot]:
            copy.wait()
        at = pl.multiple_of(where_ref[slot] * PAIR, PAIR)
        total = total + jnp.dot(
            w_buf[:, pl.ds(at, PAIR)].astype(BF16),
            x_buf[pl.ds(at, PAIR), :],
            preferred_element_type=F32,
        )
    signal_ref[...] = (total * FACTOR - target_ref[...].astype(F32)).astype(BF16)


def forward(where, target, weights, xs):
    flat = [ref for pair in xs for ref in pair]
    return pl.pallas_call(
        functools.partial(forward_kernel, len(xs), len(weights)),
        out_shape=jax.ShapeDtypeStruct((ROWS, TOK), BF16),
        in_specs=[SM, VM] + [HB] * (len(weights) + len(flat)),
        out_specs=VM,
        scratch_shapes=[
            pltpu.VMEM((WIDTH, TOK), BF16),
            pltpu.VMEM((ROWS, WIDTH), F32),
            pltpu.SemaphoreType.DMA((2 * SLOTS,)),
            pltpu.SemaphoreType.DMA((SLOTS,)),
        ],
        compiler_params=params(24),
        cost_estimate=pl.CostEstimate(
            flops=2 * ROWS * WIDTH * TOK, bytes_accessed=9 << 20, transcendentals=0
        ),
        name="forward",
    )(where, target, *weights, *flat)


def adam(step_count, gradient, one, two, current):
    one = beta_first * one + (1.0 - beta_first) * gradient
    two = beta_second * two + (1.0 - beta_second) * gradient * gradient
    update = (one * (1.0 / (1.0 - beta_first**step_count))) / (
        jnp.sqrt(two * (1.0 / (1.0 - beta_second**step_count))) + adam_epsilon
    )
    return one, two, current - inner_rate * (update + weight_decay * current)


def columns(signal, x_buf, grad, consume):
    blocks = HALF // COLS

    def product(block, slot):
        start = pl.multiple_of(block * COLS, COLS)
        grad[slot] = lax.dot_general(
            signal, x_buf[pl.ds(start, COLS), :], (((1,), (1,)), ((), ())), preferred_element_type=F32
        ) * (FACTOR / TOK)

    product(0, 0)

    def body(block, carry):
        product(block + 1, (block + 1) % 2)
        consume(block, block % 2)
        return carry

    lax.fori_loop(0, blocks - 1, body, 0)
    consume(blocks - 1, (blocks - 1) % 2)


def guarded(where_ref, half, copies, action):
    for slot in range(SLOTS):

        @pl.when(where_ref[slot] // (SLOTS // 2) == half)
        def _():
            for copy in copies[slot]:
                getattr(copy, action)()


def first_back_kernel(groups, half, where_ref, signal_ref, w_ref, one_ref, two_ref, *refs):
    xs = [(refs[2 * g], refs[2 * g + 1]) for g in range(groups)]
    outs = refs[2 * groups : 2 * groups + 3]
    (x_buf, w_buf, one_buf, two_buf, new, grad, x_sem, s_sem, o_sem) = refs[2 * groups + 3 :]
    copies = input_copies(where_ref, xs, x_buf, x_sem, half)
    guarded(where_ref, half, copies, "start")
    here = (slice(None), slice(half * HALF, (half + 1) * HALF))
    states = [
        pltpu.make_async_copy(source.at[here], buf, s_sem.at[index])
        for index, (source, buf) in enumerate(((w_ref, w_buf), (one_ref, one_buf), (two_ref, two_buf)))
    ]
    for copy in states:
        copy.start()
    guarded(where_ref, half, copies, "wait")
    for copy in states:
        copy.wait()

    def consume(block, slot):
        start = pl.multiple_of(block * COLS, COLS)
        for row in range(0, ROWS, TILE):
            tile = (slice(row, row + TILE), pl.ds(start, COLS))
            one, two, current = adam(
                PRIOR_STEPS + 1,
                grad[slot, row : row + TILE, :],
                one_buf[tile].astype(F32),
                two_buf[tile].astype(F32),
                w_buf[tile],
            )
            for index, value in enumerate((current, one, two)):
                new[(index,) + tile] = value
        for index in range(3):
            pltpu.make_async_copy(
                new.at[index, :, pl.ds(start, COLS)], outs[index].at[:, pl.ds(start, COLS)], o_sem.at[index, block]
            ).start()

    columns(signal_ref[...], x_buf, grad, consume)
    for block in range(HALF // COLS):
        at = slice(block * COLS, (block + 1) * COLS)
        for index in range(3):
            pltpu.make_async_copy(new.at[index, :, at], outs[index].at[:, at], o_sem.at[index, block]).wait()


def first_back(half, where, signal, weight, one, two, xs):
    flat = [ref for pair in xs for ref in pair]
    state = jax.ShapeDtypeStruct((ROWS, HALF), F32)
    return pl.pallas_call(
        functools.partial(first_back_kernel, len(xs), half),
        out_shape=(state, state, state),
        in_specs=[SM, VM] + [HB] * (3 + len(flat)),
        out_specs=(HB, HB, HB),
        scratch_shapes=[
            pltpu.VMEM((HALF, TOK), BF16),
            pltpu.VMEM((ROWS, HALF), F32),
            pltpu.VMEM((ROWS, HALF), BF16),
            pltpu.VMEM((ROWS, HALF), BF16),
            pltpu.VMEM((3, ROWS, HALF), F32),
            pltpu.VMEM((2, ROWS, COLS), F32),
            pltpu.SemaphoreType.DMA((2 * SLOTS,)),
            pltpu.SemaphoreType.DMA((3,)),
            pltpu.SemaphoreType.DMA((3, HALF // COLS)),
        ],
        compiler_params=params(24),
        cost_estimate=pl.CostEstimate(
            flops=ROWS * WIDTH * TOK, bytes_accessed=12 << 20, transcendentals=0
        ),
        name="first_back",
    )(where, signal, weight, one, two, *flat)


def second_back_kernel(groups, half, where_ref, signal_ref, w_ref, cur_ref, one_ref, two_ref, *refs):
    xs = [(refs[2 * g], refs[2 * g + 1]) for g in range(groups)]
    code_ref = refs[2 * groups]
    (x_buf, w_buf, cur_buf, one_buf, two_buf, grad, scale_buf, x_sem, s_sem) = refs[2 * groups + 1 :]
    copies = input_copies(where_ref, xs, x_buf, x_sem, half)
    guarded(where_ref, half, copies, "start")
    here = (slice(None), slice(half * HALF, (half + 1) * HALF))
    states = [
        pltpu.make_async_copy(w_ref.at[here], w_buf, s_sem.at[0]),
        pltpu.make_async_copy(cur_ref, cur_buf, s_sem.at[1]),
        pltpu.make_async_copy(one_ref, one_buf, s_sem.at[2]),
        pltpu.make_async_copy(two_ref, two_buf, s_sem.at[3]),
    ]
    for copy in states:
        copy.start()
    guarded(where_ref, half, copies, "wait")
    for copy in states:
        copy.wait()
    scale_buf[...] = jnp.zeros_like(scale_buf)
    blocks = COLS // BLOCK
    lane = lax.broadcasted_iota(jnp.int32, (TILE, BLOCK), 1)

    def consume(block, slot):
        for row in range(0, ROWS, TILE):
            rows = slice(row, row + TILE)
            scales = scale_buf[rows, :]
            for part in range(blocks):
                offset = pl.multiple_of(block * COLS + part * BLOCK, BLOCK)
                tile = (rows, pl.ds(offset, BLOCK))
                _, _, current = adam(
                    PRIOR_STEPS + 2,
                    grad[slot, rows, part * BLOCK : (part + 1) * BLOCK],
                    one_buf[tile],
                    two_buf[tile],
                    cur_buf[tile],
                )
                delta = w_buf[tile] - current
                top = jnp.max(jnp.abs(delta), axis=1, keepdims=True) + scale_epsilon
                scale = jnp.broadcast_to(top.astype(BF16).astype(F32), (TILE, BLOCK))
                code_ref[tile] = (delta / scale).astype(BF16)
                scales = jnp.where(lane == block * blocks + part, scale, scales)
            scale_buf[rows, :] = scales

    columns(signal_ref[...], x_buf, grad, consume)
    code_ref[:, HALF:] = scale_buf[...].astype(BF16)


def second_back(half, where, signal, weight, state, xs):
    flat = [ref for pair in xs for ref in pair]
    return pl.pallas_call(
        functools.partial(second_back_kernel, len(xs), half),
        out_shape=jax.ShapeDtypeStruct((ROWS, PAYLOAD), BF16),
        in_specs=[SM, VM] + [HB] * (4 + len(flat)),
        out_specs=VM,
        scratch_shapes=[
            pltpu.VMEM((HALF, TOK), BF16),
            pltpu.VMEM((ROWS, HALF), F32),
            pltpu.VMEM((ROWS, HALF), F32),
            pltpu.VMEM((ROWS, HALF), F32),
            pltpu.VMEM((ROWS, HALF), F32),
            pltpu.VMEM((2, ROWS, COLS), F32),
            pltpu.VMEM((ROWS, BLOCK), F32),
            pltpu.SemaphoreType.DMA((2 * SLOTS,)),
            pltpu.SemaphoreType.DMA((4,)),
        ],
        compiler_params=params(24),
        cost_estimate=pl.CostEstimate(
            flops=ROWS * WIDTH * TOK, bytes_accessed=12 << 20, transcendentals=0
        ),
        name="second_back",
    )(where, signal, weight, *state, *flat)


def partial_kernel(got_ref, out_ref, part, piece):
    sources, rows = got_ref.shape[0], got_ref.shape[1]
    scales = [got_ref[source, :, HALF:].astype(F32) for source in range(sources)]
    for block in range(HALF // BLOCK):
        here = slice(block * BLOCK, (block + 1) * BLOCK)
        total = jnp.zeros((rows, BLOCK), F32)
        for source in range(sources):
            scale = scales[source][:, block : block + 1]
            total = total + got_ref[source, :, here].astype(F32) * scale
        part[:, here] = total
    own = rows // 4
    for line in range(4):
        for group in range(4):
            piece[line, group * own : (group + 1) * own, :] = part[
                line * own : (line + 1) * own, group * QUARTER : (group + 1) * QUARTER
            ]
        out_ref[line] = piece[line].astype(BF16)


def partial_sums(got):
    sources, rows, _ = got.shape
    return pl.pallas_call(
        partial_kernel,
        out_shape=jax.ShapeDtypeStruct((4, rows, QUARTER), BF16),
        in_specs=[VM],
        out_specs=VM,
        scratch_shapes=[
            pltpu.VMEM((rows, HALF), F32),
            pltpu.VMEM((4, rows, QUARTER), F32),
        ],
        compiler_params=params(16),
        name="partial_sums",
    )(got)


def outer_kernel(half, got_ref, outer_ref, *refs):
    if half:
        before_ref, scales_ref, momentum_ref, code_ref, held, sent = refs
        momentum_ref[:, :HALF] = before_ref[...]
        scales = scales_ref[...]
    else:
        momentum_ref, scales_ref, code_ref, held, sent = refs
        scales = jnp.zeros(scales_ref.shape, F32)
    own = outer_ref.shape[0]
    first = half * HALF
    for group in range(4):
        at = first + group * QUARTER
        held[group * own : (group + 1) * own, :] = outer_ref[:, at : at + QUARTER]
    lane = lax.broadcasted_iota(jnp.int32, (4 * own, BLOCK), 1)
    blocks = QUARTER // BLOCK
    for block in range(blocks):
        here = slice(block * BLOCK, (block + 1) * BLOCK)
        total = got_ref[0, :, here].astype(F32)
        for source in range(1, 4):
            total = total + got_ref[source, :, here].astype(F32)
        average = total * (1.0 / 16)
        momentum = outer_mu * held[:, here] + average
        sent[:, here] = momentum
        update = average + outer_mu * momentum
        top = jnp.max(jnp.abs(update), axis=1, keepdims=True) + scale_epsilon
        scale = jnp.broadcast_to(top.astype(BF16).astype(F32), (4 * own, BLOCK))
        code_ref[:, here] = (update / scale).astype(BF16)
        scales = jnp.where(lane == half * blocks + block, scale, scales)
    if half:
        code_ref[:, QUARTER:] = scales.astype(BF16)
    else:
        scales_ref[...] = scales
    for group in range(4):
        at = first + group * QUARTER
        momentum_ref[:, at : at + QUARTER] = sent[group * own : (group + 1) * own, :]


def outer_step(half, got, outer_momentum, *before):
    own, width = outer_momentum.shape
    if half:
        out_shape = (
            jax.ShapeDtypeStruct((own, width), F32),
            jax.ShapeDtypeStruct((4 * own, QUARTER + BLOCK), BF16),
        )
    else:
        out_shape = (
            jax.ShapeDtypeStruct((own, HALF), F32),
            jax.ShapeDtypeStruct((4 * own, BLOCK), F32),
            jax.ShapeDtypeStruct((4 * own, QUARTER), BF16),
        )
    return pl.pallas_call(
        functools.partial(outer_kernel, half),
        out_shape=out_shape,
        in_specs=[VM] * (2 + len(before)),
        out_specs=tuple(VM for _ in out_shape),
        scratch_shapes=[
            pltpu.VMEM((4 * own, QUARTER), F32),
            pltpu.VMEM((4 * own, QUARTER), F32),
        ],
        compiler_params=params(16),
        name="outer_step",
    )(got, outer_momentum, *before)


def final_kernel(where_ref, w_ref, *refs):
    pieces = refs[:8]
    out_ref = refs[8]
    w_buf, got0, got1, block_buf, new_buf, w_sem, got_sem, out_sem = refs[9:]
    own = ROWS // 16
    load = pltpu.make_async_copy(w_ref, w_buf, w_sem)
    load.start()
    copies = []
    for half, got in enumerate((got0, got1)):
        for index in range(16):
            source = pieces[half * 4 + index // 4].at[pl.ds((index % 4) * 4 * own, 4 * own)]
            copies.append(
                pltpu.make_async_copy(source, got.at[where_ref[index]], got_sem.at[half * 16 + index])
            )
            copies[-1].start()
    for copy in copies:
        copy.wait()
    load.wait()
    outs = []
    blocks = QUARTER // BLOCK
    for x in range(4):
        for line in range(4):
            scales = got1[x * 4 + line, :, QUARTER:].astype(F32)
            for half, got in enumerate((got0, got1)):
                for block in range(blocks):
                    here = slice(block * BLOCK, (block + 1) * BLOCK)
                    lane = half * blocks + block
                    value = got[x * 4 + line, :, here].astype(F32) * scales[:, lane : lane + 1]
                    for group in range(4):
                        at = half * HALF + group * QUARTER + block * BLOCK
                        block_buf[line * own : (line + 1) * own, at : at + BLOCK] = value[
                            group * own : (group + 1) * own, :
                        ]
        rows = slice(x * 4 * own, (x + 1) * 4 * own)
        new_buf[rows, :] = w_buf[rows, :] - outer_rate * block_buf[...]
        outs.append(pltpu.make_async_copy(new_buf.at[rows], out_ref.at[rows], out_sem.at[x]))
        outs[-1].start()
    for copy in outs:
        copy.wait()


def final_step(where, weight, pieces):
    return pl.pallas_call(
        final_kernel,
        out_shape=jax.ShapeDtypeStruct((ROWS, WIDTH), F32),
        in_specs=[SM, HB] + [HB] * 8,
        out_specs=HB,
        scratch_shapes=[
            pltpu.VMEM((ROWS, WIDTH), F32),
            pltpu.VMEM((16, ROWS // 4, QUARTER), BF16),
            pltpu.VMEM((16, ROWS // 4, QUARTER + BLOCK), BF16),
            pltpu.VMEM((ROWS // 4, WIDTH), F32),
            pltpu.VMEM((ROWS, WIDTH), F32),
            pltpu.SemaphoreType.DMA,
            pltpu.SemaphoreType.DMA((32,)),
            pltpu.SemaphoreType.DMA((4,)),
        ],
        compiler_params=params(24),
        name="final_step",
    )(where, weight, *pieces)


def shift(value, axis, by):
    size = lax.axis_size(axis)
    return lax.ppermute(value, axis, [(i, (i + by) % size) for i in range(size)])


def after(value, *others):
    return lax.optimization_barrier((value,) + others)[0]


def swap(*chunks):
    own = jnp.concatenate(chunks, axis=0)
    return own, shift(own, "c", 1)


def spread(first, second):
    far1 = shift(first, "zh", 1)
    left1, right1 = shift(first, "y", 1), shift(first, "y", -1)
    opposite1 = shift(left1, "y", 1)
    right2 = shift(after(second, right1), "y", -1)
    far1, _, _ = lax.optimization_barrier((far1, opposite1, right2))
    far_left1, far_right1 = shift(far1, "y", 1), shift(far1, "y", -1)
    far2 = shift(after(second, far1), "zh", 1)
    left2 = shift(after(second, opposite1), "y", 1)
    near = swap(first, far1, left1, right1, opposite1)
    far_opposite1 = shift(far_right1, "y", -1)
    opposite2 = shift(left2, "y", 1)
    rest = swap(far_left1, far_right1, far_opposite1)
    far2, _ = lax.optimization_barrier((far2, far_opposite1))
    far_left2, far_right2 = shift(far2, "y", 1), shift(far2, "y", -1)
    far_opposite2 = shift(far_right2, "y", -1)
    near2 = swap(second, far2, left2, right2, opposite2)
    rest2 = swap(far_left2, far_right2, far_opposite2)
    return [near, rest], [near2, rest2]


def shards(weight, first_moment, second_moment, outer_momentum, act_table, token_ids, targets):
    y, zh, core = lax.axis_index("y"), lax.axis_index("zh"), lax.axis_index("c")
    x, zl = lax.axis_index("x"), lax.axis_index("zl")
    step_y = jnp.array([0, 0, -1, 1, 2, -1, 1, 2, 0], jnp.int32)
    step_z = jnp.array([0, 1, 0, 0, 0, 1, 1, 1, 0], jnp.int32)
    chip = ((y + step_y + 4) % 4) * 2 + (zh + step_z) % 2
    where = jnp.where(jnp.arange(9) == 8, core, chip).astype(jnp.int32)

    table_t = act_table.T
    ids = token_ids[0]
    wanted = jnp.transpose(targets[0], (0, 2, 1))
    inputs = spread(*[gather(ids[step : step + 1], table_t) for step in range(STEPS)])

    signal = forward(where, wanted[0], [weight], inputs[0])
    states = [
        first_back(half, where, signal, weight, first_moment[0], second_moment[0], inputs[0])
        for half in range(2)
    ]
    signal = forward(where, wanted[1], [state[0] for state in states], inputs[1])

    before, lines = (), []
    got = []
    for half in range(2):
        payload = second_back(half, where, signal, weight, states[half], inputs[1])
        got.append(lax.all_to_all(payload.reshape(4, ROWS // 4, PAYLOAD), "x", 0, 0, tiled=True))
    for half in range(2):
        sums = lax.all_to_all(partial_sums(got[half]), "zl", 0, 0, tiled=True)
        result = outer_step(half, sums, outer_momentum, *before)
        before, codes = result[:-1], result[-1]
        lines.append(jnp.concatenate([codes] + [shift(codes, "zl", by) for by in (1, 2, 3)], axis=0))
    momentum = before[0]
    pieces = []
    for line in lines:
        pieces += [line] + [shift(line, "x", by) for by in (1, 2, 3)]
    index = jnp.arange(16, dtype=jnp.int32)
    place = ((x - index // 4 + 4) % 4) * 4 + (zl - index % 4 + 4) % 4
    new_weight = final_step(place.astype(jnp.int32), weight, pieces)
    return (new_weight, momentum)


def solution(mesh):
    inner = Mesh(mesh.devices.reshape(4, 2, 2, 4, 4), ("y", "zh", "c", "x", "zl"))
    mp, replica = ("y", "zh", "c"), ("x", "zl")
    in_specs = (
        P(mp, None),
        P(replica, mp, None),
        P(replica, mp, None),
        P(mp + replica, None),
        P(None, mp),
        P(replica, None, None),
        P(replica, None, None, mp),
    )
    out_specs = (P(mp, None), P(mp + replica, None))
    return jax.shard_map(shards, mesh=inner, in_specs=in_specs, out_specs=out_specs, check_vma=False)
```

```python
import functools

import jax
import jax.numpy as jnp
from jax import lax
from jax.experimental import pallas as pl
from jax.experimental.pallas import tpu as pltpu
from jax.sharding import Mesh, PartitionSpec as P

STEPS = 2
BLOCK = 128
PRIOR_STEPS = 3

beta_first = 0.9
beta_second = 0.95
adam_epsilon = 1e-08
inner_rate = 0.1
weight_decay = 0.1
outer_mu = 0.9
outer_rate = 0.7
scale_epsilon = 1e-06

ROWS = 160
WIDTH = 5120
TOK = 512
CHUNK = 320
PAIR = 2 * CHUNK
SLOTS = 8
NEAR = 4
TILE = 16
HALF = WIDTH // 2
PAYLOAD = HALF + BLOCK
QROWS = ROWS // 4
OWN = ROWS // 16

F32 = jnp.float32
BF16 = jnp.bfloat16
FACTOR = WIDTH ** (-0.5)


HB = pl.BlockSpec(memory_space=pltpu.HBM)
VM = pl.BlockSpec(memory_space=pltpu.VMEM)
SM = pl.BlockSpec(memory_space=pltpu.SMEM)


def params(mib):
    return pltpu.CompilerParams(vmem_limit_bytes=mib << 20)


def gather_kernel(ids_ref, table_ref, out_ref):
    ids = ids_ref[...]
    total = jnp.zeros((CHUNK, TOK), F32)
    step = 512
    for start in range(0, table_ref.shape[1], step):
        row = lax.broadcasted_iota(jnp.int32, (step, TOK), 0) + start
        pick = jnp.where(row == ids, 1.0, 0.0).astype(BF16)
        total = total + jnp.dot(
            table_ref[:, start : start + step], pick, preferred_element_type=F32
        )
    out_ref[...] = total.astype(BF16)


def gather(ids, table_t):
    return pl.pallas_call(
        gather_kernel,
        out_shape=jax.ShapeDtypeStruct((CHUNK, TOK), BF16),
        in_specs=[VM, VM],
        out_specs=VM,
        compiler_params=params(16),
        name="gather",
    )(ids, table_t)


def pack_kernel(*refs):
    out_ref = refs[-1]
    rows = refs[0].shape[0]
    for index, ref in enumerate(refs[:-1]):
        out_ref[index * rows : (index + 1) * rows, :] = ref[...]


def pack(*chunks):
    rows, width = chunks[0].shape
    return pl.pallas_call(
        pack_kernel,
        out_shape=jax.ShapeDtypeStruct((len(chunks) * rows, width), chunks[0].dtype),
        in_specs=[VM] * len(chunks),
        out_specs=VM,
        compiler_params=params(8),
        name="pack",
    )(*chunks)


def input_copies(where_ref, xs, x_buf, sems):
    core = where_ref[SLOTS]
    mine = pl.multiple_of(core * CHUNK, CHUNK)
    other = pl.multiple_of((1 - core) * CHUNK, CHUNK)
    out, slot = [], 0
    for own_ref, other_ref in xs:
        for place in range(own_ref.shape[0] // CHUNK):
            rows = pl.ds(place * CHUNK, CHUNK)
            out.append(
                [
                    pltpu.make_async_copy(
                        own_ref.at[rows], x_buf.at[slot, pl.ds(mine, CHUNK)], sems.at[0, slot]
                    ),
                    pltpu.make_async_copy(
                        other_ref.at[rows], x_buf.at[slot, pl.ds(other, CHUNK)], sems.at[1, slot]
                    ),
                ]
            )
            slot += 1
    return out


def wait_inputs(xs, x_buf, sems, slot):
    rows = pl.ds(0, CHUNK)
    for index in range(2):
        pltpu.make_async_copy(xs[0][index].at[rows], x_buf.at[slot, rows], sems.at[index, slot]).wait()


def state_copy(where_ref, half, source, buf, sem, slot):
    if source.shape[1] == WIDTH:
        at = pl.multiple_of(where_ref[half * NEAR + slot] * PAIR, PAIR)
    else:
        at = pl.multiple_of(slot * PAIR, PAIR)
    return pltpu.make_async_copy(source.at[:, pl.ds(at, PAIR)], buf.at[slot], sem)


def pairs_of(refs):
    return [(refs[2 * g], refs[2 * g + 1]) for g in range(len(refs) // 2)]


def forward_kernel(half, count, where_ref, extra_ref, w_ref, *refs):
    xs = pairs_of(refs[:count])
    out_ref = refs[count]
    x_buf, w_buf, x_sem, w_sem = refs[count + 1 : count + 5]
    copies = input_copies(where_ref, xs, x_buf, x_sem)
    for slot in range(NEAR):
        copies[slot].append(state_copy(where_ref, half, w_ref, w_buf, w_sem.at[slot], slot))
        for copy in copies[slot]:
            copy.start()
    total = jnp.zeros((ROWS, TOK), F32)
    for slot in range(NEAR):
        for copy in copies[slot]:
            copy.wait()
        total = total + jnp.dot(w_buf[slot].astype(BF16), x_buf[slot], preferred_element_type=F32)
    if half == 0:
        out_ref[...] = total
    else:
        target_ref = refs[count + 5]
        out_ref[...] = ((total + extra_ref[...]) * FACTOR - target_ref[...].astype(F32)).astype(BF16)


def forward_near_kernel(count, where_ref, w_ref, *refs):
    forward_kernel(0, count, where_ref, None, w_ref, *refs)


def forward_rest_kernel(count, where_ref, total_ref, target_ref, w_ref, *refs):
    forward_kernel(1, count, where_ref, total_ref, w_ref, *refs, target_ref)


def forward(half, where, extra, weight, xs):
    flat = [ref for pair in xs for ref in pair]
    kernel = (forward_near_kernel, forward_rest_kernel)[half]
    return pl.pallas_call(
        functools.partial(kernel, len(flat)),
        out_shape=jax.ShapeDtypeStruct((ROWS, TOK), (F32, BF16)[half]),
        in_specs=[SM] + [VM] * len(extra) + [HB] * (1 + len(flat)),
        out_specs=VM,
        scratch_shapes=[
            pltpu.VMEM((NEAR, PAIR, TOK), BF16),
            pltpu.VMEM((NEAR, ROWS, PAIR), F32),
            pltpu.SemaphoreType.DMA((2, NEAR)),
            pltpu.SemaphoreType.DMA((NEAR,)),
        ],
        compiler_params=params(16),
        cost_estimate=pl.CostEstimate(
            flops=ROWS * WIDTH * TOK, bytes_accessed=5 << 20, transcendentals=0
        ),
        name="forward",
    )(where, *extra, weight, *flat)


def adam(step_count, gradient, one, two, current):
    one = beta_first * one + (1.0 - beta_first) * gradient
    two = beta_second * two + (1.0 - beta_second) * gradient * gradient
    update = (one * (1.0 / (1.0 - beta_first**step_count))) / (
        jnp.sqrt(two * (1.0 / (1.0 - beta_second**step_count))) + adam_epsilon
    )
    return one, two, current - inner_rate * (update + weight_decay * current)


def backward(signal_ref, xs, x_buf, x_sem, grad, consume):
    def product(slot, place):
        wait_inputs(xs, x_buf, x_sem, slot)
        grad[place] = lax.dot_general(
            signal_ref[...], x_buf[slot], (((1,), (1,)), ((), ())), preferred_element_type=F32
        ) * (FACTOR / TOK)

    product(0, 0)

    def body(slot, carry):
        product(slot + 1, (slot + 1) % 2)
        consume(slot, slot % 2)
        return carry

    lax.fori_loop(0, NEAR - 1, body, 0)
    consume(NEAR - 1, (NEAR - 1) % 2)


def first_back_kernel(half, count, where_ref, signal_ref, w_ref, one_ref, two_ref, *refs):
    xs = pairs_of(refs[:count])
    outs = refs[count : count + 3]
    (x_buf, w_buf, one_buf, two_buf, new, grad, x_sem, s_sem, o_sem) = refs[count + 3 :]
    states = ((w_ref, w_buf), (one_ref, one_buf), (two_ref, two_buf))
    for slot, copies in enumerate(input_copies(where_ref, xs, x_buf, x_sem)):
        for copy in copies:
            copy.start()
        for index, (source, buf) in enumerate(states):
            state_copy(where_ref, half, source, buf, s_sem.at[index, slot], slot).start()

    def out_copy(index, slot):
        at = pl.multiple_of(slot * PAIR, PAIR)
        return pltpu.make_async_copy(
            new.at[index, slot], outs[index].at[:, pl.ds(at, PAIR)], o_sem.at[index, slot]
        )

    def consume(slot, place):
        for index, (source, buf) in enumerate(states):
            state_copy(where_ref, half, source, buf, s_sem.at[index, slot], slot).wait()
        for row in range(0, ROWS, TILE):
            rows = slice(row, row + TILE)
            one, two, current = adam(
                PRIOR_STEPS + 1,
                grad[place, rows, :],
                one_buf[slot, rows, :].astype(F32),
                two_buf[slot, rows, :].astype(F32),
                w_buf[slot, rows, :],
            )
            for index, value in enumerate((current, one, two)):
                new[index, slot, rows, :] = value
        for index in range(3):
            out_copy(index, slot).start()

    backward(signal_ref, xs, x_buf, x_sem, grad, consume)
    for slot in range(NEAR):
        for index in range(3):
            out_copy(index, slot).wait()


def first_back(half, where, signal, weight, one, two, xs):
    flat = [ref for pair in xs for ref in pair]
    state = jax.ShapeDtypeStruct((ROWS, HALF), F32)
    return pl.pallas_call(
        functools.partial(first_back_kernel, half, len(flat)),
        out_shape=(state, state, state),
        in_specs=[SM, VM] + [HB] * (3 + len(flat)),
        out_specs=(HB, HB, HB),
        scratch_shapes=[
            pltpu.VMEM((NEAR, PAIR, TOK), BF16),
            pltpu.VMEM((NEAR, ROWS, PAIR), F32),
            pltpu.VMEM((NEAR, ROWS, PAIR), BF16),
            pltpu.VMEM((NEAR, ROWS, PAIR), BF16),
            pltpu.VMEM((3, NEAR, ROWS, PAIR), F32),
            pltpu.VMEM((2, ROWS, PAIR), F32),
            pltpu.SemaphoreType.DMA((2, NEAR)),
            pltpu.SemaphoreType.DMA((3, NEAR)),
            pltpu.SemaphoreType.DMA((3, NEAR)),
        ],
        compiler_params=params(20),
        cost_estimate=pl.CostEstimate(
            flops=ROWS * WIDTH * TOK, bytes_accessed=14 << 20, transcendentals=0
        ),
        name="first_back",
    )(where, signal, weight, one, two, *flat)


def second_back_kernel(half, count, where_ref, signal_ref, w_ref, cur_ref, one_ref, two_ref, *refs):
    xs = pairs_of(refs[:count])
    outs = refs[count : count + 4]
    (x_buf, w_buf, cur_buf, one_buf, two_buf, grad, scale_buf, code_buf, x_sem, s_sem, o_sem) = refs[
        count + 4 :
    ]
    states = ((w_ref, w_buf), (cur_ref, cur_buf), (one_ref, one_buf), (two_ref, two_buf))
    for slot, copies in enumerate(input_copies(where_ref, xs, x_buf, x_sem)):
        for copy in copies:
            copy.start()
        for index, (source, buf) in enumerate(states):
            state_copy(where_ref, half, source, buf, s_sem.at[index, slot], slot).start()
    scale_buf[...] = jnp.zeros_like(scale_buf)
    blocks = PAIR // BLOCK
    lane = lax.broadcasted_iota(jnp.int32, (QROWS, BLOCK), 1)

    def consume(slot, place):
        for index, (source, buf) in enumerate(states):
            state_copy(where_ref, half, source, buf, s_sem.at[index, slot], slot).wait()
        for quarter in range(4):
            rows = slice(quarter * QROWS, (quarter + 1) * QROWS)
            scales = scale_buf[quarter]
            for part in range(blocks):
                cols = slice(part * BLOCK, (part + 1) * BLOCK)
                _, _, current = adam(
                    PRIOR_STEPS + 2,
                    grad[place, rows, cols],
                    one_buf[slot, rows, cols],
                    two_buf[slot, rows, cols],
                    cur_buf[slot, rows, cols],
                )
                delta = w_buf[slot, rows, cols] - current
                top = jnp.max(jnp.abs(delta), axis=1, keepdims=True) + scale_epsilon
                scale = jnp.broadcast_to(top.astype(BF16).astype(F32), (QROWS, BLOCK))
                at = pl.multiple_of(slot * PAIR + part * BLOCK, BLOCK)
                code_buf[quarter, :, pl.ds(at, BLOCK)] = (delta / scale).astype(BF16)
                scales = jnp.where(lane == slot * blocks + part, scale, scales)
            scale_buf[quarter] = scales

    backward(signal_ref, xs, x_buf, x_sem, grad, consume)
    code_buf[:, :, HALF:] = scale_buf[...].astype(BF16)
    copies = []
    for by in range(4):
        quarter = (where_ref[SLOTS + 1] + by) % 4
        copies.append(pltpu.make_async_copy(code_buf.at[quarter], outs[by], o_sem.at[by]))
        copies[-1].start()
    for copy in copies:
        copy.wait()


def second_back(half, where, signal, weight, state, xs):
    flat = [ref for pair in xs for ref in pair]
    return pl.pallas_call(
        functools.partial(second_back_kernel, half, len(flat)),
        out_shape=(jax.ShapeDtypeStruct((QROWS, PAYLOAD), BF16),) * 4,
        in_specs=[SM, VM] + [HB] * (4 + len(flat)),
        out_specs=(HB,) * 4,
        scratch_shapes=[
            pltpu.VMEM((NEAR, PAIR, TOK), BF16),
            pltpu.VMEM((NEAR, ROWS, PAIR), F32),
            pltpu.VMEM((NEAR, ROWS, PAIR), F32),
            pltpu.VMEM((NEAR, ROWS, PAIR), F32),
            pltpu.VMEM((NEAR, ROWS, PAIR), F32),
            pltpu.VMEM((2, ROWS, PAIR), F32),
            pltpu.VMEM((4, QROWS, BLOCK), F32),
            pltpu.VMEM((4, QROWS, PAYLOAD), BF16),
            pltpu.SemaphoreType.DMA((2, NEAR)),
            pltpu.SemaphoreType.DMA((4, NEAR)),
            pltpu.SemaphoreType.DMA((4,)),
        ],
        compiler_params=params(20),
        cost_estimate=pl.CostEstimate(
            flops=ROWS * WIDTH * TOK, bytes_accessed=14 << 20, transcendentals=0
        ),
        name="second_back",
    )(where, signal, weight, *state, *flat)


def partial_kernel(where_ref, *refs):
    gots, outs = refs[:4], refs[4:8]
    part, piece = refs[8:]
    scales = [got[:, HALF:].astype(F32) for got in gots]
    for block in range(HALF // BLOCK):
        here = slice(block * BLOCK, (block + 1) * BLOCK)
        total = jnp.zeros((QROWS, BLOCK), F32)
        for got, scale in zip(gots, scales):
            total = total + got[:, here].astype(F32) * scale[:, block : block + 1]
        part[:, here] = total
    for line in range(4):
        for group in range(NEAR):
            piece[line, group * OWN : (group + 1) * OWN, :] = part[
                line * OWN : (line + 1) * OWN, group * PAIR : (group + 1) * PAIR
            ]
    for by in range(4):
        outs[by][...] = piece[(where_ref[SLOTS + 2] + by) % 4].astype(BF16)


def partial_sums(where, gots):
    return pl.pallas_call(
        partial_kernel,
        out_shape=(jax.ShapeDtypeStruct((QROWS, PAIR), BF16),) * 4,
        in_specs=[SM] + [VM] * 4,
        out_specs=(VM,) * 4,
        scratch_shapes=[
            pltpu.VMEM((QROWS, HALF), F32),
            pltpu.VMEM((4, QROWS, PAIR), F32),
        ],
        compiler_params=params(8),
        name="partial_sums",
    )(where, *gots)


def outer_kernel(half, where_ref, outer_ref, *refs):
    gots, refs = refs[:4], refs[4:]
    if half:
        before_ref, scales_ref, momentum_ref, code_ref, held, sent = refs
        scales = scales_ref[...]
    else:
        sent, scales_ref, code_ref, held = refs
        scales = jnp.zeros(scales_ref.shape, F32)

    def column(slot):
        return pl.ds(pl.multiple_of(where_ref[slot] * PAIR, PAIR), PAIR)

    for group in range(NEAR):
        held[group * OWN : (group + 1) * OWN, :] = outer_ref[:, column(half * NEAR + group)]
    lane = lax.broadcasted_iota(jnp.int32, (QROWS, BLOCK), 1)
    blocks = PAIR // BLOCK
    for block in range(blocks):
        here = slice(block * BLOCK, (block + 1) * BLOCK)
        total = gots[0][:, here].astype(F32)
        for got in gots[1:]:
            total = total + got[:, here].astype(F32)
        average = total * (1.0 / 16)
        momentum = outer_mu * held[:, here] + average
        sent[:, here] = momentum
        update = average + outer_mu * momentum
        top = jnp.max(jnp.abs(update), axis=1, keepdims=True) + scale_epsilon
        scale = jnp.broadcast_to(top.astype(BF16).astype(F32), (QROWS, BLOCK))
        code_ref[:, here] = (update / scale).astype(BF16)
        scales = jnp.where(lane == half * blocks + block, scale, scales)
    if not half:
        scales_ref[...] = scales
        return
    code_ref[:, PAIR:] = scales.astype(BF16)
    for group in range(NEAR):
        rows = slice(group * OWN, (group + 1) * OWN)
        momentum_ref[:, column(group)] = before_ref[rows, :]
        momentum_ref[:, column(NEAR + group)] = sent[rows, :]


def outer_step(half, where, outer_momentum, gots, *before):
    scratch = [pltpu.VMEM((QROWS, PAIR), F32)]
    if half:
        out_shape = (
            jax.ShapeDtypeStruct((OWN, WIDTH), F32),
            jax.ShapeDtypeStruct((QROWS, PAIR + BLOCK), BF16),
        )
        scratch = scratch * 2
    else:
        out_shape = (
            jax.ShapeDtypeStruct((QROWS, PAIR), F32),
            jax.ShapeDtypeStruct((QROWS, BLOCK), F32),
            jax.ShapeDtypeStruct((QROWS, PAIR), BF16),
        )
    return pl.pallas_call(
        functools.partial(outer_kernel, half),
        out_shape=out_shape,
        in_specs=[SM] + [VM] * (5 + len(before)),
        out_specs=tuple(VM for _ in out_shape),
        scratch_shapes=scratch,
        compiler_params=params(8),
        name="outer_step",
    )(where, outer_momentum, *gots, *before)


def final_kernel(where_ref, place_ref, w_ref, *refs):
    pieces = refs[:8]
    out_ref = refs[8]
    w_buf, got0, got1, block_buf, new_buf, w_sem, got_sem, out_sem = refs[9:]
    load = pltpu.make_async_copy(w_ref, w_buf, w_sem)
    load.start()
    copies = []
    for half, got in enumerate((got0, got1)):
        for index in range(16):
            source = pieces[half * 4 + index // 4].at[pl.ds((index % 4) * QROWS, QROWS)]
            copies.append(
                pltpu.make_async_copy(source, got.at[place_ref[index]], got_sem.at[half * 16 + index])
            )
            copies[-1].start()
    for copy in copies:
        copy.wait()
    load.wait()
    outs = []
    blocks = PAIR // BLOCK
    for x in range(4):
        for line in range(4):
            scales = got1[x * 4 + line, :, PAIR:].astype(F32)
            for half, got in enumerate((got0, got1)):
                for block in range(blocks):
                    here = slice(block * BLOCK, (block + 1) * BLOCK)
                    lane = half * blocks + block
                    value = got[x * 4 + line, :, here].astype(F32) * scales[:, lane : lane + 1]
                    for group in range(NEAR):
                        at = (half * NEAR + group) * PAIR + block * BLOCK
                        block_buf[line * OWN : (line + 1) * OWN, at : at + BLOCK] = value[
                            group * OWN : (group + 1) * OWN, :
                        ]
        rows = slice(x * QROWS, (x + 1) * QROWS)
        for slot in range(SLOTS):
            there = pl.ds(pl.multiple_of(where_ref[slot] * PAIR, PAIR), PAIR)
            new_buf[rows, there] = (
                w_buf[rows, there] - outer_rate * block_buf[:, slot * PAIR : (slot + 1) * PAIR]
            )
        outs.append(pltpu.make_async_copy(new_buf.at[rows], out_ref.at[rows], out_sem.at[x]))
        outs[-1].start()
    for copy in outs:
        copy.wait()


def final_step(where, place, weight, pieces):
    return pl.pallas_call(
        final_kernel,
        out_shape=jax.ShapeDtypeStruct((ROWS, WIDTH), F32),
        in_specs=[SM, SM, HB] + [HB] * 8,
        out_specs=HB,
        scratch_shapes=[
            pltpu.VMEM((ROWS, WIDTH), F32),
            pltpu.VMEM((16, QROWS, PAIR), BF16),
            pltpu.VMEM((16, QROWS, PAIR + BLOCK), BF16),
            pltpu.VMEM((QROWS, WIDTH), F32),
            pltpu.VMEM((ROWS, WIDTH), F32),
            pltpu.SemaphoreType.DMA,
            pltpu.SemaphoreType.DMA((32,)),
            pltpu.SemaphoreType.DMA((4,)),
        ],
        compiler_params=params(20),
        name="final_step",
    )(where, place, weight, *pieces)


def shift(value, axis, by):
    size = lax.axis_size(axis)
    return lax.ppermute(value, axis, [(i, (i + by) % size) for i in range(size)])


def after(value, *others):
    return lax.optimization_barrier((value,) + others)[0]


def swap(own):
    return own, shift(own, "c", 1)


def shards(weight, first_moment, second_moment, outer_momentum, act_table, token_ids, targets):
    y, zh, core = lax.axis_index("y"), lax.axis_index("zh"), lax.axis_index("c")
    x, zl = lax.axis_index("x"), lax.axis_index("zl")
    step_y = jnp.array([0, 0, -1, 1, 2, -1, 1, 2, 0, 0, 0], jnp.int32)
    step_z = jnp.array([0, 1, 0, 0, 0, 1, 1, 1, 0, 0, 0], jnp.int32)
    chip = ((y + step_y + 4) % 4) * 2 + (zh + step_z) % 2
    entry = jnp.arange(11)
    where = jnp.where(entry == 8, core, jnp.where(entry == 9, x, jnp.where(entry == 10, zl, chip)))
    where = where.astype(jnp.int32)
    index = jnp.arange(16, dtype=jnp.int32)
    place = ((x - index // 4 + 4) % 4) * 4 + (zl - index % 4 + 4) % 4
    place = place.astype(jnp.int32)

    table_t = act_table.T
    ids = token_ids[0]
    wanted = jnp.transpose(targets[0], (0, 2, 1))
    own1, own2 = [gather(ids[step : step + 1], table_t) for step in range(STEPS)]

    far1 = shift(own1, "zh", 1)
    left1, right1 = shift(own1, "y", 1), shift(own1, "y", -1)
    opposite1 = shift(left1, "y", 1)
    right2 = shift(after(own2, right1), "y", -1)
    far2 = shift(after(own2, far1), "zh", 1)
    near1 = swap(pack(own1, far1, left1, right1))
    far_left1 = shift(after(far1, opposite1), "y", 1)
    far_right1 = shift(after(far1, right2), "y", -1)
    left2 = shift(after(own2, opposite1), "y", 1)
    far_opposite1 = shift(far_right1, "y", -1)
    rest1 = swap(pack(opposite1, far_left1, far_right1, far_opposite1))

    total = forward(0, where, (), weight, [near1])
    total, far2, left2 = lax.optimization_barrier((total, far2, left2))
    far_left2, far_right2 = shift(far2, "y", 1), shift(far2, "y", -1)
    opposite2 = shift(left2, "y", 1)
    near2 = swap(pack(own2, far2, left2, right2))
    signal = forward(1, where, (total, wanted[0]), weight, [rest1])
    state0 = first_back(0, where, signal, weight, first_moment[0], second_moment[0], [near1])
    far_opposite2 = shift(after(far_right2, state0[0]), "y", -1)
    state1 = first_back(1, where, signal, weight, first_moment[0], second_moment[0], [rest1])
    rest2 = swap(pack(opposite2, far_left2, far_right2))
    total = forward(0, where, (), state0[0], [near2])
    last2 = swap(after(far_opposite2, total, state1[0]))
    signal = forward(1, where, (total, wanted[1]), state1[0], [rest2, last2])

    payloads = []
    for half, (state, xs) in enumerate(((state0, [near2]), (state1, [rest2, last2]))):
        sends = second_back(half, where, signal, weight, state, xs)
        payloads.append([sends[0]] + [shift(sends[by], "x", by) for by in (1, 2, 3)])
    before, pieces = (), []
    for half in range(2):
        sends = partial_sums(where, payloads[half])
        sums = [sends[0]] + [shift(sends[by], "zl", by) for by in (1, 2, 3)]
        result = outer_step(half, where, outer_momentum, sums, *before)
        before, codes = result[:-1], result[-1]
        line = pack(codes, *[shift(codes, "zl", by) for by in (1, 2, 3)])
        pieces += [line] + [shift(line, "x", by) for by in (1, 2, 3)]
    momentum = before[0]
    new_weight = final_step(where, place, weight, pieces)
    return (new_weight, momentum)


def solution(mesh):
    inner = Mesh(mesh.devices.reshape(4, 2, 2, 4, 4), ("y", "zh", "c", "x", "zl"))
    mp, replica = ("y", "zh", "c"), ("x", "zl")
    in_specs = (
        P(mp, None),
        P(replica, mp, None),
        P(replica, mp, None),
        P(mp + replica, None),
        P(None, mp),
        P(replica, None, None),
        P(replica, None, None, mp),
    )
    out_specs = (P(mp, None), P(mp + replica, None))
    return jax.shard_map(shards, mesh=inner, in_specs=in_specs, out_specs=out_specs, check_vma=False)
```

```python
import functools

import jax
import jax.numpy as jnp
from jax import lax
from jax.experimental import pallas as pl
from jax.experimental.pallas import tpu as pltpu
from jax.sharding import Mesh, PartitionSpec as P


STEPS = 2
BLOCK = 128
PRIOR_STEPS = 3

beta_first = 0.9
beta_second = 0.95
adam_epsilon = 1e-08
inner_rate = 0.1
weight_decay = 0.1
outer_mu = 0.9
outer_rate = 0.7
scale_epsilon = 1e-06

ROWS = 160
WIDTH = 5120
TOK = 512
CHUNK = 320
PAIR = 2 * CHUNK
SLOTS = 8
NEAR = 4
TILE = 16
HALF = WIDTH // 2
PAYLOAD = HALF + BLOCK
QROWS = ROWS // 4
OWN = ROWS // 16

F32 = jnp.float32
BF16 = jnp.bfloat16
FACTOR = WIDTH ** (-0.5)


HB = pl.BlockSpec(memory_space=pltpu.HBM)
VM = pl.BlockSpec(memory_space=pltpu.VMEM)
SM = pl.BlockSpec(memory_space=pltpu.SMEM)


def params(mib):
    return pltpu.CompilerParams(vmem_limit_bytes=mib << 20)


def gather_kernel(ids_ref, table_ref, out_ref, total):
    step = 512
    total[...] = jnp.zeros_like(total)

    def body(block, carry):
        start = pl.multiple_of(block * step, step)
        row = lax.broadcasted_iota(jnp.int32, (step, TOK), 0) + start
        pick = jnp.where(row == ids_ref[...], 1.0, 0.0).astype(BF16)
        total[...] += jnp.dot(table_ref[:, pl.ds(start, step)], pick, preferred_element_type=F32)
        return carry

    lax.fori_loop(0, table_ref.shape[1] // step, body, 0)
    out_ref[...] = total[...].astype(BF16)


def gather(ids, table_t):
    return pl.pallas_call(
        gather_kernel,
        out_shape=jax.ShapeDtypeStruct((CHUNK, TOK), BF16),
        in_specs=[VM, VM],
        out_specs=VM,
        scratch_shapes=[pltpu.VMEM((CHUNK, TOK), F32)],
        compiler_params=params(16),
        name="gather",
    )(ids, table_t)


def pack_kernel(*refs):
    out_ref = refs[-1]
    rows = refs[0].shape[0]
    for index, ref in enumerate(refs[:-1]):
        out_ref[index * rows : (index + 1) * rows, :] = ref[...]


def pack(*chunks):
    rows, width = chunks[0].shape
    return pl.pallas_call(
        pack_kernel,
        out_shape=jax.ShapeDtypeStruct((len(chunks) * rows, width), chunks[0].dtype),
        in_specs=[VM] * len(chunks),
        out_specs=VM,
        compiler_params=params(8),
        name="pack",
    )(*chunks)


def input_copies(where_ref, xs, x_buf, sems):
    core = where_ref[SLOTS]
    mine = pl.multiple_of(core * CHUNK, CHUNK)
    other = pl.multiple_of((1 - core) * CHUNK, CHUNK)
    out, slot = [], 0
    for own_ref, other_ref in xs:
        for place in range(own_ref.shape[0] // CHUNK):
            rows = pl.ds(place * CHUNK, CHUNK)
            out.append(
                [
                    pltpu.make_async_copy(
                        own_ref.at[rows], x_buf.at[slot, pl.ds(mine, CHUNK)], sems.at[0, slot]
                    ),
                    pltpu.make_async_copy(
                        other_ref.at[rows], x_buf.at[slot, pl.ds(other, CHUNK)], sems.at[1, slot]
                    ),
                ]
            )
            slot += 1
    return out


def wait_inputs(xs, x_buf, sems, slot):
    rows = pl.ds(0, CHUNK)
    for index in range(2):
        pltpu.make_async_copy(xs[0][index].at[rows], x_buf.at[slot, rows], sems.at[index, slot]).wait()


def state_copy(where_ref, half, source, buf, sem, slot):
    if source.shape[1] == WIDTH:
        at = pl.multiple_of(where_ref[half * NEAR + slot] * PAIR, PAIR)
    else:
        at = pl.multiple_of(slot * PAIR, PAIR)
    return pltpu.make_async_copy(source.at[:, pl.ds(at, PAIR)], buf.at[slot], sem)


def pairs_of(refs):
    return [(refs[2 * g], refs[2 * g + 1]) for g in range(len(refs) // 2)]


def forward_kernel(half, count, where_ref, extra_ref, w_ref, *refs):
    xs = pairs_of(refs[:count])
    out_ref = refs[count]
    x_buf, w_buf, total, x_sem, w_sem = refs[count + 1 : count + 6]
    copies = input_copies(where_ref, xs, x_buf, x_sem)
    for slot in range(NEAR):
        for copy in copies[slot]:
            copy.start()
        state_copy(where_ref, half, w_ref, w_buf, w_sem.at[slot], slot).start()
    total[...] = jnp.zeros_like(total) if half == 0 else extra_ref[...]

    def body(slot, carry):
        wait_inputs(xs, x_buf, x_sem, slot)
        state_copy(where_ref, half, w_ref, w_buf, w_sem.at[slot], slot).wait()
        total[...] += jnp.dot(w_buf[slot].astype(BF16), x_buf[slot], preferred_element_type=F32)
        return carry

    lax.fori_loop(0, NEAR, body, 0)
    if half == 0:
        out_ref[...] = total[...]
    else:
        target_ref = refs[count + 6]
        out_ref[...] = (total[...] * FACTOR - target_ref[...].astype(F32)).astype(BF16)


def forward_near_kernel(count, where_ref, w_ref, *refs):
    forward_kernel(0, count, where_ref, None, w_ref, *refs)


def forward_rest_kernel(count, where_ref, total_ref, target_ref, w_ref, *refs):
    forward_kernel(1, count, where_ref, total_ref, w_ref, *refs, target_ref)


def forward(half, where, extra, weight, xs):
    flat = [ref for pair in xs for ref in pair]
    kernel = (forward_near_kernel, forward_rest_kernel)[half]
    return pl.pallas_call(
        functools.partial(kernel, len(flat)),
        out_shape=jax.ShapeDtypeStruct((ROWS, TOK), (F32, BF16)[half]),
        in_specs=[SM] + [VM] * len(extra) + [HB] * (1 + len(flat)),
        out_specs=VM,
        scratch_shapes=[
            pltpu.VMEM((NEAR, PAIR, TOK), BF16),
            pltpu.VMEM((NEAR, ROWS, PAIR), weight.dtype),
            pltpu.VMEM((ROWS, TOK), F32),
            pltpu.SemaphoreType.DMA((2, NEAR)),
            pltpu.SemaphoreType.DMA((NEAR,)),
        ],
        compiler_params=params(12),
        cost_estimate=pl.CostEstimate(
            flops=ROWS * WIDTH * TOK, bytes_accessed=5 << 20, transcendentals=0
        ),
        name="forward",
    )(where, *extra, weight, *flat)


def corrections(step_count):
    return 1.0 / (1.0 - beta_first**step_count), 1.0 / (1.0 - beta_second**step_count)


def first_adam(gradient, one, two, weight):
    first, second = corrections(PRIOR_STEPS + 1)
    one = beta_first * one + (1.0 - beta_first) * gradient
    two = beta_second * two + (1.0 - beta_second) * gradient * gradient
    update = (one * first) / (jnp.sqrt(two * second) + adam_epsilon)
    current = weight - inner_rate * (update + weight_decay * weight)
    first, second = corrections(PRIOR_STEPS + 2)
    kept = weight - (1.0 - inner_rate * weight_decay) * current
    return current, one * (beta_first * first), two * (beta_second * second), kept


def second_adam(gradient, one, two, kept):
    first, second = corrections(PRIOR_STEPS + 2)
    one = one + ((1.0 - beta_first) * first) * gradient
    two = two + ((1.0 - beta_second) * second) * (gradient * gradient)
    return kept + inner_rate * (one / (jnp.sqrt(two) + adam_epsilon))


def backward(signal_ref, xs, x_buf, x_sem, grad, consume):
    def product(slot, place):
        grad[place] = lax.dot_general(
            signal_ref[...], x_buf[slot], (((1,), (1,)), ((), ())), preferred_element_type=F32
        ) * (FACTOR / TOK)

    wait_inputs(xs, x_buf, x_sem, 0)
    product(0, 0)

    def body(slot, carry):
        following = jnp.minimum(slot + 1, NEAR - 1)

        @pl.when(slot + 1 < NEAR)
        def _():
            wait_inputs(xs, x_buf, x_sem, following)

        product(following, (slot + 1) % 2)
        consume(slot, slot % 2)
        return carry

    lax.fori_loop(0, NEAR, body, 0)


def first_back_kernel(half, count, where_ref, signal_ref, w_ref, one_ref, two_ref, *refs):
    xs = pairs_of(refs[:count])
    cur_ref, *outs = refs[count : count + 4]
    (x_buf, w_buf, one_buf, two_buf, cur_new, new, grad, x_sem, s_sem, o_sem) = refs[count + 4 :]
    states = ((w_ref, w_buf), (one_ref, one_buf), (two_ref, two_buf))
    for slot, copies in enumerate(input_copies(where_ref, xs, x_buf, x_sem)):
        for copy in copies:
            copy.start()
        for index, (source, buf) in enumerate(states):
            state_copy(where_ref, half, source, buf, s_sem.at[index, slot], slot).start()

    def out_copies(slot):
        at = pl.ds(pl.multiple_of(slot * PAIR, PAIR), PAIR)
        copies = [pltpu.make_async_copy(cur_new.at[slot], cur_ref.at[:, at], o_sem.at[3, slot])]
        for index in range(3):
            copies.append(
                pltpu.make_async_copy(new.at[index, slot], outs[index].at[:, at], o_sem.at[index, slot])
            )
        return copies

    def consume(slot, place):
        for index, (source, buf) in enumerate(states):
            state_copy(where_ref, half, source, buf, s_sem.at[index, slot], slot).wait()
        for row in range(0, ROWS, TILE):
            rows = slice(row, row + TILE)
            current, *values = first_adam(
                grad[place, rows, :],
                one_buf[slot, rows, :].astype(F32),
                two_buf[slot, rows, :].astype(F32),
                w_buf[slot, rows, :],
            )
            cur_new[slot, rows, :] = current.astype(BF16)
            for index, value in enumerate(values):
                new[index, slot, rows, :] = value
        for copy in out_copies(slot):
            copy.start()

    backward(signal_ref, xs, x_buf, x_sem, grad, consume)
    for slot in range(NEAR):
        for copy in out_copies(slot):
            copy.wait()


def first_back(half, where, signal, weight, one, two, xs):
    flat = [ref for pair in xs for ref in pair]
    state = jax.ShapeDtypeStruct((ROWS, HALF), F32)
    return pl.pallas_call(
        functools.partial(first_back_kernel, half, len(flat)),
        out_shape=(jax.ShapeDtypeStruct((ROWS, HALF), BF16), state, state, state),
        in_specs=[SM, VM] + [HB] * (3 + len(flat)),
        out_specs=(HB,) * 4,
        scratch_shapes=[
            pltpu.VMEM((NEAR, PAIR, TOK), BF16),
            pltpu.VMEM((NEAR, ROWS, PAIR), F32),
            pltpu.VMEM((NEAR, ROWS, PAIR), BF16),
            pltpu.VMEM((NEAR, ROWS, PAIR), BF16),
            pltpu.VMEM((NEAR, ROWS, PAIR), BF16),
            pltpu.VMEM((3, NEAR, ROWS, PAIR), F32),
            pltpu.VMEM((2, ROWS, PAIR), F32),
            pltpu.SemaphoreType.DMA((2, NEAR)),
            pltpu.SemaphoreType.DMA((3, NEAR)),
            pltpu.SemaphoreType.DMA((4, NEAR)),
        ],
        compiler_params=params(20),
        cost_estimate=pl.CostEstimate(
            flops=ROWS * WIDTH * TOK, bytes_accessed=14 << 20, transcendentals=0
        ),
        name="first_back",
    )(where, signal, weight, one, two, *flat)


def second_back_kernel(half, count, where_ref, signal_ref, one_ref, two_ref, kept_ref, *refs):
    xs = pairs_of(refs[:count])
    outs = refs[count : count + 4]
    (x_buf, one_buf, two_buf, kept_buf, grad, scale_buf, code_buf, x_sem, s_sem, o_sem) = refs[count + 4 :]
    states = ((one_ref, one_buf), (two_ref, two_buf), (kept_ref, kept_buf))
    for slot, copies in enumerate(input_copies(where_ref, xs, x_buf, x_sem)):
        for copy in copies:
            copy.start()
        for index, (source, buf) in enumerate(states):
            state_copy(where_ref, half, source, buf, s_sem.at[index, slot], slot).start()
    scale_buf[...] = jnp.zeros_like(scale_buf)
    blocks = PAIR // BLOCK
    lane = lax.broadcasted_iota(jnp.int32, (QROWS, BLOCK), 1)

    def consume(slot, place):
        for index, (source, buf) in enumerate(states):
            state_copy(where_ref, half, source, buf, s_sem.at[index, slot], slot).wait()
        for quarter in range(4):
            rows = slice(quarter * QROWS, (quarter + 1) * QROWS)
            scales = scale_buf[quarter]
            for part in range(blocks):
                cols = slice(part * BLOCK, (part + 1) * BLOCK)
                delta = second_adam(
                    grad[place, rows, cols],
                    one_buf[slot, rows, cols],
                    two_buf[slot, rows, cols],
                    kept_buf[slot, rows, cols],
                )
                top = jnp.max(jnp.abs(delta), axis=1, keepdims=True) + scale_epsilon
                scale = jnp.broadcast_to(top.astype(BF16).astype(F32), (QROWS, BLOCK))
                at = pl.multiple_of(slot * PAIR + part * BLOCK, BLOCK)
                code_buf[quarter, :, pl.ds(at, BLOCK)] = (delta / scale).astype(BF16)
                scales = jnp.where(lane == slot * blocks + part, scale, scales)
            scale_buf[quarter] = scales

    backward(signal_ref, xs, x_buf, x_sem, grad, consume)
    code_buf[:, :, HALF:] = scale_buf[...].astype(BF16)
    copies = []
    for by in range(4):
        quarter = (where_ref[SLOTS + 1] + by) % 4
        copies.append(pltpu.make_async_copy(code_buf.at[quarter], outs[by], o_sem.at[by]))
        copies[-1].start()
    for copy in copies:
        copy.wait()


def second_back(half, where, signal, state, xs):
    flat = [ref for pair in xs for ref in pair]
    return pl.pallas_call(
        functools.partial(second_back_kernel, half, len(flat)),
        out_shape=(jax.ShapeDtypeStruct((QROWS, PAYLOAD), BF16),) * 4,
        in_specs=[SM, VM] + [HB] * (3 + len(flat)),
        out_specs=(HB,) * 4,
        scratch_shapes=[
            pltpu.VMEM((NEAR, PAIR, TOK), BF16),
            pltpu.VMEM((NEAR, ROWS, PAIR), F32),
            pltpu.VMEM((NEAR, ROWS, PAIR), F32),
            pltpu.VMEM((NEAR, ROWS, PAIR), F32),
            pltpu.VMEM((2, ROWS, PAIR), F32),
            pltpu.VMEM((4, QROWS, BLOCK), F32),
            pltpu.VMEM((4, QROWS, PAYLOAD), BF16),
            pltpu.SemaphoreType.DMA((2, NEAR)),
            pltpu.SemaphoreType.DMA((3, NEAR)),
            pltpu.SemaphoreType.DMA((4,)),
        ],
        compiler_params=params(20),
        cost_estimate=pl.CostEstimate(
            flops=ROWS * WIDTH * TOK, bytes_accessed=14 << 20, transcendentals=0
        ),
        name="second_back",
    )(where, signal, *state, *flat)


def partial_kernel(where_ref, *refs):
    gots, outs = refs[:4], refs[4:8]
    part, piece = refs[8:]
    scales = [got[:, HALF:].astype(F32) for got in gots]
    for block in range(HALF // BLOCK):
        here = slice(block * BLOCK, (block + 1) * BLOCK)
        total = jnp.zeros((QROWS, BLOCK), F32)
        for got, scale in zip(gots, scales):
            total = total + got[:, here].astype(F32) * scale[:, block : block + 1]
        part[:, here] = total
    for line in range(4):
        for group in range(NEAR):
            piece[line, group * OWN : (group + 1) * OWN, :] = part[
                line * OWN : (line + 1) * OWN, group * PAIR : (group + 1) * PAIR
            ]
    for by in range(4):
        outs[by][...] = piece[(where_ref[SLOTS + 2] + by) % 4].astype(BF16)


def partial_sums(where, gots):
    return pl.pallas_call(
        partial_kernel,
        out_shape=(jax.ShapeDtypeStruct((QROWS, PAIR), BF16),) * 4,
        in_specs=[SM] + [VM] * 4,
        out_specs=(VM,) * 4,
        scratch_shapes=[
            pltpu.VMEM((QROWS, HALF), F32),
            pltpu.VMEM((4, QROWS, PAIR), F32),
        ],
        compiler_params=params(8),
        name="partial_sums",
    )(where, *gots)


def outer_kernel(half, where_ref, outer_ref, *refs):
    gots, refs = refs[:4], refs[4:]
    if half:
        before_ref, scales_ref, momentum_ref, code_ref, held, sent = refs
        scales = scales_ref[...]
    else:
        sent, scales_ref, code_ref, held = refs
        scales = jnp.zeros(scales_ref.shape, F32)

    def column(slot):
        return pl.ds(pl.multiple_of(where_ref[slot] * PAIR, PAIR), PAIR)

    for group in range(NEAR):
        held[group * OWN : (group + 1) * OWN, :] = outer_ref[:, column(half * NEAR + group)]
    lane = lax.broadcasted_iota(jnp.int32, (QROWS, BLOCK), 1)
    blocks = PAIR // BLOCK
    for block in range(blocks):
        here = slice(block * BLOCK, (block + 1) * BLOCK)
        total = gots[0][:, here].astype(F32)
        for got in gots[1:]:
            total = total + got[:, here].astype(F32)
        average = total * (1.0 / 16)
        momentum = outer_mu * held[:, here] + average
        sent[:, here] = momentum
        update = average + outer_mu * momentum
        top = jnp.max(jnp.abs(update), axis=1, keepdims=True) + scale_epsilon
        scale = jnp.broadcast_to(top.astype(BF16).astype(F32), (QROWS, BLOCK))
        code_ref[:, here] = (update / scale).astype(BF16)
        scales = jnp.where(lane == half * blocks + block, scale, scales)
    if not half:
        scales_ref[...] = scales
        return
    code_ref[:, PAIR:] = scales.astype(BF16)
    for group in range(NEAR):
        rows = slice(group * OWN, (group + 1) * OWN)
        momentum_ref[:, column(group)] = before_ref[rows, :]
        momentum_ref[:, column(NEAR + group)] = sent[rows, :]


def outer_step(half, where, outer_momentum, gots, *before):
    scratch = [pltpu.VMEM((QROWS, PAIR), F32)]
    if half:
        out_shape = (
            jax.ShapeDtypeStruct((OWN, WIDTH), F32),
            jax.ShapeDtypeStruct((QROWS, PAIR + BLOCK), BF16),
        )
        scratch = scratch * 2
    else:
        out_shape = (
            jax.ShapeDtypeStruct((QROWS, PAIR), F32),
            jax.ShapeDtypeStruct((QROWS, BLOCK), F32),
            jax.ShapeDtypeStruct((QROWS, PAIR), BF16),
        )
    return pl.pallas_call(
        functools.partial(outer_kernel, half),
        out_shape=out_shape,
        in_specs=[SM] + [VM] * (5 + len(before)),
        out_specs=tuple(VM for _ in out_shape),
        scratch_shapes=scratch,
        compiler_params=params(8),
        name="outer_step",
    )(where, outer_momentum, *gots, *before)


def final_kernel(where_ref, w_ref, *refs):
    pieces = refs[:8]
    out_ref = refs[8]
    new_buf, out_sem = refs[9:]
    x, zl = where_ref[SLOTS + 1], where_ref[SLOTS + 2]
    to = lax.broadcasted_iota(jnp.int32, (ROWS, ROWS), 0)
    source = lax.broadcasted_iota(jnp.int32, (ROWS, ROWS), 1)
    group, line, row = to // QROWS, (to % QROWS) // OWN, to % OWN
    wanted = ((zl - line + 4) % 4) * QROWS + group * OWN + row
    order = jnp.where(source == wanted, 1.0, 0.0).astype(BF16)
    blocks = PAIR // BLOCK

    def ordered(value):
        return jnp.dot(order, value, preferred_element_type=F32)

    copies = []
    for by in range(4):
        rows = pl.ds(pl.multiple_of(((x - by + 4) % 4) * QROWS, 8), QROWS)
        scales = ordered(pieces[4 + by][:, PAIR:])
        for half in range(2):
            codes = ordered(pieces[half * 4 + by][:, :PAIR])
            for group in range(NEAR):
                here = slice(group * QROWS, (group + 1) * QROWS)
                base = where_ref[half * NEAR + group] * PAIR
                for block in range(blocks):
                    lane = half * blocks + block
                    at = pl.ds(pl.multiple_of(base + block * BLOCK, BLOCK), BLOCK)
                    value = codes[here, block * BLOCK : (block + 1) * BLOCK] * scales[here, lane : lane + 1]
                    new_buf[rows, at] = w_ref[rows, at] - outer_rate * value
        copies.append(pltpu.make_async_copy(new_buf.at[rows], out_ref.at[rows], out_sem.at[by]))
        copies[-1].start()
    for copy in copies:
        copy.wait()


def final_step(where, weight, pieces):
    return pl.pallas_call(
        final_kernel,
        out_shape=jax.ShapeDtypeStruct((ROWS, WIDTH), F32),
        in_specs=[SM, VM] + [VM] * 8,
        out_specs=HB,
        scratch_shapes=[pltpu.VMEM((ROWS, WIDTH), F32), pltpu.SemaphoreType.DMA((4,))],
        compiler_params=params(16),
        name="final_step",
    )(where, weight, *pieces)


def shift(value, axis, by):
    size = lax.axis_size(axis)
    return lax.ppermute(value, axis, [(i, (i + by) % size) for i in range(size)])


def shifts(values, axis):
    return [shift(value, axis, by) for by, value in zip((1, 2, 3), values)]


def after(value, *others):
    return lax.optimization_barrier((value,) + others)[0]


def swap(own):
    return own, shift(own, "c", 1)


def window(weight, first_moment, second_moment, outer_momentum, act_table, token_ids, targets):
    y, zh, core = lax.axis_index("y"), lax.axis_index("zh"), lax.axis_index("c")
    x, zl = lax.axis_index("x"), lax.axis_index("zl")
    step_y = jnp.array([0, 0, -1, 1, 2, -1, 1, 2, 0, 0, 0], jnp.int32)
    step_z = jnp.array([0, 1, 0, 0, 0, 1, 1, 1, 0, 0, 0], jnp.int32)
    chip = ((y + step_y + 4) % 4) * 2 + (zh + step_z) % 2
    entry = jnp.arange(11)
    where = jnp.where(entry == 8, core, jnp.where(entry == 9, x, jnp.where(entry == 10, zl, chip)))
    where = where.astype(jnp.int32)

    table_t = act_table.T
    ids = token_ids[0]
    wanted = jnp.transpose(targets[0], (0, 2, 1))
    moments = (first_moment[0], second_moment[0])
    own1, own2 = [gather(ids[step : step + 1], table_t) for step in range(STEPS)]

    far1 = shift(own1, "zh", 1)
    left1, right1 = shift(own1, "y", 1), shift(own1, "y", -1)
    opposite1 = shift(left1, "y", 1)
    right2 = shift(after(own2, right1), "y", -1)
    far2 = shift(after(own2, far1), "zh", 1)
    far_left1 = shift(after(far1, opposite1), "y", 1)
    far_right1 = shift(after(far1, right2), "y", -1)
    left2 = shift(after(own2, opposite1), "y", 1)
    near1 = swap(pack(own1, far1, left1, right1))
    far_opposite1 = shift(far_right1, "y", -1)
    opposite2 = shift(left2, "y", 1)
    rest1 = swap(pack(opposite1, far_left1, far_right1, far_opposite1))
    total = forward(0, where, (), weight, [near1])

    far_left2, far_right2 = shift(far2, "y", 1), shift(far2, "y", -1)
    near2 = swap(pack(own2, far2, left2, right2))
    signal = forward(1, where, (total, wanted[0]), weight, [rest1])
    current0, *state0 = first_back(0, where, signal, weight, *moments, [near1])
    far_opposite2 = shift(after(far_right2, current0), "y", -1)
    current1, *state1 = first_back(1, where, signal, weight, *moments, [rest1])
    rest2 = swap(pack(opposite2, far_left2, far_right2))
    total = forward(0, where, (), current0, [near2])
    last2 = swap(after(far_opposite2, total, current1))
    signal = forward(1, where, (total, wanted[1]), current1, [rest2, last2])

    payloads = []
    for half, (state, xs) in enumerate(((state0, [near2]), (state1, [rest2, last2]))):
        sends = second_back(half, where, signal, state, xs)
        payloads.append([sends[0]] + shifts(sends[1:], "x"))
    kept, pieces = (), []
    for half in range(2):
        sends = partial_sums(where, payloads[half])
        sums = [sends[0]] + shifts(sends[1:], "zl")
        *kept, codes = outer_step(half, where, outer_momentum, sums, *kept)
        line = pack(codes, *shifts([codes] * 3, "zl"))
        pieces += [line] + shifts([line] * 3, "x")
    new_weight = final_step(where, weight, pieces)
    return (new_weight, kept[0])


def solution(mesh):
    inner = Mesh(mesh.devices.reshape(4, 2, 2, 4, 4), ("y", "zh", "c", "x", "zl"))
    mp, replica = ("y", "zh", "c"), ("x", "zl")
    in_specs = (
        P(mp, None),
        P(replica, mp, None),
        P(replica, mp, None),
        P(mp + replica, None),
        P(None, mp),
        P(replica, None, None),
        P(replica, None, None, mp),
    )
    out_specs = (P(mp, None), P(mp + replica, None))
    return jax.shard_map(window, mesh=inner, in_specs=in_specs, out_specs=out_specs, check_vma=False)
```

```python
import functools

import jax
import jax.numpy as jnp
from jax import lax
from jax.experimental import pallas as pl
from jax.experimental.pallas import tpu as pltpu
from jax.sharding import Mesh, PartitionSpec as P


STEPS = 2
BLOCK = 128
PRIOR_STEPS = 3

beta_first = 0.9
beta_second = 0.95
adam_epsilon = 1e-08
inner_rate = 0.1
weight_decay = 0.1
outer_mu = 0.9
outer_rate = 0.7
scale_epsilon = 1e-06

ROWS = 160
WIDTH = 5120
TOK = 512
CHUNK = 320
PAIR = 2 * CHUNK
SLOTS = 8
NEAR = 4
TILE = 32
COLS = 256
HALF = WIDTH // 2
PAYLOAD = HALF + BLOCK
QROWS = ROWS // 4
OWN = ROWS // 16

F32 = jnp.float32
BF16 = jnp.bfloat16
FACTOR = WIDTH ** (-0.5)


HB = pl.BlockSpec(memory_space=pltpu.HBM)
VM = pl.BlockSpec(memory_space=pltpu.VMEM)
SM = pl.BlockSpec(memory_space=pltpu.SMEM)


def params(mib):
    return pltpu.CompilerParams(vmem_limit_bytes=mib << 20)


def gather_kernel(where_ref, ids_ref, table_ref, out_ref, total):
    step = 512
    total[...] = jnp.zeros_like(total)

    def body(block, carry):
        start = pl.multiple_of(block * step, step)
        row = lax.broadcasted_iota(jnp.int32, (step, TOK), 0) + start
        pick = jnp.where(row == ids_ref[...], 1.0, 0.0).astype(BF16)
        total[...] += jnp.dot(table_ref[:, pl.ds(start, step)], pick, preferred_element_type=F32)
        return carry

    lax.fori_loop(0, table_ref.shape[1] // step, body, 0)
    out_ref[...] = total[...].astype(BF16)


def gather(where, ids, table_t):
    return pl.pallas_call(
        gather_kernel,
        out_shape=jax.ShapeDtypeStruct((CHUNK, TOK), BF16),
        in_specs=[SM, VM, VM],
        out_specs=VM,
        scratch_shapes=[pltpu.VMEM((CHUNK, TOK), F32)],
        compiler_params=params(16),
        name="gather",
    )(where, ids, table_t)


def pack_kernel(*refs):
    out_ref = refs[-1]
    rows = refs[0].shape[0]
    for index, ref in enumerate(refs[:-1]):
        out_ref[index * rows : (index + 1) * rows, :] = ref[...]


def pack(*chunks):
    rows, width = chunks[0].shape
    return pl.pallas_call(
        pack_kernel,
        out_shape=jax.ShapeDtypeStruct((len(chunks) * rows, width), chunks[0].dtype),
        in_specs=[VM] * len(chunks),
        out_specs=VM,
        compiler_params=params(8),
        name="pack",
    )(*chunks)


def forward_kernel(half, counts, step, where_ref, extra_ref, w_ref, *refs):
    stacks = refs[: 2 * len(counts)]
    out_ref, x_ref, total = refs[2 * len(counts) : 2 * len(counts) + 3]
    core = where_ref[SLOTS]
    total[...] = jnp.zeros_like(total) if half == 0 else extra_ref[...]
    done = 0
    for group, count in enumerate(counts):

        def body(place, carry, group=group, done=done):
            slot = done + place
            rows = pl.ds(pl.multiple_of(place * CHUNK, CHUNK), CHUNK)
            base = slot * PAIR
            for index, at in enumerate((core, 1 - core)):
                to = pl.ds(pl.multiple_of(base + at * CHUNK, CHUNK), CHUNK)
                x_ref[to, :] = stacks[2 * group + index][rows, :]
            if w_ref.shape[1] == WIDTH:
                column = where_ref[half * NEAR + slot] * PAIR
            else:
                column = base
            weight = w_ref[:, pl.ds(pl.multiple_of(column, PAIR), PAIR)].astype(BF16)
            total[...] += jnp.dot(
                weight, x_ref[pl.ds(pl.multiple_of(base, PAIR), PAIR), :], preferred_element_type=F32
            )
            return carry

        lax.fori_loop(0, count, body, 0)
        done += count
    if half == 0:
        out_ref[...] = total[...]
    else:
        target_ref = refs[2 * len(counts) + 3]
        out_ref[...] = (total[...] * FACTOR - target_ref[step].astype(F32)).astype(BF16)


def forward_near_kernel(counts, step, where_ref, w_ref, *refs):
    forward_kernel(0, counts, step, where_ref, None, w_ref, *refs)


def forward_rest_kernel(counts, step, where_ref, total_ref, target_ref, w_ref, *refs):
    forward_kernel(1, counts, step, where_ref, total_ref, w_ref, *refs, target_ref)


def forward(half, step, where, extra, weight, xs):
    flat = [ref for pair in xs for ref in pair]
    counts = tuple(own.shape[0] // CHUNK for own, _ in xs)
    kernel = (forward_near_kernel, forward_rest_kernel)[half]
    return pl.pallas_call(
        functools.partial(kernel, counts, step),
        out_shape=(
            jax.ShapeDtypeStruct((ROWS, TOK), (F32, BF16)[half]),
            jax.ShapeDtypeStruct((HALF, TOK), BF16),
        ),
        in_specs=[SM] + [VM] * (len(extra) + 1 + len(flat)),
        out_specs=(VM, VM),
        scratch_shapes=[pltpu.VMEM((ROWS, TOK), F32)],
        compiler_params=params(24),
        cost_estimate=pl.CostEstimate(
            flops=ROWS * WIDTH * TOK, bytes_accessed=5 << 20, transcendentals=0
        ),
        name="forward",
    )(where, *extra, weight, *flat)


def corrections(step_count):
    return 1.0 / (1.0 - beta_first**step_count), 1.0 / (1.0 - beta_second**step_count)


def first_adam(gradient, one, two, weight):
    first, second = corrections(PRIOR_STEPS + 1)
    one = beta_first * one + (1.0 - beta_first) * gradient
    two = beta_second * two + (1.0 - beta_second) * gradient * gradient
    update = (one * first) / (jnp.sqrt(two * second) + adam_epsilon)
    current = weight - inner_rate * (update + weight_decay * weight)
    first, second = corrections(PRIOR_STEPS + 2)
    kept = weight - (1.0 - inner_rate * weight_decay) * current
    return current, one * (beta_first * first), two * (beta_second * second), kept


def second_adam(gradient, one, two, kept):
    first, second = corrections(PRIOR_STEPS + 2)
    one = one + ((1.0 - beta_first) * first) * gradient
    two = two + ((1.0 - beta_second) * second) * (gradient * gradient)
    return kept + inner_rate * (one / (jnp.sqrt(two) + adam_epsilon))


def backward(signal_ref, x_ref, grad, consume):
    steps = HALF // COLS

    def product(step, place):
        rows = pl.ds(pl.multiple_of(step * COLS, COLS), COLS)
        grad[place] = lax.dot_general(
            signal_ref[...], x_ref[rows, :], (((1,), (1,)), ((), ())), preferred_element_type=F32
        ) * (FACTOR / TOK)

    product(0, 0)

    def body(step, carry):
        product(jnp.minimum(step + 1, steps - 1), (step + 1) % 2)
        for part in range(COLS // BLOCK):
            consume(step * (COLS // BLOCK) + part, part, step % 2)
        return carry

    lax.fori_loop(0, steps, body, 0)


def first_back_kernel(half, where_ref, signal_ref, x_ref, w_ref, one_ref, two_ref, *refs):
    cur_ref, *outs, grad = refs
    per = PAIR // BLOCK

    def consume(block, part, place):
        column = where_ref[half * NEAR + block // per] * PAIR + (block % per) * BLOCK
        source = pl.ds(pl.multiple_of(column, BLOCK), BLOCK)
        to = pl.ds(pl.multiple_of(block * BLOCK, BLOCK), BLOCK)
        for row in range(0, ROWS, TILE):
            rows = slice(row, row + TILE)
            current, *values = first_adam(
                grad[place, rows, part * BLOCK : (part + 1) * BLOCK],
                one_ref[rows, source].astype(F32),
                two_ref[rows, source].astype(F32),
                w_ref[rows, source],
            )
            cur_ref[rows, to] = current.astype(BF16)
            for out, value in zip(outs, values):
                out[rows, to] = value

    backward(signal_ref, x_ref, grad, consume)


def first_back(half, where, signal, x, weight, one, two):
    state = jax.ShapeDtypeStruct((ROWS, HALF), F32)
    return pl.pallas_call(
        functools.partial(first_back_kernel, half),
        out_shape=(jax.ShapeDtypeStruct((ROWS, HALF), BF16), state, state, state),
        in_specs=[SM] + [VM] * 5,
        out_specs=(VM,) * 4,
        scratch_shapes=[pltpu.VMEM((2, ROWS, COLS), F32)],
        compiler_params=params(24),
        cost_estimate=pl.CostEstimate(
            flops=ROWS * WIDTH * TOK, bytes_accessed=14 << 20, transcendentals=0
        ),
        name="first_back",
    )(where, signal, x, weight, one, two)


def second_back_kernel(where_ref, signal_ref, x_ref, one_ref, two_ref, kept_ref, *refs):
    outs = refs[:4]
    grad, scale_buf, code_buf = refs[4:]
    scale_buf[...] = jnp.zeros_like(scale_buf)
    lane = lax.broadcasted_iota(jnp.int32, (QROWS, BLOCK), 1)

    def consume(block, part, place):
        here = pl.ds(pl.multiple_of(block * BLOCK, BLOCK), BLOCK)
        for quarter in range(4):
            rows = slice(quarter * QROWS, (quarter + 1) * QROWS)
            delta = second_adam(
                grad[place, rows, part * BLOCK : (part + 1) * BLOCK],
                one_ref[rows, here],
                two_ref[rows, here],
                kept_ref[rows, here],
            )
            top = jnp.max(jnp.abs(delta), axis=1, keepdims=True) + scale_epsilon
            scale = jnp.broadcast_to(top.astype(BF16).astype(F32), (QROWS, BLOCK))
            code_buf[quarter, :, here] = (delta / scale).astype(BF16)
            scale_buf[quarter] = jnp.where(lane == block, scale, scale_buf[quarter])

    backward(signal_ref, x_ref, grad, consume)
    code_buf[:, :, HALF:] = scale_buf[...].astype(BF16)
    for by in range(4):
        outs[by][...] = code_buf[(where_ref[SLOTS + 1] + by) % 4]


def second_back(where, signal, x, state):
    return pl.pallas_call(
        second_back_kernel,
        out_shape=(jax.ShapeDtypeStruct((QROWS, PAYLOAD), BF16),) * 4,
        in_specs=[SM] + [VM] * 5,
        out_specs=(VM,) * 4,
        scratch_shapes=[
            pltpu.VMEM((2, ROWS, COLS), F32),
            pltpu.VMEM((4, QROWS, BLOCK), F32),
            pltpu.VMEM((4, QROWS, PAYLOAD), BF16),
        ],
        compiler_params=params(24),
        cost_estimate=pl.CostEstimate(
            flops=ROWS * WIDTH * TOK, bytes_accessed=14 << 20, transcendentals=0
        ),
        name="second_back",
    )(where, signal, x, *state)


def partial_kernel(where_ref, *refs):
    gots, outs = refs[:4], refs[4:8]
    part, piece = refs[8:]
    scales = [got[:, HALF:].astype(F32) for got in gots]
    for block in range(HALF // BLOCK):
        here = slice(block * BLOCK, (block + 1) * BLOCK)
        total = jnp.zeros((QROWS, BLOCK), F32)
        for got, scale in zip(gots, scales):
            total = total + got[:, here].astype(F32) * scale[:, block : block + 1]
        part[:, here] = total
    for line in range(4):
        for group in range(NEAR):
            piece[line, group * OWN : (group + 1) * OWN, :] = part[
                line * OWN : (line + 1) * OWN, group * PAIR : (group + 1) * PAIR
            ]
    for by in range(4):
        outs[by][...] = piece[(where_ref[SLOTS + 2] + by) % 4].astype(BF16)


def partial_sums(where, gots):
    return pl.pallas_call(
        partial_kernel,
        out_shape=(jax.ShapeDtypeStruct((QROWS, PAIR), BF16),) * 4,
        in_specs=[SM] + [VM] * 4,
        out_specs=(VM,) * 4,
        scratch_shapes=[
            pltpu.VMEM((QROWS, HALF), F32),
            pltpu.VMEM((4, QROWS, PAIR), F32),
        ],
        compiler_params=params(8),
        name="partial_sums",
    )(where, *gots)


def outer_kernel(half, where_ref, outer_ref, *refs):
    gots, refs = refs[:4], refs[4:]
    if half:
        before_ref, scales_ref, momentum_ref, code_ref, held, sent = refs
        scales = scales_ref[...]
    else:
        sent, scales_ref, code_ref, held = refs
        scales = jnp.zeros(scales_ref.shape, F32)

    def column(slot):
        return pl.ds(pl.multiple_of(where_ref[slot] * PAIR, PAIR), PAIR)

    for group in range(NEAR):
        held[group * OWN : (group + 1) * OWN, :] = outer_ref[:, column(half * NEAR + group)]
    lane = lax.broadcasted_iota(jnp.int32, (QROWS, BLOCK), 1)
    blocks = PAIR // BLOCK
    for block in range(blocks):
        here = slice(block * BLOCK, (block + 1) * BLOCK)
        total = gots[0][:, here].astype(F32)
        for got in gots[1:]:
            total = total + got[:, here].astype(F32)
        average = total * (1.0 / 16)
        momentum = outer_mu * held[:, here] + average
        sent[:, here] = momentum
        update = average + outer_mu * momentum
        top = jnp.max(jnp.abs(update), axis=1, keepdims=True) + scale_epsilon
        scale = jnp.broadcast_to(top.astype(BF16).astype(F32), (QROWS, BLOCK))
        code_ref[:, here] = (update / scale).astype(BF16)
        scales = jnp.where(lane == half * blocks + block, scale, scales)
    if not half:
        scales_ref[...] = scales
        return
    code_ref[:, PAIR:] = scales.astype(BF16)
    for group in range(NEAR):
        rows = slice(group * OWN, (group + 1) * OWN)
        momentum_ref[:, column(group)] = before_ref[rows, :]
        momentum_ref[:, column(NEAR + group)] = sent[rows, :]


def outer_step(half, where, outer_momentum, gots, *before):
    scratch = [pltpu.VMEM((QROWS, PAIR), F32)]
    if half:
        out_shape = (
            jax.ShapeDtypeStruct((OWN, WIDTH), F32),
            jax.ShapeDtypeStruct((QROWS, PAIR + BLOCK), BF16),
        )
        scratch = scratch * 2
    else:
        out_shape = (
            jax.ShapeDtypeStruct((QROWS, PAIR), F32),
            jax.ShapeDtypeStruct((QROWS, BLOCK), F32),
            jax.ShapeDtypeStruct((QROWS, PAIR), BF16),
        )
    return pl.pallas_call(
        functools.partial(outer_kernel, half),
        out_shape=out_shape,
        in_specs=[SM] + [VM] * (5 + len(before)),
        out_specs=tuple(VM for _ in out_shape),
        scratch_shapes=scratch,
        compiler_params=params(8),
        name="outer_step",
    )(where, outer_momentum, *gots, *before)


def final_kernel(where_ref, w_ref, *refs):
    pieces = refs[:8]
    out_ref = refs[8]
    new_buf, code_buf, scale_buf, out_sem = refs[9:]
    x, zl = where_ref[SLOTS + 1], where_ref[SLOTS + 2]
    to = lax.broadcasted_iota(jnp.int32, (ROWS, ROWS), 0)
    source = lax.broadcasted_iota(jnp.int32, (ROWS, ROWS), 1)
    group, line, row = to // QROWS, (to % QROWS) // OWN, to % OWN
    wanted = ((zl - line + 4) % 4) * QROWS + group * OWN + row
    order = jnp.where(source == wanted, 1.0, 0.0).astype(BF16)
    blocks = PAIR // BLOCK

    def ordered(value):
        return jnp.dot(order, value, preferred_element_type=F32)

    copies = []
    for by in range(4):
        rows = pl.ds(pl.multiple_of(((x - by + 4) % 4) * QROWS, 8), QROWS)
        scale_buf[...] = ordered(pieces[4 + by][:, PAIR:])
        for half in range(2):
            code_buf[half] = ordered(pieces[half * 4 + by][:, :PAIR])

        def slots(group, carry, rows=rows):
            here = pl.ds(pl.multiple_of(group * QROWS, 8), QROWS)
            scales = scale_buf[here, :]
            for half in range(2):
                base = where_ref[half * NEAR + group] * PAIR
                for block in range(blocks):
                    lane = half * blocks + block
                    at = pl.ds(pl.multiple_of(base + block * BLOCK, BLOCK), BLOCK)
                    codes = code_buf[half, here, block * BLOCK : (block + 1) * BLOCK]
                    new_buf[rows, at] = w_ref[rows, at] - outer_rate * (codes * scales[:, lane : lane + 1])
            return carry

        lax.fori_loop(0, NEAR, slots, 0)
        copies.append(pltpu.make_async_copy(new_buf.at[rows], out_ref.at[rows], out_sem.at[by]))
        copies[-1].start()
    for copy in copies:
        copy.wait()


def final_step(where, weight, pieces):
    return pl.pallas_call(
        final_kernel,
        out_shape=jax.ShapeDtypeStruct((ROWS, WIDTH), F32),
        in_specs=[SM, VM] + [VM] * 8,
        out_specs=HB,
        scratch_shapes=[
            pltpu.VMEM((ROWS, WIDTH), F32),
            pltpu.VMEM((2, ROWS, PAIR), F32),
            pltpu.VMEM((ROWS, BLOCK), F32),
            pltpu.SemaphoreType.DMA((4,)),
        ],
        compiler_params=params(16),
        name="final_step",
    )(where, weight, *pieces)


def shift(value, axis, by):
    size = lax.axis_size(axis)
    return lax.ppermute(value, axis, [(i, (i + by) % size) for i in range(size)])


def shifts(values, axis):
    return [shift(value, axis, by) for by, value in zip((1, 2, 3), values)]


def after(value, *others):
    return lax.optimization_barrier((value,) + others)[0]


def swap(own):
    return own, shift(own, "c", 1)


def window(weight, first_moment, second_moment, outer_momentum, act_table, token_ids, targets):
    y, zh, core = lax.axis_index("y"), lax.axis_index("zh"), lax.axis_index("c")
    x, zl = lax.axis_index("x"), lax.axis_index("zl")
    step_y = jnp.array([0, 0, -1, 1, 2, -1, 1, 2, 0, 0, 0], jnp.int32)
    step_z = jnp.array([0, 1, 0, 0, 0, 1, 1, 1, 0, 0, 0], jnp.int32)
    chip = ((y + step_y + 4) % 4) * 2 + (zh + step_z) % 2
    entry = jnp.arange(11)
    where = jnp.where(entry == 8, core, jnp.where(entry == 9, x, jnp.where(entry == 10, zl, chip)))
    where = where.astype(jnp.int32)

    table_t = act_table.T
    ids = token_ids[0]
    wanted = jnp.transpose(targets[0], (0, 2, 1))
    moments = (first_moment[0], second_moment[0])
    own1, own2 = [gather(where, ids[step : step + 1], table_t) for step in range(STEPS)]

    far1 = shift(own1, "zh", 1)
    left1, right1 = shift(own1, "y", 1), shift(own1, "y", -1)
    opposite1 = shift(left1, "y", 1)
    right2 = shift(after(own2, right1), "y", -1)
    far2 = shift(after(own2, far1), "zh", 1)
    far_left1 = shift(after(far1, opposite1), "y", 1)
    far_right1 = shift(after(far1, right2), "y", -1)
    left2 = shift(after(own2, opposite1), "y", 1)
    near1 = swap(pack(own1, far1, left1, right1))
    far_opposite1 = shift(far_right1, "y", -1)
    opposite2 = shift(left2, "y", 1)
    rest1 = swap(pack(opposite1, far_left1, far_right1, far_opposite1))
    total, near1 = forward(0, 0, where, (), weight, [near1])

    far_left2, far_right2 = shift(far2, "y", 1), shift(far2, "y", -1)
    near2 = swap(pack(own2, far2, left2, right2))
    signal, rest1 = forward(1, 0, where, (total, wanted), weight, [rest1])
    current0, *state0 = first_back(0, where, signal, near1, weight, *moments)
    far_opposite2 = shift(after(far_right2, current0), "y", -1)
    current1, *state1 = first_back(1, where, signal, rest1, weight, *moments)
    rest2 = swap(pack(opposite2, far_left2, far_right2))
    total, near2 = forward(0, 1, where, (), current0, [near2])
    last2 = swap(after(far_opposite2, total, current1))
    signal, rest2 = forward(1, 1, where, (total, wanted), current1, [rest2, last2])

    payloads = []
    for state, x_half in ((state0, near2), (state1, rest2)):
        sends = second_back(where, signal, x_half, state)
        payloads.append([sends[0]] + shifts(sends[1:], "x"))
    kept, pieces = (), []
    for half in range(2):
        sends = partial_sums(where, payloads[half])
        sums = [sends[0]] + shifts(sends[1:], "zl")
        *kept, codes = outer_step(half, where, outer_momentum, sums, *kept)
        line = pack(codes, *shifts([codes] * 3, "zl"))
        pieces += [line] + shifts([line] * 3, "x")
    new_weight = final_step(where, weight, pieces)
    return (new_weight, kept[0])


def solution(mesh):
    inner = Mesh(mesh.devices.reshape(4, 2, 2, 4, 4), ("y", "zh", "c", "x", "zl"))
    mp, replica = ("y", "zh", "c"), ("x", "zl")
    in_specs = (
        P(mp, None),
        P(replica, mp, None),
        P(replica, mp, None),
        P(mp + replica, None),
        P(None, mp),
        P(replica, None, None),
        P(replica, None, None, mp),
    )
    out_specs = (P(mp, None), P(mp + replica, None))
    return jax.shard_map(window, mesh=inner, in_specs=in_specs, out_specs=out_specs, check_vma=False)
```

```python
import functools

import jax
import jax.numpy as jnp
from jax import lax
from jax.experimental import pallas as pl
from jax.experimental.pallas import tpu as pltpu
from jax.sharding import Mesh, PartitionSpec as P


STEPS = 2
BLOCK = 128
PRIOR_STEPS = 3

beta_first = 0.9
beta_second = 0.95
adam_epsilon = 1e-08
inner_rate = 0.1
weight_decay = 0.1
outer_mu = 0.9
outer_rate = 0.7
scale_epsilon = 1e-06

ROWS = 160
WIDTH = 5120
TOK = 512
CHUNK = 320
PAIR = 2 * CHUNK
SLOTS = 8
NEAR = 4
TILE = 32
COLS = 256
HALF = WIDTH // 2
PAYLOAD = HALF + BLOCK
QROWS = ROWS // 4
OWN = ROWS // 16

F32 = jnp.float32
BF16 = jnp.bfloat16
FACTOR = WIDTH ** (-0.5)
SCALE = FACTOR / TOK


HB = pl.BlockSpec(memory_space=pltpu.HBM)
VM = pl.BlockSpec(memory_space=pltpu.VMEM)
SM = pl.BlockSpec(memory_space=pltpu.SMEM)


def params(mib):
    return pltpu.CompilerParams(vmem_limit_bytes=mib << 20)


def gather_kernel(where_ref, ids_ref, table_ref, out_ref, total):
    step = 512
    total[...] = jnp.zeros_like(total)

    def body(block, carry):
        start = pl.multiple_of(block * step, step)
        row = lax.broadcasted_iota(jnp.int32, (step, TOK), 0) + start
        pick = jnp.where(row == ids_ref[...], 1.0, 0.0).astype(BF16)
        total[...] += jnp.dot(table_ref[:, pl.ds(start, step)], pick, preferred_element_type=F32)
        return carry

    lax.fori_loop(0, table_ref.shape[1] // step, body, 0)
    out_ref[...] = total[...].astype(BF16)


def gather(where, ids, table_t):
    return pl.pallas_call(
        gather_kernel,
        out_shape=jax.ShapeDtypeStruct((CHUNK, TOK), BF16),
        in_specs=[SM, VM, VM],
        out_specs=VM,
        scratch_shapes=[pltpu.VMEM((CHUNK, TOK), F32)],
        compiler_params=params(16),
        name="gather",
    )(where, ids, table_t)


def pack_kernel(*refs):
    out_ref = refs[-1]
    rows = refs[0].shape[0]
    for index, ref in enumerate(refs[:-1]):
        out_ref[index * rows : (index + 1) * rows, :] = ref[...]


def pack(*chunks):
    rows, width = chunks[0].shape
    return pl.pallas_call(
        pack_kernel,
        out_shape=jax.ShapeDtypeStruct((len(chunks) * rows, width), chunks[0].dtype),
        in_specs=[VM] * len(chunks),
        out_specs=VM,
        compiler_params=params(8),
        name="pack",
    )(*chunks)


def forward_kernel(half, counts, step, where_ref, extra_ref, w_ref, *refs):
    stacks = refs[: 2 * len(counts)]
    out_ref, x_ref, total = refs[2 * len(counts) : 2 * len(counts) + 3]
    core = where_ref[SLOTS]
    total[...] = jnp.zeros_like(total) if half == 0 else extra_ref[...]
    done = 0
    for group, count in enumerate(counts):

        def body(place, carry, group=group, done=done):
            slot = done + place
            rows = pl.ds(pl.multiple_of(place * CHUNK, CHUNK), CHUNK)
            base = slot * PAIR
            for index, at in enumerate((core, 1 - core)):
                to = pl.ds(pl.multiple_of(base + at * CHUNK, CHUNK), CHUNK)
                x_ref[to, :] = stacks[2 * group + index][rows, :]
            if w_ref.shape[1] == WIDTH:
                column = where_ref[half * NEAR + slot] * PAIR
            else:
                column = base
            weight = w_ref[:, pl.ds(pl.multiple_of(column, PAIR), PAIR)].astype(BF16)
            total[...] += jnp.dot(
                weight, x_ref[pl.ds(pl.multiple_of(base, PAIR), PAIR), :], preferred_element_type=F32
            )
            return carry

        lax.fori_loop(0, count, body, 0)
        done += count
    if half == 0:
        out_ref[...] = total[...]
    else:
        target_ref = refs[2 * len(counts) + 3]
        out_ref[...] = (total[...] * FACTOR - target_ref[step].astype(F32)).astype(BF16)


def forward_near_kernel(counts, step, where_ref, w_ref, *refs):
    forward_kernel(0, counts, step, where_ref, None, w_ref, *refs)


def forward_rest_kernel(counts, step, where_ref, total_ref, target_ref, w_ref, *refs):
    forward_kernel(1, counts, step, where_ref, total_ref, w_ref, *refs, target_ref)


def forward(half, step, where, extra, weight, xs):
    flat = [ref for pair in xs for ref in pair]
    counts = tuple(own.shape[0] // CHUNK for own, _ in xs)
    kernel = (forward_near_kernel, forward_rest_kernel)[half]
    return pl.pallas_call(
        functools.partial(kernel, counts, step),
        out_shape=(
            jax.ShapeDtypeStruct((ROWS, TOK), (F32, BF16)[half]),
            jax.ShapeDtypeStruct((HALF, TOK), BF16),
        ),
        in_specs=[SM] + [VM] * (len(extra) + 1 + len(flat)),
        out_specs=(VM, VM),
        scratch_shapes=[pltpu.VMEM((ROWS, TOK), F32)],
        compiler_params=params(24),
        cost_estimate=pl.CostEstimate(
            flops=ROWS * WIDTH * TOK, bytes_accessed=5 << 20, transcendentals=0
        ),
        name="forward",
    )(where, *extra, weight, *flat)


def corrections(step_count):
    return 1.0 / (1.0 - beta_first**step_count), 1.0 / (1.0 - beta_second**step_count)


def first_adam(product, one, two, weight):
    first, second = corrections(PRIOR_STEPS + 1)
    one = beta_first * one + ((1.0 - beta_first) * SCALE) * product
    two = beta_second * two + ((1.0 - beta_second) * SCALE * SCALE) * (product * product)
    update = (one * first) / (jnp.sqrt(two * second) + adam_epsilon)
    current = (1.0 - inner_rate * weight_decay) * weight - inner_rate * update
    first, second = corrections(PRIOR_STEPS + 2)
    kept = weight - (1.0 - inner_rate * weight_decay) * current
    return current, one * (beta_first * first), two * (beta_second * second), kept


def second_adam(product, one, two, kept):
    first, second = corrections(PRIOR_STEPS + 2)
    one = one + ((1.0 - beta_first) * first * SCALE) * product
    two = two + ((1.0 - beta_second) * second * SCALE * SCALE) * (product * product)
    return kept + inner_rate * (one / (jnp.sqrt(two) + adam_epsilon))


def backward(signal_ref, x_ref, grad, consume):
    steps = HALF // COLS

    def product(step, place):
        rows = pl.ds(pl.multiple_of(step * COLS, COLS), COLS)
        grad[place] = lax.dot_general(
            signal_ref[...], x_ref[rows, :], (((1,), (1,)), ((), ())), preferred_element_type=F32
        )

    product(0, 0)

    def body(step, carry):
        product(jnp.minimum(step + 1, steps - 1), (step + 1) % 2)
        for part in range(COLS // BLOCK):
            consume(step * (COLS // BLOCK) + part, part, step % 2)
        return carry

    lax.fori_loop(0, steps, body, 0)


def first_back_kernel(half, where_ref, signal_ref, x_ref, w_ref, one_ref, two_ref, *refs):
    cur_ref, *outs, grad = refs
    per = PAIR // BLOCK

    def consume(block, part, place):
        column = where_ref[half * NEAR + block // per] * PAIR + (block % per) * BLOCK
        source = pl.ds(pl.multiple_of(column, BLOCK), BLOCK)
        to = pl.ds(pl.multiple_of(block * BLOCK, BLOCK), BLOCK)
        for row in range(0, ROWS, TILE):
            rows = slice(row, row + TILE)
            current, *values = first_adam(
                grad[place, rows, part * BLOCK : (part + 1) * BLOCK],
                one_ref[rows, source].astype(F32),
                two_ref[rows, source].astype(F32),
                w_ref[rows, source],
            )
            cur_ref[rows, to] = current.astype(BF16)
            for out, value in zip(outs, values):
                out[rows, to] = value

    backward(signal_ref, x_ref, grad, consume)


def first_back(half, where, signal, x, weight, one, two):
    state = jax.ShapeDtypeStruct((ROWS, HALF), F32)
    return pl.pallas_call(
        functools.partial(first_back_kernel, half),
        out_shape=(jax.ShapeDtypeStruct((ROWS, HALF), BF16), state, state, state),
        in_specs=[SM] + [VM] * 5,
        out_specs=(VM,) * 4,
        scratch_shapes=[pltpu.VMEM((2, ROWS, COLS), F32)],
        compiler_params=params(24),
        cost_estimate=pl.CostEstimate(
            flops=ROWS * WIDTH * TOK, bytes_accessed=14 << 20, transcendentals=0
        ),
        name="first_back",
    )(where, signal, x, weight, one, two)


def second_back_kernel(where_ref, signal_ref, x_ref, one_ref, two_ref, kept_ref, *refs):
    outs = refs[:4]
    grad, scale_buf, code_buf = refs[4:]
    scale_buf[...] = jnp.zeros_like(scale_buf)
    lane = lax.broadcasted_iota(jnp.int32, (QROWS, BLOCK), 1)

    def consume(block, part, place):
        here = pl.ds(pl.multiple_of(block * BLOCK, BLOCK), BLOCK)
        for quarter in range(4):
            rows = slice(quarter * QROWS, (quarter + 1) * QROWS)
            delta = second_adam(
                grad[place, rows, part * BLOCK : (part + 1) * BLOCK],
                one_ref[rows, here],
                two_ref[rows, here],
                kept_ref[rows, here],
            )
            top = jnp.max(jnp.abs(delta), axis=1, keepdims=True) + scale_epsilon
            scale = jnp.broadcast_to(top.astype(BF16).astype(F32), (QROWS, BLOCK))
            code_buf[quarter, :, here] = (delta / scale).astype(BF16)
            scale_buf[quarter] = jnp.where(lane == block, scale, scale_buf[quarter])

    backward(signal_ref, x_ref, grad, consume)
    code_buf[:, :, HALF:] = scale_buf[...].astype(BF16)
    for by in range(4):
        outs[by][...] = code_buf[(where_ref[SLOTS + 1] + by) % 4]


def second_back(where, signal, x, state):
    return pl.pallas_call(
        second_back_kernel,
        out_shape=(jax.ShapeDtypeStruct((QROWS, PAYLOAD), BF16),) * 4,
        in_specs=[SM] + [VM] * 5,
        out_specs=(VM,) * 4,
        scratch_shapes=[
            pltpu.VMEM((2, ROWS, COLS), F32),
            pltpu.VMEM((4, QROWS, BLOCK), F32),
            pltpu.VMEM((4, QROWS, PAYLOAD), BF16),
        ],
        compiler_params=params(24),
        cost_estimate=pl.CostEstimate(
            flops=ROWS * WIDTH * TOK, bytes_accessed=14 << 20, transcendentals=0
        ),
        name="second_back",
    )(where, signal, x, *state)


def partial_kernel(where_ref, *refs):
    gots, outs = refs[:4], refs[4:8]
    part, piece = refs[8:]
    scales = [got[:, HALF:].astype(F32) for got in gots]
    for block in range(HALF // BLOCK):
        here = slice(block * BLOCK, (block + 1) * BLOCK)
        total = jnp.zeros((QROWS, BLOCK), F32)
        for got, scale in zip(gots, scales):
            total = total + got[:, here].astype(F32) * scale[:, block : block + 1]
        part[:, here] = total
    for line in range(4):
        for group in range(NEAR):
            piece[line, group * OWN : (group + 1) * OWN, :] = part[
                line * OWN : (line + 1) * OWN, group * PAIR : (group + 1) * PAIR
            ]
    for by in range(4):
        outs[by][...] = piece[(where_ref[SLOTS + 2] + by) % 4].astype(BF16)


def partial_sums(where, gots):
    return pl.pallas_call(
        partial_kernel,
        out_shape=(jax.ShapeDtypeStruct((QROWS, PAIR), BF16),) * 4,
        in_specs=[SM] + [VM] * 4,
        out_specs=(VM,) * 4,
        scratch_shapes=[
            pltpu.VMEM((QROWS, HALF), F32),
            pltpu.VMEM((4, QROWS, PAIR), F32),
        ],
        compiler_params=params(8),
        name="partial_sums",
    )(where, *gots)


def outer_kernel(half, where_ref, outer_ref, *refs):
    gots, refs = refs[:4], refs[4:]
    if half:
        before_ref, momentum_ref, code_ref, held, sent = refs
    else:
        sent, code_ref, held = refs

    def column(slot):
        return pl.ds(pl.multiple_of(where_ref[slot] * PAIR, PAIR), PAIR)

    for group in range(NEAR):
        held[group * OWN : (group + 1) * OWN, :] = outer_ref[:, column(half * NEAR + group)]
    lane = lax.broadcasted_iota(jnp.int32, (QROWS, BLOCK), 1)
    scales = jnp.zeros((QROWS, BLOCK), F32)
    for block in range(PAIR // BLOCK):
        here = slice(block * BLOCK, (block + 1) * BLOCK)
        total = gots[0][:, here].astype(F32)
        for got in gots[1:]:
            total = total + got[:, here].astype(F32)
        average = total * (1.0 / 16)
        momentum = outer_mu * held[:, here] + average
        sent[:, here] = momentum
        update = average + outer_mu * momentum
        top = jnp.max(jnp.abs(update), axis=1, keepdims=True) + scale_epsilon
        scale = jnp.broadcast_to(top.astype(BF16).astype(F32), (QROWS, BLOCK))
        code_ref[:, here] = (update / scale).astype(BF16)
        scales = jnp.where(lane == block, scale, scales)
    code_ref[:, PAIR:] = scales.astype(BF16)
    if half:
        for group in range(NEAR):
            rows = slice(group * OWN, (group + 1) * OWN)
            momentum_ref[:, column(group)] = before_ref[rows, :]
            momentum_ref[:, column(NEAR + group)] = sent[rows, :]


def outer_step(half, where, outer_momentum, gots, *before):
    momentum = ((QROWS, PAIR), (OWN, WIDTH))[half]
    return pl.pallas_call(
        functools.partial(outer_kernel, half),
        out_shape=(
            jax.ShapeDtypeStruct(momentum, F32),
            jax.ShapeDtypeStruct((QROWS, PAIR + BLOCK), BF16),
        ),
        in_specs=[SM] + [VM] * (5 + len(before)),
        out_specs=(VM, VM),
        scratch_shapes=[pltpu.VMEM((QROWS, PAIR), F32)] * (1 + half),
        compiler_params=params(8),
        name="outer_step",
    )(where, outer_momentum, *gots, *before)


def final_kernel(half, where_ref, w_ref, *refs):
    pieces = refs[:4]
    out_ref, new_buf, code_buf, out_sem = refs[4 + half :]
    x, zl = where_ref[SLOTS + 1], where_ref[SLOTS + 2]
    to = lax.broadcasted_iota(jnp.int32, (ROWS, ROWS), 0)
    source = lax.broadcasted_iota(jnp.int32, (ROWS, ROWS), 1)
    group, line, row = to // QROWS, (to % QROWS) // OWN, to % OWN
    wanted = ((zl - line + 4) % 4) * QROWS + group * OWN + row
    order = jnp.where(source == wanted, 1.0, 0.0).astype(BF16)

    copies = []
    for by in range(4):
        rows = pl.ds(pl.multiple_of(((x - by + 4) % 4) * QROWS, 8), QROWS)
        code_buf[...] = jnp.dot(order, pieces[by][...], preferred_element_type=F32)

        def slots(group, carry, rows=rows):
            here = pl.ds(pl.multiple_of(group * QROWS, 8), QROWS)
            scales = code_buf[here, PAIR:]
            base = where_ref[half * NEAR + group] * PAIR
            for block in range(PAIR // BLOCK):
                at = pl.ds(pl.multiple_of(base + block * BLOCK, BLOCK), BLOCK)
                value = code_buf[here, block * BLOCK : (block + 1) * BLOCK] * scales[:, block : block + 1]
                into = pl.ds(pl.multiple_of(group * PAIR + block * BLOCK, BLOCK), BLOCK)
                new_buf[rows, into] = w_ref[rows, at] - outer_rate * value
            return carry

        lax.fori_loop(0, NEAR, slots, 0)
        for group in range(NEAR):
            there = pl.ds(pl.multiple_of(where_ref[half * NEAR + group] * PAIR, PAIR), PAIR)
            copies.append(
                pltpu.make_async_copy(
                    new_buf.at[rows, pl.ds(group * PAIR, PAIR)], out_ref.at[rows, there], out_sem.at[by, group]
                )
            )
            copies[-1].start()
    for copy in copies:
        copy.wait()


def final_step(half, where, weight, pieces, *before):
    return pl.pallas_call(
        functools.partial(final_kernel, half),
        out_shape=jax.ShapeDtypeStruct((ROWS, WIDTH), F32),
        in_specs=[SM, VM] + [VM] * 4 + [HB] * len(before),
        out_specs=HB,
        input_output_aliases={6: 0} if half else {},
        scratch_shapes=[
            pltpu.VMEM((ROWS, HALF), F32),
            pltpu.VMEM((ROWS, PAIR + BLOCK), F32),
            pltpu.SemaphoreType.DMA((4, NEAR)),
        ],
        compiler_params=params(16),
        name="final_step",
    )(where, weight, *pieces, *before)


def shift(value, axis, by):
    size = lax.axis_size(axis)
    return lax.ppermute(value, axis, [(i, (i + by) % size) for i in range(size)])


def shifts(values, axis):
    return [shift(value, axis, by) for by, value in zip((1, 2, 3), values)]


def after(value, *others):
    return lax.optimization_barrier((value,) + others)[0]


def swap(own):
    return own, shift(own, "c", 1)


def window(weight, first_moment, second_moment, outer_momentum, act_table, token_ids, targets):
    y, zh, core = lax.axis_index("y"), lax.axis_index("zh"), lax.axis_index("c")
    x, zl = lax.axis_index("x"), lax.axis_index("zl")
    step_y = jnp.array([0, 0, -1, 1, 2, -1, 1, 2, 0, 0, 0], jnp.int32)
    step_z = jnp.array([0, 1, 0, 0, 0, 1, 1, 1, 0, 0, 0], jnp.int32)
    chip = ((y + step_y + 4) % 4) * 2 + (zh + step_z) % 2
    entry = jnp.arange(11)
    where = jnp.where(entry == 8, core, jnp.where(entry == 9, x, jnp.where(entry == 10, zl, chip)))
    where = where.astype(jnp.int32)

    table_t = act_table.T
    ids = token_ids[0]
    wanted = jnp.transpose(targets[0], (0, 2, 1))
    moments = (first_moment[0], second_moment[0])
    own1, own2 = [gather(where, ids[step : step + 1], table_t) for step in range(STEPS)]

    far1 = shift(own1, "zh", 1)
    left1, right1 = shift(own1, "y", 1), shift(own1, "y", -1)
    left2, right2 = shift(own2, "y", 1), shift(own2, "y", -1)
    opposite1, opposite2 = shift(left1, "y", 1), shift(right2, "y", -1)
    far2 = shift(own2, "zh", 1)
    far_left1, far_right1 = shift(far1, "y", 1), shift(far1, "y", -1)
    near1 = swap(pack(own1, far1, left1, right1))
    far_opposite1 = shift(far_right1, "y", -1)
    far_left2 = shift(far2, "y", 1)
    rest1 = swap(pack(opposite1, far_left1, far_right1, far_opposite1))
    total, near1 = forward(0, 0, where, (), weight, [near1])
    far_right2 = shift(after(far2, far_opposite1), "y", -1)
    near2 = swap(pack(own2, far2, left2, right2))
    signal, rest1 = forward(1, 0, where, (total, wanted), weight, [rest1])
    far_opposite2 = shift(far_left2, "y", 1)
    current0, *state0 = first_back(0, where, signal, near1, weight, *moments)
    rest2 = swap(pack(opposite2, far_left2, far_right2))
    current1, *state1 = first_back(1, where, signal, rest1, weight, *moments)
    last2 = swap(far_opposite2)
    total, near2 = forward(0, 1, where, (), current0, [near2])
    signal, rest2 = forward(1, 1, where, (total, wanted), current1, [rest2, last2])

    payloads = []
    for state, x_half in ((state0, near2), (state1, rest2)):
        sends = second_back(where, signal, x_half, state)
        payloads.append([sends[0]] + shifts(sends[1:], "x"))
    momentum, pieces = (), []
    for half in range(2):
        sends = partial_sums(where, payloads[half])
        sums = [sends[0]] + shifts(sends[1:], "zl")
        *momentum, codes = outer_step(half, where, outer_momentum, sums, *momentum)
        line = pack(codes, *shifts([codes] * 3, "zl"))
        left, right = shift(line, "x", 1), shift(line, "x", 3)
        opposite = shift((left, right)[half], "x", (1, 3)[half])
        pieces.append([line, left, opposite, right])
    new_weight = final_step(0, where, weight, pieces[0])
    new_weight = final_step(1, where, weight, pieces[1], new_weight)
    return (new_weight, momentum[0])


def solution(mesh):
    inner = Mesh(mesh.devices.reshape(4, 2, 2, 4, 4), ("y", "zh", "c", "x", "zl"))
    mp, replica = ("y", "zh", "c"), ("x", "zl")
    in_specs = (
        P(mp, None),
        P(replica, mp, None),
        P(replica, mp, None),
        P(mp + replica, None),
        P(None, mp),
        P(replica, None, None),
        P(replica, None, None, mp),
    )
    out_specs = (P(mp, None), P(mp + replica, None))
    return jax.shard_map(window, mesh=inner, in_specs=in_specs, out_specs=out_specs, check_vma=False)
```

```python
import functools

import jax
import jax.numpy as jnp
from jax import lax
from jax.experimental import pallas as pl
from jax.experimental.pallas import tpu as pltpu
from jax.sharding import Mesh, PartitionSpec as P


STEPS = 2
BLOCK = 128
PRIOR_STEPS = 3

beta_first = 0.9
beta_second = 0.95
adam_epsilon = 1e-08
inner_rate = 0.1
weight_decay = 0.1
outer_mu = 0.9
outer_rate = 0.7
scale_epsilon = 1e-06

ROWS = 160
WIDTH = 5120
TOK = 512
CHUNK = 320
PAIR = 2 * CHUNK
SLOTS = 8
NEAR = 4
TILE = 32
COLS = 256
HALF = WIDTH // 2
PAYLOAD = HALF + BLOCK
QROWS = ROWS // 4
OWN = ROWS // 16

F32 = jnp.float32
BF16 = jnp.bfloat16
FACTOR = WIDTH ** (-0.5)
SCALE = FACTOR / TOK


HB = pl.BlockSpec(memory_space=pltpu.HBM)
VM = pl.BlockSpec(memory_space=pltpu.VMEM)
SM = pl.BlockSpec(memory_space=pltpu.SMEM)


def params(mib):
    return pltpu.CompilerParams(vmem_limit_bytes=mib << 20)


def gather_kernel(where_ref, ids_ref, table_ref, out_ref, total):
    step = 512
    total[...] = jnp.zeros_like(total)

    def body(block, carry):
        start = pl.multiple_of(block * step, step)
        row = lax.broadcasted_iota(jnp.int32, (step, TOK), 0) + start
        pick = jnp.where(row == ids_ref[...], 1.0, 0.0).astype(BF16)
        total[...] += jnp.dot(table_ref[:, pl.ds(start, step)], pick, preferred_element_type=F32)
        return carry

    lax.fori_loop(0, table_ref.shape[1] // step, body, 0)
    out_ref[...] = total[...].astype(BF16)


def gather(where, ids, table_t):
    return pl.pallas_call(
        gather_kernel,
        out_shape=jax.ShapeDtypeStruct((CHUNK, TOK), BF16),
        in_specs=[SM, VM, VM],
        out_specs=VM,
        scratch_shapes=[pltpu.VMEM((CHUNK, TOK), F32)],
        compiler_params=params(16),
        name="gather",
    )(where, ids, table_t)


def pack_kernel(*refs):
    out_ref = refs[-1]
    rows = refs[0].shape[0]
    for index, ref in enumerate(refs[:-1]):
        out_ref[index * rows : (index + 1) * rows, :] = ref[...]


def pack(*chunks):
    rows, width = chunks[0].shape
    return pl.pallas_call(
        pack_kernel,
        out_shape=jax.ShapeDtypeStruct((len(chunks) * rows, width), chunks[0].dtype),
        in_specs=[VM] * len(chunks),
        out_specs=VM,
        compiler_params=params(8),
        name="pack",
    )(*chunks)


def forward_kernel(half, counts, step, where_ref, extra_ref, w_ref, *refs):
    stacks = refs[: 2 * len(counts)]
    out_ref, x_ref, total = refs[2 * len(counts) : 2 * len(counts) + 3]
    core = where_ref[SLOTS]
    total[...] = jnp.zeros_like(total) if half == 0 else extra_ref[...]
    done = 0
    for group, count in enumerate(counts):

        def body(place, carry, group=group, done=done):
            slot = done + place
            rows = pl.ds(pl.multiple_of(place * CHUNK, CHUNK), CHUNK)
            base = slot * PAIR
            for index, at in enumerate((core, 1 - core)):
                to = pl.ds(pl.multiple_of(base + at * CHUNK, CHUNK), CHUNK)
                x_ref[to, :] = stacks[2 * group + index][rows, :]
            if w_ref.shape[1] == WIDTH:
                column = where_ref[half * NEAR + slot] * PAIR
            else:
                column = base
            weight = w_ref[:, pl.ds(pl.multiple_of(column, PAIR), PAIR)].astype(BF16)
            total[...] += jnp.dot(
                weight, x_ref[pl.ds(pl.multiple_of(base, PAIR), PAIR), :], preferred_element_type=F32
            )
            return carry

        lax.fori_loop(0, count, body, 0)
        done += count
    if half == 0:
        out_ref[...] = total[...]
    else:
        target_ref = refs[2 * len(counts) + 3]
        out_ref[...] = (total[...] * FACTOR - target_ref[step].astype(F32)).astype(BF16)


def forward_near_kernel(counts, step, where_ref, w_ref, *refs):
    forward_kernel(0, counts, step, where_ref, None, w_ref, *refs)


def forward_rest_kernel(counts, step, where_ref, total_ref, target_ref, w_ref, *refs):
    forward_kernel(1, counts, step, where_ref, total_ref, w_ref, *refs, target_ref)


def forward(half, step, where, extra, weight, xs):
    flat = [ref for pair in xs for ref in pair]
    counts = tuple(own.shape[0] // CHUNK for own, _ in xs)
    kernel = (forward_near_kernel, forward_rest_kernel)[half]
    return pl.pallas_call(
        functools.partial(kernel, counts, step),
        out_shape=(
            jax.ShapeDtypeStruct((ROWS, TOK), (F32, BF16)[half]),
            jax.ShapeDtypeStruct((HALF, TOK), BF16),
        ),
        in_specs=[SM] + [VM] * (len(extra) + 1 + len(flat)),
        out_specs=(VM, VM),
        scratch_shapes=[pltpu.VMEM((ROWS, TOK), F32)],
        compiler_params=params(24),
        cost_estimate=pl.CostEstimate(
            flops=ROWS * WIDTH * TOK, bytes_accessed=5 << 20, transcendentals=0
        ),
        name="forward",
    )(where, *extra, weight, *flat)


def corrections(step_count):
    return 1.0 / (1.0 - beta_first**step_count), 1.0 / (1.0 - beta_second**step_count)


def first_adam(product, one, two, weight):
    first, second = corrections(PRIOR_STEPS + 1)
    one = beta_first * one + ((1.0 - beta_first) * SCALE) * product
    two = beta_second * two + ((1.0 - beta_second) * SCALE * SCALE) * (product * product)
    update = (one * first) / (jnp.sqrt(two * second) + adam_epsilon)
    current = (1.0 - inner_rate * weight_decay) * weight - inner_rate * update
    first, second = corrections(PRIOR_STEPS + 2)
    kept = weight - (1.0 - inner_rate * weight_decay) * current
    return current, one * (beta_first * first), two * (beta_second * second), kept


def second_adam(product, one, two, kept):
    first, second = corrections(PRIOR_STEPS + 2)
    one = one + ((1.0 - beta_first) * first * SCALE) * product
    two = two + ((1.0 - beta_second) * second * SCALE * SCALE) * (product * product)
    return kept + inner_rate * (one / (jnp.sqrt(two) + adam_epsilon))


def backward(signal_ref, x_ref, grad, consume):
    steps = HALF // COLS

    def product(step, place):
        rows = pl.ds(pl.multiple_of(step * COLS, COLS), COLS)
        grad[place] = lax.dot_general(
            signal_ref[...], x_ref[rows, :], (((1,), (1,)), ((), ())), preferred_element_type=F32
        )

    product(0, 0)

    def body(step, carry):
        product(jnp.minimum(step + 1, steps - 1), (step + 1) % 2)
        for part in range(COLS // BLOCK):
            consume(step * (COLS // BLOCK) + part, part, step % 2)
        return carry

    lax.fori_loop(0, steps, body, 0)


def first_back_kernel(half, where_ref, signal_ref, x_ref, w_ref, one_ref, two_ref, *refs):
    cur_ref, *outs, grad = refs
    per = PAIR // BLOCK

    def consume(block, part, place):
        column = where_ref[half * NEAR + block // per] * PAIR + (block % per) * BLOCK
        source = pl.ds(pl.multiple_of(column, BLOCK), BLOCK)
        to = pl.ds(pl.multiple_of(block * BLOCK, BLOCK), BLOCK)
        for row in range(0, ROWS, TILE):
            rows = slice(row, row + TILE)
            current, *values = first_adam(
                grad[place, rows, part * BLOCK : (part + 1) * BLOCK],
                one_ref[rows, source].astype(F32),
                two_ref[rows, source].astype(F32),
                w_ref[rows, source],
            )
            cur_ref[rows, to] = current.astype(BF16)
            for out, value in zip(outs, values):
                out[rows, to] = value

    backward(signal_ref, x_ref, grad, consume)


def first_back(half, where, signal, x, weight, one, two):
    state = jax.ShapeDtypeStruct((ROWS, HALF), F32)
    return pl.pallas_call(
        functools.partial(first_back_kernel, half),
        out_shape=(jax.ShapeDtypeStruct((ROWS, HALF), BF16), state, state, state),
        in_specs=[SM] + [VM] * 5,
        out_specs=(VM,) * 4,
        scratch_shapes=[pltpu.VMEM((2, ROWS, COLS), F32)],
        compiler_params=params(24),
        cost_estimate=pl.CostEstimate(
            flops=ROWS * WIDTH * TOK, bytes_accessed=14 << 20, transcendentals=0
        ),
        name="first_back",
    )(where, signal, x, weight, one, two)


def second_back_kernel(where_ref, signal_ref, x_ref, one_ref, two_ref, kept_ref, *refs):
    outs = refs[:4]
    grad, scale_buf, code_buf = refs[4:]
    scale_buf[...] = jnp.zeros_like(scale_buf)
    lane = lax.broadcasted_iota(jnp.int32, (QROWS, BLOCK), 1)

    def consume(block, part, place):
        here = pl.ds(pl.multiple_of(block * BLOCK, BLOCK), BLOCK)
        for quarter in range(4):
            rows = slice(quarter * QROWS, (quarter + 1) * QROWS)
            delta = second_adam(
                grad[place, rows, part * BLOCK : (part + 1) * BLOCK],
                one_ref[rows, here],
                two_ref[rows, here],
                kept_ref[rows, here],
            )
            top = jnp.max(jnp.abs(delta), axis=1, keepdims=True) + scale_epsilon
            scale = jnp.broadcast_to(top.astype(BF16).astype(F32), (QROWS, BLOCK))
            code_buf[quarter, :, here] = (delta / scale).astype(BF16)
            scale_buf[quarter] = jnp.where(lane == block, scale, scale_buf[quarter])

    backward(signal_ref, x_ref, grad, consume)
    code_buf[:, :, HALF:] = scale_buf[...].astype(BF16)
    for by in range(4):
        outs[by][...] = code_buf[(where_ref[SLOTS + 1] + by) % 4]


def second_back(where, signal, x, state):
    return pl.pallas_call(
        second_back_kernel,
        out_shape=(jax.ShapeDtypeStruct((QROWS, PAYLOAD), BF16),) * 4,
        in_specs=[SM] + [VM] * 5,
        out_specs=(VM,) * 4,
        scratch_shapes=[
            pltpu.VMEM((2, ROWS, COLS), F32),
            pltpu.VMEM((4, QROWS, BLOCK), F32),
            pltpu.VMEM((4, QROWS, PAYLOAD), BF16),
        ],
        compiler_params=params(24),
        cost_estimate=pl.CostEstimate(
            flops=ROWS * WIDTH * TOK, bytes_accessed=14 << 20, transcendentals=0
        ),
        name="second_back",
    )(where, signal, x, *state)


def partial_kernel(where_ref, *refs):
    gots, outs = refs[:4], refs[4:8]
    part, piece = refs[8:]
    scales = [got[:, HALF:].astype(F32) for got in gots]
    for block in range(HALF // BLOCK):
        here = slice(block * BLOCK, (block + 1) * BLOCK)
        total = jnp.zeros((QROWS, BLOCK), F32)
        for got, scale in zip(gots, scales):
            total = total + got[:, here].astype(F32) * scale[:, block : block + 1]
        part[:, here] = total
    for line in range(4):
        for group in range(NEAR):
            piece[line, group * OWN : (group + 1) * OWN, :] = part[
                line * OWN : (line + 1) * OWN, group * PAIR : (group + 1) * PAIR
            ]
    for by in range(4):
        outs[by][...] = piece[(where_ref[SLOTS + 2] + by) % 4].astype(BF16)


def partial_sums(where, gots):
    return pl.pallas_call(
        partial_kernel,
        out_shape=(jax.ShapeDtypeStruct((QROWS, PAIR), BF16),) * 4,
        in_specs=[SM] + [VM] * 4,
        out_specs=(VM,) * 4,
        scratch_shapes=[
            pltpu.VMEM((QROWS, HALF), F32),
            pltpu.VMEM((4, QROWS, PAIR), F32),
        ],
        compiler_params=params(8),
        name="partial_sums",
    )(where, *gots)


def outer_kernel(half, where_ref, outer_ref, *refs):
    gots, refs = refs[:4], refs[4:]
    if half:
        before_ref, momentum_ref, code_ref, held, sent = refs
    else:
        sent, code_ref, held = refs

    def column(slot):
        return pl.ds(pl.multiple_of(where_ref[slot] * PAIR, PAIR), PAIR)

    for group in range(NEAR):
        held[group * OWN : (group + 1) * OWN, :] = outer_ref[:, column(half * NEAR + group)]
    lane = lax.broadcasted_iota(jnp.int32, (QROWS, BLOCK), 1)
    scales = jnp.zeros((QROWS, BLOCK), F32)
    for block in range(PAIR // BLOCK):
        here = slice(block * BLOCK, (block + 1) * BLOCK)
        total = gots[0][:, here].astype(F32)
        for got in gots[1:]:
            total = total + got[:, here].astype(F32)
        average = total * (1.0 / 16)
        momentum = outer_mu * held[:, here] + average
        sent[:, here] = momentum
        update = average + outer_mu * momentum
        top = jnp.max(jnp.abs(update), axis=1, keepdims=True) + scale_epsilon
        scale = jnp.broadcast_to(top.astype(BF16).astype(F32), (QROWS, BLOCK))
        code_ref[:, here] = (update / scale).astype(BF16)
        scales = jnp.where(lane == block, scale, scales)
    code_ref[:, PAIR:] = scales.astype(BF16)
    if half:
        for group in range(NEAR):
            rows = slice(group * OWN, (group + 1) * OWN)
            momentum_ref[:, column(group)] = before_ref[rows, :]
            momentum_ref[:, column(NEAR + group)] = sent[rows, :]


def outer_step(half, where, outer_momentum, gots, *before):
    momentum = ((QROWS, PAIR), (OWN, WIDTH))[half]
    return pl.pallas_call(
        functools.partial(outer_kernel, half),
        out_shape=(
            jax.ShapeDtypeStruct(momentum, F32),
            jax.ShapeDtypeStruct((QROWS, PAIR + BLOCK), BF16),
        ),
        in_specs=[SM] + [VM] * (5 + len(before)),
        out_specs=(VM, VM),
        scratch_shapes=[pltpu.VMEM((QROWS, PAIR), F32)] * (1 + half),
        compiler_params=params(8),
        name="outer_step",
    )(where, outer_momentum, *gots, *before)


def line_kernel(where_ref, *refs):
    pieces, out_ref, stack = refs[:4], refs[4], refs[5]
    for index, piece in enumerate(pieces):
        stack[index * QROWS : (index + 1) * QROWS, :] = piece[...].astype(F32)
    to = lax.broadcasted_iota(jnp.int32, (ROWS, ROWS), 0)
    source = lax.broadcasted_iota(jnp.int32, (ROWS, ROWS), 1)
    group, line, row = to // QROWS, (to % QROWS) // OWN, to % OWN
    wanted = ((where_ref[SLOTS + 2] - line + 4) % 4) * QROWS + group * OWN + row
    order = jnp.where(source == wanted, 1.0, 0.0).astype(BF16)
    rows = jnp.dot(order, stack[...].astype(BF16), preferred_element_type=F32)
    for group in range(NEAR):
        out_ref[group] = rows[group * QROWS : (group + 1) * QROWS, :].astype(BF16)


def line_rows(where, *pieces):
    return pl.pallas_call(
        line_kernel,
        out_shape=jax.ShapeDtypeStruct((NEAR, QROWS, PAIR + BLOCK), BF16),
        in_specs=[SM] + [VM] * 4,
        out_specs=VM,
        scratch_shapes=[pltpu.VMEM((ROWS, PAIR + BLOCK), F32)],
        compiler_params=params(8),
        name="line_rows",
    )(where, *pieces)


def final_kernel(where_ref, w_ref, *refs):
    pieces = refs[:8]
    out_ref, new_buf, out_sem = refs[8:]
    x = where_ref[SLOTS + 1]
    copies = []
    for by in (0, 1, 3, 2):
        rows = pl.ds(pl.multiple_of(((x - by + 4) % 4) * QROWS, 8), QROWS)

        def slots(group, carry, rows=rows, by=by):
            for half in range(2):
                piece = pieces[half * 4 + by]
                scales = piece[group, :, PAIR:].astype(F32)
                base = where_ref[half * NEAR + group] * PAIR
                for block in range(PAIR // BLOCK):
                    at = pl.ds(pl.multiple_of(base + block * BLOCK, BLOCK), BLOCK)
                    codes = piece[group, :, block * BLOCK : (block + 1) * BLOCK].astype(F32)
                    new_buf[rows, at] = w_ref[rows, at] - outer_rate * (codes * scales[:, block : block + 1])
            return carry

        lax.fori_loop(0, NEAR, slots, 0)
        copies.append(pltpu.make_async_copy(new_buf.at[rows], out_ref.at[rows], out_sem.at[by]))
        copies[-1].start()
    for copy in copies:
        copy.wait()


def final_step(where, weight, pieces):
    return pl.pallas_call(
        final_kernel,
        out_shape=jax.ShapeDtypeStruct((ROWS, WIDTH), F32),
        in_specs=[SM, VM] + [VM] * 8,
        out_specs=HB,
        scratch_shapes=[pltpu.VMEM((ROWS, WIDTH), F32), pltpu.SemaphoreType.DMA((4,))],
        compiler_params=params(16),
        name="final_step",
    )(where, weight, *pieces)


def shift(value, axis, by):
    size = lax.axis_size(axis)
    return lax.ppermute(value, axis, [(i, (i + by) % size) for i in range(size)])


def shifts(values, axis):
    return [shift(value, axis, by) for by, value in zip((1, 2, 3), values)]


def after(value, *others):
    return lax.optimization_barrier((value,) + others)[0]


def swap(own):
    return own, shift(own, "c", 1)


def window(weight, first_moment, second_moment, outer_momentum, act_table, token_ids, targets):
    y, zh, core = lax.axis_index("y"), lax.axis_index("zh"), lax.axis_index("c")
    x, zl = lax.axis_index("x"), lax.axis_index("zl")
    step_y = jnp.array([0, 0, -1, 1, 2, -1, 1, 2, 0, 0, 0], jnp.int32)
    step_z = jnp.array([0, 1, 0, 0, 0, 1, 1, 1, 0, 0, 0], jnp.int32)
    chip = ((y + step_y + 4) % 4) * 2 + (zh + step_z) % 2
    entry = jnp.arange(11)
    where = jnp.where(entry == 8, core, jnp.where(entry == 9, x, jnp.where(entry == 10, zl, chip)))
    where = where.astype(jnp.int32)

    table_t = act_table.T
    ids = token_ids[0]
    wanted = jnp.transpose(targets[0], (0, 2, 1))
    moments = (first_moment[0], second_moment[0])
    own1, own2 = [gather(where, ids[step : step + 1], table_t) for step in range(STEPS)]

    far1 = shift(own1, "zh", 1)
    left1, right1 = shift(own1, "y", 1), shift(own1, "y", -1)
    left2, right2 = shift(own2, "y", 1), shift(own2, "y", -1)
    opposite1, opposite2 = shift(left1, "y", 1), shift(right2, "y", -1)
    far2 = shift(own2, "zh", 1)
    far_left1, far_right1 = shift(far1, "y", 1), shift(far1, "y", -1)
    near1 = swap(pack(own1, far1, left1, right1))
    far_opposite1 = shift(far_right1, "y", -1)
    far_left2 = shift(far2, "y", 1)
    rest1 = swap(pack(opposite1, far_left1, far_right1, far_opposite1))
    total, near1 = forward(0, 0, where, (), weight, [near1])
    far_right2 = shift(after(far2, far_opposite1), "y", -1)
    near2 = swap(pack(own2, far2, left2, right2))
    signal, rest1 = forward(1, 0, where, (total, wanted), weight, [rest1])
    far_opposite2 = shift(far_left2, "y", 1)
    current0, *state0 = first_back(0, where, signal, near1, weight, *moments)
    rest2 = swap(pack(opposite2, far_left2, far_right2))
    current1, *state1 = first_back(1, where, signal, rest1, weight, *moments)
    last2 = swap(far_opposite2)
    total, near2 = forward(0, 1, where, (), current0, [near2])
    signal, rest2 = forward(1, 1, where, (total, wanted), current1, [rest2, last2])

    payloads = []
    for state, x_half in ((state0, near2), (state1, rest2)):
        sends = second_back(where, signal, x_half, state)
        payloads.append([sends[0]] + shifts(sends[1:], "x"))
    momentum, pieces = (), []
    for half in range(2):
        sends = partial_sums(where, payloads[half])
        sums = [sends[0]] + shifts(sends[1:], "zl")
        *momentum, codes = outer_step(half, where, outer_momentum, sums, *momentum)
        line = line_rows(where, codes, *shifts([codes] * 3, "zl"))
        left, right = shift(line, "x", 1), shift(line, "x", 3)
        opposite = shift((left, right)[half], "x", (1, 3)[half])
        pieces += [line, left, opposite, right]
    new_weight = final_step(where, weight, pieces)
    return (new_weight, momentum[0])


def solution(mesh):
    inner = Mesh(mesh.devices.reshape(4, 2, 2, 4, 4), ("y", "zh", "c", "x", "zl"))
    mp, replica = ("y", "zh", "c"), ("x", "zl")
    in_specs = (
        P(mp, None),
        P(replica, mp, None),
        P(replica, mp, None),
        P(mp + replica, None),
        P(None, mp),
        P(replica, None, None),
        P(replica, None, None, mp),
    )
    out_specs = (P(mp, None), P(mp + replica, None))
    return jax.shard_map(window, mesh=inner, in_specs=in_specs, out_specs=out_specs, check_vma=False)
```

```python
import functools

import jax
import jax.numpy as jnp
from jax import lax
from jax.experimental import pallas as pl
from jax.experimental.pallas import tpu as pltpu
from jax.sharding import Mesh, PartitionSpec as P


BLOCK = 128
PRIOR_STEPS = 3

beta_first = 0.9
beta_second = 0.95
adam_epsilon = 1e-08
inner_rate = 0.1
weight_decay = 0.1
outer_mu = 0.9
outer_rate = 0.7
scale_epsilon = 1e-06

ROWS = 160
WIDTH = 5120
TOK = 512
CHUNK = 320
PAIR = 2 * CHUNK
SLOTS = 8
NEAR = 4
TILE = 32
COLS = 256
HALF = WIDTH // 2
PAYLOAD = HALF + BLOCK
QROWS = ROWS // 4
OWN = ROWS // 16

F32 = jnp.float32
BF16 = jnp.bfloat16
FACTOR = WIDTH ** (-0.5)
SCALE = FACTOR / TOK


HB = pl.BlockSpec(memory_space=pltpu.HBM)
VM = pl.BlockSpec(memory_space=pltpu.VMEM)
SM = pl.BlockSpec(memory_space=pltpu.SMEM)


def params(mib):
    return pltpu.CompilerParams(vmem_limit_bytes=mib << 20)


def gather_kernel(step, unroll, ids_ref, table_ref, *refs):
    out_ref, total = refs[-2:]
    width = 512
    total[...] = jnp.zeros_like(total)

    def body(block, carry):
        start = pl.multiple_of(block * width, width)
        row = lax.broadcasted_iota(jnp.int32, (width, TOK), 0) + start
        pick = jnp.where(row == ids_ref[step : step + 1, :], 1.0, 0.0).astype(BF16)
        total[...] += jnp.dot(table_ref[:, pl.ds(start, width)], pick, preferred_element_type=F32)
        return carry

    lax.fori_loop(0, table_ref.shape[1] // width, body, 0, unroll=unroll)
    out_ref[...] = total[...].astype(BF16)


def gather(step, unroll, ids, table_t, *early):
    return pl.pallas_call(
        functools.partial(gather_kernel, step, unroll),
        out_shape=jax.ShapeDtypeStruct((CHUNK, TOK), BF16),
        in_specs=[VM, VM] + [SM] * len(early),
        out_specs=VM,
        scratch_shapes=[pltpu.VMEM((CHUNK, TOK), F32)],
        compiler_params=params(16),
        name="gather",
    )(ids, table_t, *early)


def pack_kernel(*refs):
    out_ref = refs[-1]
    rows = refs[0].shape[0]
    for index, ref in enumerate(refs[:-1]):
        out_ref[index * rows : (index + 1) * rows, :] = ref[...]


def pack(*chunks):
    rows, width = chunks[0].shape
    return pl.pallas_call(
        pack_kernel,
        out_shape=jax.ShapeDtypeStruct((len(chunks) * rows, width), chunks[0].dtype),
        in_specs=[VM] * len(chunks),
        out_specs=VM,
        compiler_params=params(8),
        name="pack",
    )(*chunks)


def forward_kernel(half, counts, step, where_ref, extra_ref, w_ref, *refs):
    stacks = refs[: 2 * len(counts)]
    out_ref, x_ref, total = refs[2 * len(counts) : 2 * len(counts) + 3]
    core = where_ref[SLOTS]
    total[...] = jnp.zeros_like(total) if half == 0 else extra_ref[...]
    done = 0
    for group, count in enumerate(counts):

        def body(place, carry, group=group, done=done):
            slot = done + place
            rows = pl.ds(pl.multiple_of(place * CHUNK, CHUNK), CHUNK)
            base = slot * PAIR
            for index, at in enumerate((core, 1 - core)):
                to = pl.ds(pl.multiple_of(base + at * CHUNK, CHUNK), CHUNK)
                x_ref[to, :] = stacks[2 * group + index][rows, :]
            if w_ref.shape[1] == WIDTH:
                column = where_ref[half * NEAR + slot] * PAIR
            else:
                column = base
            weight = w_ref[:, pl.ds(pl.multiple_of(column, PAIR), PAIR)].astype(BF16)
            total[...] += jnp.dot(
                weight, x_ref[pl.ds(pl.multiple_of(base, PAIR), PAIR), :], preferred_element_type=F32
            )
            return carry

        lax.fori_loop(0, count, body, 0)
        done += count
    if half == 0:
        out_ref[...] = total[...]
    else:
        target_ref = refs[2 * len(counts) + 3]
        out_ref[...] = (total[...] * FACTOR - target_ref[step].astype(F32)).astype(BF16)


def forward_near_kernel(counts, step, where_ref, w_ref, *refs):
    forward_kernel(0, counts, step, where_ref, None, w_ref, *refs)


def forward_rest_kernel(counts, step, where_ref, total_ref, target_ref, w_ref, *refs):
    forward_kernel(1, counts, step, where_ref, total_ref, w_ref, *refs, target_ref)


def forward(half, step, where, extra, weight, xs):
    flat = [ref for pair in xs for ref in pair]
    counts = tuple(own.shape[0] // CHUNK for own, _ in xs)
    kernel = (forward_near_kernel, forward_rest_kernel)[half]
    return pl.pallas_call(
        functools.partial(kernel, counts, step),
        out_shape=(
            jax.ShapeDtypeStruct((ROWS, TOK), (F32, BF16)[half]),
            jax.ShapeDtypeStruct((HALF, TOK), BF16),
        ),
        in_specs=[SM] + [VM] * (len(extra) + 1 + len(flat)),
        out_specs=(VM, VM),
        scratch_shapes=[pltpu.VMEM((ROWS, TOK), F32)],
        compiler_params=params(24),
        cost_estimate=pl.CostEstimate(
            flops=ROWS * WIDTH * TOK, bytes_accessed=5 << 20, transcendentals=0
        ),
        name="forward",
    )(where, *extra, weight, *flat)


def corrections(step_count):
    return 1.0 / (1.0 - beta_first**step_count), 1.0 / (1.0 - beta_second**step_count)


def root(value):
    return value * lax.rsqrt(value)


def first_adam(product, one, two, weight):
    first, second = corrections(PRIOR_STEPS + 1)
    one = beta_first * one + ((1.0 - beta_first) * SCALE) * product
    two = beta_second * two + ((1.0 - beta_second) * SCALE * SCALE) * (product * product)
    update = (one * first) / (root(two * second) + adam_epsilon)
    current = (1.0 - inner_rate * weight_decay) * weight - inner_rate * update
    first, second = corrections(PRIOR_STEPS + 2)
    kept = weight - (1.0 - inner_rate * weight_decay) * current
    return current, one * (beta_first * first), two * (beta_second * second), kept


def second_adam(product, one, two, kept):
    first, second = corrections(PRIOR_STEPS + 2)
    one = one + ((1.0 - beta_first) * first * SCALE) * product
    two = two + ((1.0 - beta_second) * second * SCALE * SCALE) * (product * product)
    return kept + inner_rate * (one / (root(two) + adam_epsilon))


def backward(signal_ref, x_ref, grad, consume):
    steps = HALF // COLS

    def product(step, place):
        rows = pl.ds(pl.multiple_of(step * COLS, COLS), COLS)
        grad[place] = lax.dot_general(
            signal_ref[...], x_ref[rows, :], (((1,), (1,)), ((), ())), preferred_element_type=F32
        )

    product(0, 0)

    def body(step, carry):
        product(jnp.minimum(step + 1, steps - 1), (step + 1) % 2)
        for part in range(COLS // BLOCK):
            consume(step * (COLS // BLOCK) + part, part, step % 2)
        return carry

    lax.fori_loop(0, steps, body, 0)


def first_back_kernel(half, where_ref, signal_ref, x_ref, w_ref, one_ref, two_ref, *refs):
    cur_ref, *outs, grad = refs
    per = PAIR // BLOCK

    def consume(block, part, place):
        column = where_ref[half * NEAR + block // per] * PAIR + (block % per) * BLOCK
        source = pl.ds(pl.multiple_of(column, BLOCK), BLOCK)
        to = pl.ds(pl.multiple_of(block * BLOCK, BLOCK), BLOCK)
        for row in range(0, ROWS, TILE):
            rows = slice(row, row + TILE)
            current, *values = first_adam(
                grad[place, rows, part * BLOCK : (part + 1) * BLOCK],
                one_ref[rows, source].astype(F32),
                two_ref[rows, source].astype(F32),
                w_ref[rows, source],
            )
            cur_ref[rows, to] = current.astype(BF16)
            for out, value in zip(outs, values):
                out[rows, to] = value

    backward(signal_ref, x_ref, grad, consume)


def first_back(half, where, signal, x, weight, one, two):
    state = jax.ShapeDtypeStruct((ROWS, HALF), F32)
    return pl.pallas_call(
        functools.partial(first_back_kernel, half),
        out_shape=(jax.ShapeDtypeStruct((ROWS, HALF), BF16), state, state, state),
        in_specs=[SM] + [VM] * 5,
        out_specs=(VM,) * 4,
        scratch_shapes=[pltpu.VMEM((2, ROWS, COLS), F32)],
        compiler_params=params(24),
        cost_estimate=pl.CostEstimate(
            flops=ROWS * WIDTH * TOK, bytes_accessed=14 << 20, transcendentals=0
        ),
        name="first_back",
    )(where, signal, x, weight, one, two)


def second_back_kernel(where_ref, signal_ref, x_ref, one_ref, two_ref, kept_ref, *refs):
    outs = refs[:4]
    grad, scale_buf, code_buf = refs[4:]
    scale_buf[...] = jnp.zeros_like(scale_buf)
    lane = lax.broadcasted_iota(jnp.int32, (QROWS, BLOCK), 1)

    def consume(block, part, place):
        here = pl.ds(pl.multiple_of(block * BLOCK, BLOCK), BLOCK)
        for quarter in range(4):
            rows = slice(quarter * QROWS, (quarter + 1) * QROWS)
            delta = second_adam(
                grad[place, rows, part * BLOCK : (part + 1) * BLOCK],
                one_ref[rows, here],
                two_ref[rows, here],
                kept_ref[rows, here],
            )
            top = jnp.max(jnp.abs(delta), axis=1, keepdims=True) + scale_epsilon
            scale = jnp.broadcast_to(top.astype(BF16).astype(F32), (QROWS, BLOCK))
            code_buf[quarter, :, here] = (delta / scale).astype(BF16)
            scale_buf[quarter] = jnp.where(lane == block, scale, scale_buf[quarter])

    backward(signal_ref, x_ref, grad, consume)
    code_buf[:, :, HALF:] = scale_buf[...].astype(BF16)
    for by in range(4):
        outs[by][...] = code_buf[(where_ref[SLOTS + 1] + by) % 4]


def second_back(where, signal, x, state):
    return pl.pallas_call(
        second_back_kernel,
        out_shape=(jax.ShapeDtypeStruct((QROWS, PAYLOAD), BF16),) * 4,
        in_specs=[SM] + [VM] * 5,
        out_specs=(VM,) * 4,
        scratch_shapes=[
            pltpu.VMEM((2, ROWS, COLS), F32),
            pltpu.VMEM((4, QROWS, BLOCK), F32),
            pltpu.VMEM((4, QROWS, PAYLOAD), BF16),
        ],
        compiler_params=params(24),
        cost_estimate=pl.CostEstimate(
            flops=ROWS * WIDTH * TOK, bytes_accessed=14 << 20, transcendentals=0
        ),
        name="second_back",
    )(where, signal, x, *state)


def partial_kernel(where_ref, *refs):
    gots, outs = refs[:4], refs[4:8]
    part, piece = refs[8:]
    scales = [got[:, HALF:].astype(F32) for got in gots]
    for block in range(HALF // BLOCK):
        here = slice(block * BLOCK, (block + 1) * BLOCK)
        total = jnp.zeros((QROWS, BLOCK), F32)
        for got, scale in zip(gots, scales):
            total = total + got[:, here].astype(F32) * scale[:, block : block + 1]
        part[:, here] = total
    for line in range(4):
        for group in range(NEAR):
            piece[line, group * OWN : (group + 1) * OWN, :] = part[
                line * OWN : (line + 1) * OWN, group * PAIR : (group + 1) * PAIR
            ]
    for by in range(4):
        outs[by][...] = piece[(where_ref[SLOTS + 2] + by) % 4].astype(BF16)


def partial_sums(where, gots):
    return pl.pallas_call(
        partial_kernel,
        out_shape=(jax.ShapeDtypeStruct((QROWS, PAIR), BF16),) * 4,
        in_specs=[SM] + [VM] * 4,
        out_specs=(VM,) * 4,
        scratch_shapes=[
            pltpu.VMEM((QROWS, HALF), F32),
            pltpu.VMEM((4, QROWS, PAIR), F32),
        ],
        compiler_params=params(8),
        name="partial_sums",
    )(where, *gots)


def outer_kernel(half, where_ref, outer_ref, *refs):
    gots, refs = refs[:4], refs[4:]
    if half:
        before_ref, momentum_ref, code_ref, held, sent = refs
    else:
        sent, code_ref, held = refs

    def column(slot):
        return pl.ds(pl.multiple_of(where_ref[slot] * PAIR, PAIR), PAIR)

    for group in range(NEAR):
        held[group * OWN : (group + 1) * OWN, :] = outer_ref[:, column(half * NEAR + group)]
    lane = lax.broadcasted_iota(jnp.int32, (QROWS, BLOCK), 1)
    scales = jnp.zeros((QROWS, BLOCK), F32)
    for block in range(PAIR // BLOCK):
        here = slice(block * BLOCK, (block + 1) * BLOCK)
        total = gots[0][:, here].astype(F32)
        for got in gots[1:]:
            total = total + got[:, here].astype(F32)
        average = total * (1.0 / 16)
        momentum = outer_mu * held[:, here] + average
        sent[:, here] = momentum
        update = average + outer_mu * momentum
        top = jnp.max(jnp.abs(update), axis=1, keepdims=True) + scale_epsilon
        scale = jnp.broadcast_to(top.astype(BF16).astype(F32), (QROWS, BLOCK))
        code_ref[:, here] = (update / scale).astype(BF16)
        scales = jnp.where(lane == block, scale, scales)
    code_ref[:, PAIR:] = scales.astype(BF16)
    if half:
        for group in range(NEAR):
            rows = slice(group * OWN, (group + 1) * OWN)
            momentum_ref[:, column(group)] = before_ref[rows, :]
            momentum_ref[:, column(NEAR + group)] = sent[rows, :]


def outer_step(half, where, outer_momentum, gots, *before):
    momentum = ((QROWS, PAIR), (OWN, WIDTH))[half]
    return pl.pallas_call(
        functools.partial(outer_kernel, half),
        out_shape=(
            jax.ShapeDtypeStruct(momentum, F32),
            jax.ShapeDtypeStruct((QROWS, PAIR + BLOCK), BF16),
        ),
        in_specs=[SM] + [VM] * (5 + len(before)),
        out_specs=(VM, VM),
        scratch_shapes=[pltpu.VMEM((QROWS, PAIR), F32)] * (1 + half),
        compiler_params=params(8),
        name="outer_step",
    )(where, outer_momentum, *gots, *before)


def line_kernel(where_ref, *refs):
    pieces, out_ref, stack = refs[:4], refs[4], refs[5]
    for index, piece in enumerate(pieces):
        stack[index * QROWS : (index + 1) * QROWS, :] = piece[...].astype(F32)
    to = lax.broadcasted_iota(jnp.int32, (ROWS, ROWS), 0)
    source = lax.broadcasted_iota(jnp.int32, (ROWS, ROWS), 1)
    group, line, row = to // QROWS, (to % QROWS) // OWN, to % OWN
    wanted = ((where_ref[SLOTS + 2] - line + 4) % 4) * QROWS + group * OWN + row
    order = jnp.where(source == wanted, 1.0, 0.0).astype(BF16)
    rows = jnp.dot(order, stack[...].astype(BF16), preferred_element_type=F32)
    for group in range(NEAR):
        out_ref[group] = rows[group * QROWS : (group + 1) * QROWS, :].astype(BF16)


def line_rows(where, *pieces):
    return pl.pallas_call(
        line_kernel,
        out_shape=jax.ShapeDtypeStruct((NEAR, QROWS, PAIR + BLOCK), BF16),
        in_specs=[SM] + [VM] * 4,
        out_specs=VM,
        scratch_shapes=[pltpu.VMEM((ROWS, PAIR + BLOCK), F32)],
        compiler_params=params(8),
        name="line_rows",
    )(where, *pieces)


def final_kernel(where_ref, w_ref, *refs):
    pieces = refs[:8]
    out_ref, new_buf, out_sem = refs[8:]
    x = where_ref[SLOTS + 1]
    copies = []
    for by in (0, 1, 3, 2):
        rows = pl.ds(pl.multiple_of(((x - by + 4) % 4) * QROWS, 8), QROWS)

        def slots(group, carry, rows=rows, by=by):
            for half in range(2):
                piece = pieces[half * 4 + by]
                scales = piece[group, :, PAIR:].astype(F32)
                base = where_ref[half * NEAR + group] * PAIR
                for block in range(PAIR // BLOCK):
                    at = pl.ds(pl.multiple_of(base + block * BLOCK, BLOCK), BLOCK)
                    codes = piece[group, :, block * BLOCK : (block + 1) * BLOCK].astype(F32)
                    new_buf[rows, at] = w_ref[rows, at] - outer_rate * (codes * scales[:, block : block + 1])
            return carry

        lax.fori_loop(0, NEAR, slots, 0)
        copies.append(pltpu.make_async_copy(new_buf.at[rows], out_ref.at[rows], out_sem.at[by]))
        copies[-1].start()
    for copy in copies:
        copy.wait()


def final_step(where, weight, pieces):
    return pl.pallas_call(
        final_kernel,
        out_shape=jax.ShapeDtypeStruct((ROWS, WIDTH), F32),
        in_specs=[SM, VM] + [VM] * 8,
        out_specs=HB,
        scratch_shapes=[pltpu.VMEM((ROWS, WIDTH), F32), pltpu.SemaphoreType.DMA((4,))],
        compiler_params=params(16),
        name="final_step",
    )(where, weight, *pieces)


def shift(value, axis, by):
    size = lax.axis_size(axis)
    return lax.ppermute(value, axis, [(i, (i + by) % size) for i in range(size)])


def shifts(values, axis):
    return [shift(value, axis, by) for by, value in zip((1, 2, 3), values)]


def after(value, *others):
    return lax.optimization_barrier((value,) + others)[0]


def swap(own):
    return own, shift(own, "c", 1)


def window(weight, first_moment, second_moment, outer_momentum, act_table, token_ids, targets):
    y, zh, core = lax.axis_index("y"), lax.axis_index("zh"), lax.axis_index("c")
    x, zl = lax.axis_index("x"), lax.axis_index("zl")
    step_y = jnp.array([0, 0, -1, 1, 2, -1, 1, 2, 0, 0, 0], jnp.int32)
    step_z = jnp.array([0, 1, 0, 0, 0, 1, 1, 1, 0, 0, 0], jnp.int32)
    chip = ((y + step_y + 4) % 4) * 2 + (zh + step_z) % 2
    entry = jnp.arange(11)
    where = jnp.where(entry == 8, core, jnp.where(entry == 9, x, jnp.where(entry == 10, zl, chip)))
    where = where.astype(jnp.int32)

    table_t = act_table.T
    ids = token_ids[0]
    wanted = jnp.transpose(targets[0], (0, 2, 1))
    moments = (first_moment[0], second_moment[0])
    own1 = gather(0, True, ids, table_t)
    own2 = gather(1, False, ids, table_t, where)

    far1 = shift(own1, "zh", 1)
    left1, right1 = shift(own1, "y", 1), shift(own1, "y", -1)
    left2, right2 = shift(own2, "y", 1), shift(own2, "y", -1)
    opposite1, opposite2 = shift(left1, "y", 1), shift(right2, "y", -1)
    far2 = shift(own2, "zh", 1)
    far_left1, far_right1 = shift(far1, "y", 1), shift(far1, "y", -1)
    near1 = swap(pack(own1, far1, left1, right1))
    far_opposite1 = shift(far_right1, "y", -1)
    far_left2 = shift(far2, "y", 1)
    rest1 = swap(pack(opposite1, far_left1, far_right1, far_opposite1))
    total, near1 = forward(0, 0, where, (), weight, [near1])
    far_right2 = shift(after(far2, far_opposite1), "y", -1)
    near2 = swap(pack(own2, far2, left2, right2))
    signal, rest1 = forward(1, 0, where, (total, wanted), weight, [rest1])
    far_opposite2 = shift(far_left2, "y", 1)
    current0, *state0 = first_back(0, where, signal, near1, weight, *moments)
    rest2 = swap(pack(opposite2, far_left2, far_right2))
    current1, *state1 = first_back(1, where, signal, rest1, weight, *moments)
    last2 = swap(far_opposite2)
    total, near2 = forward(0, 1, where, (), current0, [near2])
    signal, rest2 = forward(1, 1, where, (total, wanted), current1, [rest2, last2])

    payloads = []
    for state, x_half in ((state0, near2), (state1, rest2)):
        sends = second_back(where, signal, x_half, state)
        payloads.append([sends[0]] + shifts(sends[1:], "x"))
    momentum, pieces = (), []
    for half in range(2):
        sends = partial_sums(where, payloads[half])
        sums = [sends[0]] + shifts(sends[1:], "zl")
        *momentum, codes = outer_step(half, where, outer_momentum, sums, *momentum)
        line = line_rows(where, codes, *shifts([codes] * 3, "zl"))
        left, right = shift(line, "x", 1), shift(line, "x", 3)
        opposite = shift((left, right)[half], "x", (1, 3)[half])
        pieces += [line, left, opposite, right]
    new_weight = final_step(where, weight, pieces)
    return (new_weight, momentum[0])


def solution(mesh):
    inner = Mesh(mesh.devices.reshape(4, 2, 2, 4, 4), ("y", "zh", "c", "x", "zl"))
    mp, replica = ("y", "zh", "c"), ("x", "zl")
    in_specs = (
        P(mp, None),
        P(replica, mp, None),
        P(replica, mp, None),
        P(mp + replica, None),
        P(None, mp),
        P(replica, None, None),
        P(replica, None, None, mp),
    )
    out_specs = (P(mp, None), P(mp + replica, None))
    return jax.shard_map(window, mesh=inner, in_specs=in_specs, out_specs=out_specs, check_vma=False)
```

```python
import functools

import jax
import jax.numpy as jnp
from jax import lax
from jax.experimental import pallas as pl
from jax.experimental.pallas import tpu as pltpu
from jax.sharding import Mesh, PartitionSpec as P


BLOCK = 128
PRIOR_STEPS = 3

beta_first = 0.9
beta_second = 0.95
adam_epsilon = 1e-08
inner_rate = 0.1
weight_decay = 0.1
outer_mu = 0.9
outer_rate = 0.7
scale_epsilon = 1e-06

ROWS = 160
WIDTH = 5120
TOK = 512
CHUNK = 320
PAIR = 2 * CHUNK
SLOTS = 8
NEAR = 4
TILE = 32
COLS = 256
HALF = WIDTH // 2
PAYLOAD = HALF + BLOCK
QROWS = ROWS // 4
OWN = ROWS // 16

F32 = jnp.float32
BF16 = jnp.bfloat16
FACTOR = WIDTH ** (-0.5)
SCALE = FACTOR / TOK


HB = pl.BlockSpec(memory_space=pltpu.HBM)
VM = pl.BlockSpec(memory_space=pltpu.VMEM)
SM = pl.BlockSpec(memory_space=pltpu.SMEM)


def params(mib):
    return pltpu.CompilerParams(vmem_limit_bytes=mib << 20)


def gather_kernel(step, unroll, ids_ref, table_ref, *refs):
    out_ref, total = refs[-2:]
    width = 512
    total[...] = jnp.zeros_like(total)

    def body(block, carry):
        start = pl.multiple_of(block * width, width)
        row = lax.broadcasted_iota(jnp.int32, (width, TOK), 0) + start
        pick = jnp.where(row == ids_ref[step : step + 1, :], 1.0, 0.0).astype(BF16)
        total[...] += jnp.dot(table_ref[:, pl.ds(start, width)], pick, preferred_element_type=F32)
        return carry

    lax.fori_loop(0, table_ref.shape[1] // width, body, 0, unroll=unroll)
    out_ref[...] = total[...].astype(BF16)


def gather(step, unroll, ids, table_t, *early):
    return pl.pallas_call(
        functools.partial(gather_kernel, step, unroll),
        out_shape=jax.ShapeDtypeStruct((CHUNK, TOK), BF16),
        in_specs=[VM, VM] + [SM] * len(early),
        out_specs=VM,
        scratch_shapes=[pltpu.VMEM((CHUNK, TOK), F32)],
        compiler_params=params(16),
        name="gather",
    )(ids, table_t, *early)


def pack_kernel(*refs):
    out_ref = refs[-1]
    rows = refs[0].shape[0]
    for index, ref in enumerate(refs[:-1]):
        out_ref[index * rows : (index + 1) * rows, :] = ref[...]


def pack(*chunks):
    rows, width = chunks[0].shape
    return pl.pallas_call(
        pack_kernel,
        out_shape=jax.ShapeDtypeStruct((len(chunks) * rows, width), chunks[0].dtype),
        in_specs=[VM] * len(chunks),
        out_specs=VM,
        compiler_params=params(8),
        name="pack",
    )(*chunks)


def forward_kernel(half, counts, step, where_ref, extra_ref, w_ref, *refs):
    stacks = refs[: 2 * len(counts)]
    out_ref, x_ref, total = refs[2 * len(counts) : 2 * len(counts) + 3]
    core = where_ref[SLOTS]
    total[...] = jnp.zeros_like(total) if half == 0 else extra_ref[...]

    def ordered(slot, place, group):
        rows = pl.ds(pl.multiple_of(place * CHUNK, CHUNK), CHUNK)
        for index, at in enumerate((core, 1 - core)):
            to = pl.ds(pl.multiple_of(slot * PAIR + at * CHUNK, CHUNK), CHUNK)
            x_ref[to, :] = stacks[2 * group + index][rows, :]

    done = counts[0]
    for group, count in enumerate(counts[1:]):
        for place in range(count):
            ordered(done + place, place, group + 1)
        done += count

    def body(slot, carry):
        if len(counts) == 1:
            ordered(slot, slot, 0)
        else:
            pl.when(slot < counts[0])(lambda: ordered(slot, slot, 0))
        base = slot * PAIR
        if w_ref.shape[1] == WIDTH:
            column = where_ref[half * NEAR + slot] * PAIR
        else:
            column = base
        weight = w_ref[:, pl.ds(pl.multiple_of(column, PAIR), PAIR)].astype(BF16)
        total[...] += jnp.dot(
            weight, x_ref[pl.ds(pl.multiple_of(base, PAIR), PAIR), :], preferred_element_type=F32
        )
        return carry

    lax.fori_loop(0, NEAR, body, 0)
    if half == 0:
        out_ref[...] = total[...]
    else:
        target_ref = refs[2 * len(counts) + 3]
        out_ref[...] = (total[...] * FACTOR - target_ref[step].astype(F32)).astype(BF16)


def forward_near_kernel(counts, step, where_ref, w_ref, *refs):
    forward_kernel(0, counts, step, where_ref, None, w_ref, *refs)


def forward_rest_kernel(counts, step, where_ref, total_ref, target_ref, w_ref, *refs):
    forward_kernel(1, counts, step, where_ref, total_ref, w_ref, *refs, target_ref)


def forward(half, step, where, extra, weight, xs):
    flat = [ref for pair in xs for ref in pair]
    counts = tuple(own.shape[0] // CHUNK for own, _ in xs)
    kernel = (forward_near_kernel, forward_rest_kernel)[half]
    return pl.pallas_call(
        functools.partial(kernel, counts, step),
        out_shape=(
            jax.ShapeDtypeStruct((ROWS, TOK), (F32, BF16)[half]),
            jax.ShapeDtypeStruct((HALF, TOK), BF16),
        ),
        in_specs=[SM] + [VM] * (len(extra) + 1 + len(flat)),
        out_specs=(VM, VM),
        scratch_shapes=[pltpu.VMEM((ROWS, TOK), F32)],
        compiler_params=params(24),
        cost_estimate=pl.CostEstimate(
            flops=ROWS * WIDTH * TOK, bytes_accessed=5 << 20, transcendentals=0
        ),
        name="forward",
    )(where, *extra, weight, *flat)


def corrections(step_count):
    return 1.0 / (1.0 - beta_first**step_count), 1.0 / (1.0 - beta_second**step_count)


def root(value):
    return value * lax.rsqrt(value)


def first_adam(product, one, two, weight):
    first, second = corrections(PRIOR_STEPS + 1)
    one = beta_first * one + ((1.0 - beta_first) * SCALE) * product
    two = beta_second * two + ((1.0 - beta_second) * SCALE * SCALE) * (product * product)
    update = (one * first) / (root(two * second) + adam_epsilon)
    current = (1.0 - inner_rate * weight_decay) * weight - inner_rate * update
    first, second = corrections(PRIOR_STEPS + 2)
    kept = weight - (1.0 - inner_rate * weight_decay) * current
    return current, one * (beta_first * first), two * (beta_second * second), kept


def second_adam(product, one, two, kept):
    first, second = corrections(PRIOR_STEPS + 2)
    one = one + ((1.0 - beta_first) * first * SCALE) * product
    two = two + ((1.0 - beta_second) * second * SCALE * SCALE) * (product * product)
    return kept + inner_rate * (one / (root(two) + adam_epsilon))


def backward(signal_ref, x_ref, grad, consume):
    steps = HALF // COLS

    def product(step, place):
        rows = pl.ds(pl.multiple_of(step * COLS, COLS), COLS)
        grad[place] = lax.dot_general(
            signal_ref[...], x_ref[rows, :], (((1,), (1,)), ((), ())), preferred_element_type=F32
        )

    product(0, 0)

    def body(step, carry):
        product(jnp.minimum(step + 1, steps - 1), (step + 1) % 2)
        for part in range(COLS // BLOCK):
            consume(step * (COLS // BLOCK) + part, part, step % 2)
        return carry

    lax.fori_loop(0, steps, body, 0)


def first_back_kernel(half, where_ref, signal_ref, x_ref, w_ref, one_ref, two_ref, *refs):
    cur_ref, *outs, grad = refs
    per = PAIR // BLOCK

    def consume(block, part, place):
        column = where_ref[half * NEAR + block // per] * PAIR + (block % per) * BLOCK
        source = pl.ds(pl.multiple_of(column, BLOCK), BLOCK)
        to = pl.ds(pl.multiple_of(block * BLOCK, BLOCK), BLOCK)
        for row in range(0, ROWS, TILE):
            rows = slice(row, row + TILE)
            current, *values = first_adam(
                grad[place, rows, part * BLOCK : (part + 1) * BLOCK],
                one_ref[rows, source].astype(F32),
                two_ref[rows, source].astype(F32),
                w_ref[rows, source],
            )
            cur_ref[rows, to] = current.astype(BF16)
            for out, value in zip(outs, values):
                out[rows, to] = value

    backward(signal_ref, x_ref, grad, consume)


def first_back(half, where, signal, x, weight, one, two):
    state = jax.ShapeDtypeStruct((ROWS, HALF), F32)
    return pl.pallas_call(
        functools.partial(first_back_kernel, half),
        out_shape=(jax.ShapeDtypeStruct((ROWS, HALF), BF16), state, state, state),
        in_specs=[SM] + [VM] * 5,
        out_specs=(VM,) * 4,
        scratch_shapes=[pltpu.VMEM((2, ROWS, COLS), F32)],
        compiler_params=params(24),
        cost_estimate=pl.CostEstimate(
            flops=ROWS * WIDTH * TOK, bytes_accessed=14 << 20, transcendentals=0
        ),
        name="first_back",
    )(where, signal, x, weight, one, two)


def second_back_kernel(where_ref, signal_ref, x_ref, one_ref, two_ref, kept_ref, *refs):
    outs = refs[:4]
    grad, scale_buf, code_buf = refs[4:]
    scale_buf[...] = jnp.zeros_like(scale_buf)
    lane = lax.broadcasted_iota(jnp.int32, (QROWS, BLOCK), 1)

    def consume(block, part, place):
        here = pl.ds(pl.multiple_of(block * BLOCK, BLOCK), BLOCK)
        for quarter in range(4):
            rows = slice(quarter * QROWS, (quarter + 1) * QROWS)
            delta = second_adam(
                grad[place, rows, part * BLOCK : (part + 1) * BLOCK],
                one_ref[rows, here],
                two_ref[rows, here],
                kept_ref[rows, here],
            )
            top = jnp.max(jnp.abs(delta), axis=1, keepdims=True) + scale_epsilon
            scale = jnp.broadcast_to(top.astype(BF16).astype(F32), (QROWS, BLOCK))
            code_buf[quarter, :, here] = (delta / scale).astype(BF16)
            scale_buf[quarter] = jnp.where(lane == block, scale, scale_buf[quarter])

    backward(signal_ref, x_ref, grad, consume)
    code_buf[:, :, HALF:] = scale_buf[...].astype(BF16)
    for by in range(4):
        outs[by][...] = code_buf[(where_ref[SLOTS + 1] + by) % 4]


def second_back(where, signal, x, state):
    return pl.pallas_call(
        second_back_kernel,
        out_shape=(jax.ShapeDtypeStruct((QROWS, PAYLOAD), BF16),) * 4,
        in_specs=[SM] + [VM] * 5,
        out_specs=(VM,) * 4,
        scratch_shapes=[
            pltpu.VMEM((2, ROWS, COLS), F32),
            pltpu.VMEM((4, QROWS, BLOCK), F32),
            pltpu.VMEM((4, QROWS, PAYLOAD), BF16),
        ],
        compiler_params=params(24),
        cost_estimate=pl.CostEstimate(
            flops=ROWS * WIDTH * TOK, bytes_accessed=14 << 20, transcendentals=0
        ),
        name="second_back",
    )(where, signal, x, *state)


def partial_kernel(where_ref, *refs):
    gots, outs = refs[:4], refs[4:8]
    part, piece = refs[8:]
    scales = [got[:, HALF:].astype(F32) for got in gots]
    for block in range(HALF // BLOCK):
        here = slice(block * BLOCK, (block + 1) * BLOCK)
        total = jnp.zeros((QROWS, BLOCK), F32)
        for got, scale in zip(gots, scales):
            total = total + got[:, here].astype(F32) * scale[:, block : block + 1]
        part[:, here] = total
    for line in range(4):
        for group in range(NEAR):
            piece[line, group * OWN : (group + 1) * OWN, :] = part[
                line * OWN : (line + 1) * OWN, group * PAIR : (group + 1) * PAIR
            ]
    for by in range(4):
        outs[by][...] = piece[(where_ref[SLOTS + 2] + by) % 4].astype(BF16)


def partial_sums(where, gots):
    return pl.pallas_call(
        partial_kernel,
        out_shape=(jax.ShapeDtypeStruct((QROWS, PAIR), BF16),) * 4,
        in_specs=[SM] + [VM] * 4,
        out_specs=(VM,) * 4,
        scratch_shapes=[
            pltpu.VMEM((QROWS, HALF), F32),
            pltpu.VMEM((4, QROWS, PAIR), F32),
        ],
        compiler_params=params(8),
        name="partial_sums",
    )(where, *gots)


def column(where_ref, slot):
    return pl.ds(pl.multiple_of(where_ref[slot] * PAIR, PAIR), PAIR)


def outer_kernel(half, where_ref, outer_ref, *refs):
    gots, refs = refs[:4], refs[4:]
    if half:
        scales_ref, sent, code_ref, held = refs
        scales = scales_ref[...]
    else:
        sent, code_ref, scales_ref, held = refs
        scales = jnp.zeros((QROWS, BLOCK), F32)
    for group in range(NEAR):
        held[group * OWN : (group + 1) * OWN, :] = outer_ref[:, column(where_ref, half * NEAR + group)]
    lane = lax.broadcasted_iota(jnp.int32, (QROWS, BLOCK), 1)
    blocks = PAIR // BLOCK
    for block in range(blocks):
        here = slice(block * BLOCK, (block + 1) * BLOCK)
        total = gots[0][:, here].astype(F32)
        for got in gots[1:]:
            total = total + got[:, here].astype(F32)
        average = total * (1.0 / 16)
        momentum = outer_mu * held[:, here] + average
        sent[:, here] = momentum
        update = average + outer_mu * momentum
        top = jnp.max(jnp.abs(update), axis=1, keepdims=True) + scale_epsilon
        scale = jnp.broadcast_to(top.astype(BF16).astype(F32), (QROWS, BLOCK))
        code_ref[:, here] = (update / scale).astype(BF16)
        scales = jnp.where(lane == half * blocks + block, scale, scales)
    if half:
        code_ref[:, PAIR:] = scales.astype(BF16)
    else:
        scales_ref[...] = scales


def outer_step(half, where, outer_momentum, gots, *scales):
    out_shape = [
        jax.ShapeDtypeStruct((QROWS, PAIR), F32),
        jax.ShapeDtypeStruct((QROWS, PAIR + half * BLOCK), BF16),
    ]
    if not half:
        out_shape.append(jax.ShapeDtypeStruct((QROWS, BLOCK), F32))
    return pl.pallas_call(
        functools.partial(outer_kernel, half),
        out_shape=tuple(out_shape),
        in_specs=[SM] + [VM] * (5 + len(scales)),
        out_specs=(VM,) * len(out_shape),
        scratch_shapes=[pltpu.VMEM((QROWS, PAIR), F32)],
        compiler_params=params(8),
        name="outer_step",
    )(where, outer_momentum, *gots, *scales)


def momentum_kernel(where_ref, near_ref, rest_ref, out_ref):
    for group in range(NEAR):
        rows = slice(group * OWN, (group + 1) * OWN)
        out_ref[:, column(where_ref, group)] = near_ref[rows, :]
        out_ref[:, column(where_ref, NEAR + group)] = rest_ref[rows, :]


def momentum_rows(where, near, rest):
    return pl.pallas_call(
        momentum_kernel,
        out_shape=jax.ShapeDtypeStruct((OWN, WIDTH), F32),
        in_specs=[SM, VM, VM],
        out_specs=VM,
        compiler_params=params(8),
        name="momentum_rows",
    )(where, near, rest)


def line_kernel(where_ref, *refs):
    pieces, out_ref, stack = refs[:4], refs[4], refs[5]
    for index, piece in enumerate(pieces):
        stack[index * QROWS : (index + 1) * QROWS, :] = piece[...].astype(F32)
    to = lax.broadcasted_iota(jnp.int32, (ROWS, ROWS), 0)
    source = lax.broadcasted_iota(jnp.int32, (ROWS, ROWS), 1)
    group, line, row = to // QROWS, (to % QROWS) // OWN, to % OWN
    wanted = ((where_ref[SLOTS + 2] - line + 4) % 4) * QROWS + group * OWN + row
    order = jnp.where(source == wanted, 1.0, 0.0).astype(BF16)
    rows = jnp.dot(order, stack[...].astype(BF16), preferred_element_type=F32)
    for group in range(NEAR):
        out_ref[group] = rows[group * QROWS : (group + 1) * QROWS, :].astype(BF16)


def line_rows(where, *pieces):
    return pl.pallas_call(
        line_kernel,
        out_shape=jax.ShapeDtypeStruct((NEAR,) + pieces[0].shape, BF16),
        in_specs=[SM] + [VM] * 4,
        out_specs=VM,
        scratch_shapes=[pltpu.VMEM((ROWS, pieces[0].shape[1]), F32)],
        compiler_params=params(8),
        name="line_rows",
    )(where, *pieces)


def final_kernel(where_ref, w_ref, *refs):
    pieces = refs[:8]
    out_ref, new_buf, out_sem = refs[8:]
    x = where_ref[SLOTS + 1]
    copies = []
    for by in (0, 1, 3, 2):
        rows = pl.ds(pl.multiple_of(((x - by + 4) % 4) * QROWS, 8), QROWS)

        def slots(group, carry, rows=rows, by=by):
            scales = pieces[4 + by][group, :, PAIR:].astype(F32)
            for half in range(2):
                piece = pieces[half * 4 + by]
                first = half * (PAIR // BLOCK)
                base = where_ref[half * NEAR + group] * PAIR
                for block in range(PAIR // BLOCK):
                    at = pl.ds(pl.multiple_of(base + block * BLOCK, BLOCK), BLOCK)
                    codes = piece[group, :, block * BLOCK : (block + 1) * BLOCK].astype(F32)
                    value = codes * scales[:, first + block : first + block + 1]
                    new_buf[rows, at] = w_ref[rows, at] - outer_rate * value
            return carry

        lax.fori_loop(0, NEAR, slots, 0)
        copies.append(pltpu.make_async_copy(new_buf.at[rows], out_ref.at[rows], out_sem.at[by]))
        copies[-1].start()
    for copy in copies:
        copy.wait()


def final_step(where, weight, pieces):
    return pl.pallas_call(
        final_kernel,
        out_shape=jax.ShapeDtypeStruct((ROWS, WIDTH), F32),
        in_specs=[SM, VM] + [VM] * 8,
        out_specs=HB,
        scratch_shapes=[pltpu.VMEM((ROWS, WIDTH), F32), pltpu.SemaphoreType.DMA((4,))],
        compiler_params=params(16),
        name="final_step",
    )(where, weight, *pieces)


def shift(value, axis, by):
    size = lax.axis_size(axis)
    return lax.ppermute(value, axis, [(i, (i + by) % size) for i in range(size)])


def shifts(values, axis):
    return [shift(value, axis, by) for by, value in zip((1, 2, 3), values)]


def after(value, *others):
    return lax.optimization_barrier((value,) + others)[0]


def swap(own):
    return own, shift(own, "c", 1)


def window(weight, first_moment, second_moment, outer_momentum, act_table, token_ids, targets):
    y, zh, core = lax.axis_index("y"), lax.axis_index("zh"), lax.axis_index("c")
    x, zl = lax.axis_index("x"), lax.axis_index("zl")
    step_y = jnp.array([0, 0, -1, 1, 2, -1, 1, 2, 0, 0, 0], jnp.int32)
    step_z = jnp.array([0, 1, 0, 0, 0, 1, 1, 1, 0, 0, 0], jnp.int32)
    chip = ((y + step_y + 4) % 4) * 2 + (zh + step_z) % 2
    entry = jnp.arange(11)
    where = jnp.where(entry == 8, core, jnp.where(entry == 9, x, jnp.where(entry == 10, zl, chip)))
    where = where.astype(jnp.int32)

    table_t = act_table.T
    ids = token_ids[0]
    wanted = jnp.transpose(targets[0], (0, 2, 1))
    moments = (first_moment[0], second_moment[0])
    own1 = gather(0, 2, ids, table_t)
    own2 = gather(1, 1, ids, table_t, where)

    far1 = shift(own1, "zh", 1)
    left1, right1 = shift(own1, "y", 1), shift(own1, "y", -1)
    left2, right2 = shift(own2, "y", 1), shift(own2, "y", -1)
    opposite1, opposite2 = shift(left1, "y", 1), shift(right2, "y", -1)
    far2 = shift(own2, "zh", 1)
    far_left1, far_right1 = shift(far1, "y", 1), shift(far1, "y", -1)
    near1 = swap(pack(own1, far1, left1, right1))
    far_opposite1 = shift(far_right1, "y", -1)
    far_left2 = shift(far2, "y", 1)
    rest1 = swap(pack(opposite1, far_left1, far_right1))
    last1 = swap(far_opposite1)
    total, near1 = forward(0, 0, where, (), weight, [near1])
    far_right2 = shift(after(far2, far_opposite1), "y", -1)
    near2 = swap(pack(own2, far2, left2, right2))
    signal, rest1 = forward(1, 0, where, (total, wanted), weight, [rest1, last1])
    far_opposite2 = shift(far_left2, "y", 1)
    current0, *state0 = first_back(0, where, signal, near1, weight, *moments)
    rest2 = swap(pack(opposite2, far_left2, far_right2))
    current1, *state1 = first_back(1, where, signal, rest1, weight, *moments)
    last2 = swap(far_opposite2)
    total, near2 = forward(0, 1, where, (), current0, [near2])
    signal, rest2 = forward(1, 1, where, (total, wanted), current1, [rest2, last2])

    payloads = []
    for state, x_half in ((state0, near2), (state1, rest2)):
        sends = second_back(where, signal, x_half, state)
        payloads.append([sends[0]] + shifts(sends[1:], "x"))
    momenta, scales, pieces = [], [], []
    for half in range(2):
        sends = partial_sums(where, payloads[half])
        sums = [sends[0]] + shifts(sends[1:], "zl")
        result = outer_step(half, where, outer_momentum, sums, *scales)
        momenta.append(result[0])
        codes, *scales = result[1:]
        line = line_rows(where, codes, *shifts([codes] * 3, "zl"))
        left, right = shift(line, "x", 1), shift(line, "x", 3)
        opposite = shift((left, right)[half], "x", (1, 3)[half])
        pieces += [line, left, opposite, right]
    new_weight = final_step(where, weight, pieces)
    return (new_weight, momentum_rows(where, *momenta))


def solution(mesh):
    inner = Mesh(mesh.devices.reshape(4, 2, 2, 4, 4), ("y", "zh", "c", "x", "zl"))
    mp, replica = ("y", "zh", "c"), ("x", "zl")
    in_specs = (
        P(mp, None),
        P(replica, mp, None),
        P(replica, mp, None),
        P(mp + replica, None),
        P(None, mp),
        P(replica, None, None),
        P(replica, None, None, mp),
    )
    out_specs = (P(mp, None), P(mp + replica, None))
    return jax.shard_map(window, mesh=inner, in_specs=in_specs, out_specs=out_specs, check_vma=False)
```
